128 devices in a mesh: slab: 8 (over y, core), sub: 16 (over z, x).
Axes of the slice: x: 4, y: 4, z: 4, core: 2. Of those that a mesh axis runs over, the one named last changes fastest.
Arguments:
- positions: float32 [3, 8388608], P(None, ('slab', 'sub')), may hold values from 0 to 64, as said below
- masses: float32 [8388608], P(('slab', 'sub')), may hold values from 0.001 to 0.01
- leaf_counts: int32 [32768], P(('slab', 'sub')), may hold values from 64 to 256, as said below
- send_leaves: int32 [128, 256], P(('slab', 'sub')), may hold values from 0 to 255, as said below
- send_parents: int32 [128, 64], P(('slab', 'sub')), may hold values from 0 to 31, as said below
- near_pairs: int32 [128, 3, 256], P(('slab', 'sub')), may hold values from -1 to 511, as said below
- far_pairs: int32 [128, 3, 1024], P(('slab', 'sub')), may hold values from -1 to 511, as said below
- parent_pairs: int32 [128, 3, 64], P(('slab', 'sub')), may hold values from -1 to 95, as said below
Outputs:
- field: float32 [4, 8388608], P(None, ('slab', 'sub'))
The draws below stay inside these ranges and needn't reach their ends.
Inputs may be any that keep to these rules, and one draw needn't show every extreme that they name: `positions`: the coordinates of a body of leaf c on device (s, u) lie within one unit above that leaf's integer coordinates along each dimension. `leaf_counts`: every device has a leaf whose 256 slots are all used. `send_leaves`: within one direction of a row, the 64 leaves are different. `send_parents`: within one direction of a row, the 16 parent cells are different. `near_pairs`: row 0 is an own leaf, row 1 a leaf table entry or -1 for an unused entry (unused entries come last), row 2 the z image -1, 0 or 1 (0 where unused). Own pairs have a < b; no pair repeats; pairs are leaves at most one leaf apart along each dimension after the image. `far_pairs`: as near_pairs, for leaves whose squared separation after the image is 4 to 12 leaf units. `parent_pairs`: as near_pairs, for parent cells whose squared separation after the image is 2 parent units or more, with the parent table.
All inputs are finite; a program needn't handle non-finite values.
Results may differ from the reference program's by a relative error of at most 0.0003.
Values sent between devices are 32-bit elements; how exact they have to be, the bound alone decides.
A program may use at most 320 MiB of HBM per device.

```python
import math
import jax
import jax.numpy as jnp
from jax import lax

LEAF = 256
CX = 2
CY = 4
CZ = 32
LEAVES = 256
PARENTS = 32
SLOTS = 64
PSLOTS = 16
NEAR = 256
FAR = 1024
PFAR = 64
BODIES = 8388608
N_SLAB = 8
N_SUB = 16


slab_steps = (1, 0, 1, 1)


sub_steps = (0, 1, 1, -1)


def cell_coords(cell_ids, span_y, span_z):
    return (cell_ids // (span_y * span_z), cell_ids // span_z % span_y, cell_ids % span_z)


def send_table(key, cell_total, slots):
    devices = N_SLAB * N_SUB

    def one_device(device_id):
        device_key = jax.random.fold_in(key, device_id)
        chosen = [jax.random.permutation(jax.random.fold_in(device_key, direction), cell_total)[:slots] for direction in range(4)]
        return jnp.concatenate(chosen).astype(jnp.int32)
    return jax.vmap(one_device)(jnp.arange(devices, dtype=jnp.int32))


def pair_lists(key, span_x, span_y, span_z, slots, length, lower, upper, sent_table):
    devices = N_SLAB * N_SUB
    local_total = span_x * span_y * span_z
    table_total = local_total + 4 * slots
    full_device = jax.random.randint(jax.random.fold_in(key, 7), (), 0, devices)

    def one_device(device_id):
        slab_at = device_id // N_SUB
        sub_at = device_id % N_SUB
        local_ids = jnp.arange(local_total, dtype=jnp.int32)
        own_x, own_y, own_z = cell_coords(local_ids, span_y, span_z)
        table_x = [slab_at * span_x + own_x]
        table_y = [sub_at * span_y + own_y]
        table_z = [own_z]
        for direction in range(4):
            reach_x = slab_at + slab_steps[direction]
            reach_y = sub_at + sub_steps[direction]
            partner = reach_x % N_SLAB * N_SUB + reach_y % N_SUB
            sent_ids = sent_table[partner][direction * slots:(direction + 1) * slots]
            cell_x, cell_y, cell_z = cell_coords(sent_ids, span_y, span_z)
            table_x.append(reach_x * span_x + cell_x)
            table_y.append(reach_y * span_y + cell_y)
            table_z.append(cell_z)
        table_x = jnp.concatenate(table_x)
        table_y = jnp.concatenate(table_y)
        table_z = jnp.concatenate(table_z)
        gap_x = table_x[None, :] - own_x[:, None] - slab_at * span_x
        gap_y = table_y[None, :] - own_y[:, None] - sub_at * span_y
        gap_z = table_z[None, :] - own_z[:, None]
        z_image = jnp.where(gap_z > span_z // 2, -1, jnp.where(gap_z < -(span_z // 2), 1, 0))
        gap_z = gap_z + z_image * span_z
        squared = gap_x * gap_x + gap_y * gap_y + gap_z * gap_z
        others = jnp.arange(table_total, dtype=jnp.int32)
        allowed = (others[None, :] >= local_total) | (local_ids[:, None] < others[None, :])
        wanted = allowed & (squared >= lower) & (squared <= upper)
        device_key = jax.random.fold_in(key, device_id)
        ordering = jax.random.permutation(jax.random.fold_in(device_key, 1), local_total * table_total).astype(jnp.int32)
        scores = jnp.where(wanted.reshape(-1), ordering + local_total * table_total, ordering)
        ranked, chosen = lax.top_k(scores, length)
        owned_ids = chosen // table_total
        partner_ids = chosen % table_total
        lifts = z_image.reshape(-1)[chosen]
        live_count = jax.random.randint(jax.random.fold_in(device_key, 2), (), length // 2, length + 1)
        live_count = jnp.where(device_id == full_device, length, live_count)
        active = jnp.arange(length) < live_count
        return jnp.stack([owned_ids, jnp.where(active, partner_ids, -1), jnp.where(active, lifts, 0)]).astype(jnp.int32)
    return jax.vmap(one_device)(jnp.arange(devices, dtype=jnp.int32))


def draw_positions(key, part):
    total = N_SLAB * N_SUB * LEAVES * LEAF
    body_ids = jnp.arange(total, dtype=jnp.int32)
    device_id = body_ids // (LEAVES * LEAF)
    cell_ids = body_ids // LEAF % LEAVES
    slab_at = device_id // N_SUB
    sub_at = device_id % N_SUB
    cell_x, cell_y, cell_z = cell_coords(cell_ids, CY, CZ)
    corner = jnp.stack([slab_at * CX + cell_x, sub_at * CY + cell_y, cell_z]).astype(jnp.float32)
    inside = jax.random.uniform(key, (3, total), jnp.float32, 0.02, 0.98)
    return corner + inside


def draw_leaf_counts(key, part):
    devices = N_SLAB * N_SUB
    counts = jax.random.randint(jax.random.fold_in(key, 11), (devices, LEAVES), LEAF // 4, LEAF + 1)
    full_leaf = jax.random.randint(jax.random.fold_in(key, 12), (devices, 1), 0, LEAVES)
    counts = jnp.where(jnp.arange(LEAVES)[None, :] == full_leaf, LEAF, counts)
    return counts.reshape(-1).astype(jnp.int32)


def draw_send_leaves(key, part):
    return send_table(jax.random.fold_in(key, 101), LEAVES, SLOTS)


def draw_send_parents(key, part):
    return send_table(jax.random.fold_in(key, 202), PARENTS, PSLOTS)


def draw_near_pairs(key, part):
    sent_table = send_table(jax.random.fold_in(key, 101), LEAVES, SLOTS)
    return pair_lists(jax.random.fold_in(key, 303), CX, CY, CZ, SLOTS, NEAR, 1, 3, sent_table)


def draw_far_pairs(key, part):
    sent_table = send_table(jax.random.fold_in(key, 101), LEAVES, SLOTS)
    return pair_lists(jax.random.fold_in(key, 404), CX, CY, CZ, SLOTS, FAR, 4, 12, sent_table)


def draw_parent_pairs(key, part):
    sent_table = send_table(jax.random.fold_in(key, 202), PARENTS, PSLOTS)
    return pair_lists(jax.random.fold_in(key, 505), CX // 2, CY // 2, CZ // 2, PSLOTS, PFAR, 2, 1000000, sent_table)


def steps_of(rng, shape, cuts, smallest, top_value):
    gain, own = 1.0, jax.random.fold_in(rng, 6)
    for axis_at, shards_of in cuts:
        draws = jnp.exp(jax.random.uniform(jax.random.fold_in(own, axis_at), (shards_of,), jnp.float32, smallest / len(cuts), top_value / len(cuts)))
        gain = gain * jnp.repeat(draws, shape[axis_at] // shards_of).reshape([-1 if axis == axis_at else 1 for axis in range(len(shape))])
    return gain


def setup_inputs(seed: int = 0) -> dict:
    key_list = jax.random.split(jax.random.key(seed), 9)
    positions = draw_positions(jax.random.fold_in(key_list[8], 71), 0)
    masses = jnp.clip(jnp.exp(math.log(0.01) - 2.30258502 * jax.random.uniform(key_list[1], (BODIES,), jnp.float32) ** steps_of(key_list[1], (BODIES,), ((0, 128),), -0.2, 0.2)), 0.001, 0.01)
    leaf_counts = draw_leaf_counts(jax.random.fold_in(key_list[8], 71), 0)
    send_leaves = draw_send_leaves(jax.random.fold_in(key_list[8], 71), 0)
    send_parents = draw_send_parents(jax.random.fold_in(key_list[8], 71), 0)
    near_pairs = draw_near_pairs(jax.random.fold_in(key_list[8], 71), 0)
    far_pairs = draw_far_pairs(jax.random.fold_in(key_list[8], 71), 0)
    parent_pairs = draw_parent_pairs(jax.random.fold_in(key_list[8], 71), 0)
    return {"positions": positions, "masses": masses, "leaf_counts": leaf_counts, "send_leaves": send_leaves, "send_parents": send_parents, "near_pairs": near_pairs, "far_pairs": far_pairs, "parent_pairs": parent_pairs}


tensor_offsets = (0, 1, 4, 13, 40, 121)
factorials = (1.0, 1.0, 2.0, 6.0, 24.0)
soft_square = 0.0025
slab_steps = (1, 0, 1, 1)
sub_steps = (0, 1, 1, -1)

def outer_powers(offset):
    tail = offset.shape[1:]
    powers = [jnp.ones((1,) + tail, offset.dtype)]
    for degree in range(4):
        before = powers[-1]
        grown = before[:, None] * offset[None, :]
        powers.append(grown.reshape((before.shape[0] * 3,) + tail))
    return powers

def inverse_distance(vector):
    return 1.0 / jnp.sqrt(jnp.sum(vector * vector))

def jacobian_of(inner):

    def result(vector):
        values, pullback = jax.vjp(inner, vector)
        unit_rows = jnp.eye(values.shape[0], dtype=values.dtype)
        stacked = jax.vmap(pullback)(unit_rows)[0]
        return stacked.reshape(-1)
    return result

def derivative_tensors(separation):
    first_grad = jax.grad(inverse_distance)
    second_grad = jacobian_of(first_grad)
    third_grad = jacobian_of(second_grad)
    fourth_grad = jacobian_of(third_grad)

    def single(vector):
        return (inverse_distance(vector).reshape(1), first_grad(vector).reshape(-1), second_grad(vector).reshape(-1), third_grad(vector).reshape(-1), fourth_grad(vector).reshape(-1))
    return jax.vmap(single)(separation)

def mutual_locals(moments_a, moments_b, separation):
    tensors = derivative_tensors(separation)
    pair_count = separation.shape[0]
    locals_a = []
    locals_b = []
    for degree in range(5):
        summed_a = jnp.zeros((pair_count, 3 ** degree), jnp.float32)
        summed_b = jnp.zeros((pair_count, 3 ** degree), jnp.float32)
        for source in range(5 - degree):
            tensor_block = tensors[source + degree].reshape(pair_count, 3 ** source, 3 ** degree)
            piece_b = moments_b[:, tensor_offsets[source]:tensor_offsets[source + 1]]
            piece_a = moments_a[:, tensor_offsets[source]:tensor_offsets[source + 1]]
            summed_a = summed_a + (-1.0) ** source / factorials[source] * jnp.einsum('pa,pab->pb', piece_b, tensor_block, precision=lax.Precision.HIGHEST)
            summed_b = summed_b + 1.0 / factorials[source] * jnp.einsum('pa,pab->pb', piece_a, tensor_block, precision=lax.Precision.HIGHEST)
        locals_a.append(-summed_a)
        locals_b.append(-(-1.0) ** degree * summed_b)
    return (jnp.concatenate(locals_a, 1), jnp.concatenate(locals_b, 1))

def shift_locals(parent_terms, offset):
    powers = outer_powers(offset)
    result = []
    for degree in range(5):
        summed = jnp.zeros((3 ** degree,) + offset.shape[1:], jnp.float32)
        for source in range(degree, 5):
            spacing = source - degree
            tensor_block = parent_terms[tensor_offsets[source]:tensor_offsets[source + 1]].reshape((3 ** spacing, 3 ** degree) + offset.shape[1:])
            summed = summed + lax.optimization_barrier(jnp.sum(tensor_block * powers[spacing][:, None], 0)) / factorials[spacing]
        result.append(summed)
    return jnp.concatenate(result, 0)

def evaluate_locals(leaf_terms, powers):
    cell_count = leaf_terms.shape[1]
    potential = jnp.zeros(powers[0].shape[1:], jnp.float32)
    accel = jnp.zeros((3,) + powers[0].shape[1:], jnp.float32)
    for degree in range(5):
        tensor_block = leaf_terms[tensor_offsets[degree]:tensor_offsets[degree + 1]]
        potential = potential + lax.optimization_barrier(jnp.sum(tensor_block[:, :, None] * powers[degree], 0)) / factorials[degree]
        if degree < 4:
            upper = leaf_terms[tensor_offsets[degree + 1]:tensor_offsets[degree + 2]].reshape(3 ** degree, 3, cell_count)
            accel = accel - lax.optimization_barrier(jnp.sum(upper[:, :, :, None] * powers[degree][:, None], 0)) / factorials[degree]
    return jnp.concatenate([potential[None], accel], 0)

def pair_block(place_a, weight_a, place_b, weight_b):
    spacing = place_a[:, :, None] - place_b[:, None, :]
    inverse = lax.rsqrt(lax.optimization_barrier(jnp.sum(spacing * spacing, 0)) + soft_square)
    cubed = inverse * inverse * inverse
    potential_a = -lax.optimization_barrier(jnp.sum(weight_b[None, :] * inverse, 1))
    potential_b = -lax.optimization_barrier(jnp.sum(weight_a[:, None] * inverse, 0))
    accel_a = -lax.optimization_barrier(jnp.sum(spacing * (weight_b[None, :] * cubed)[None], 2))
    accel_b = lax.optimization_barrier(jnp.sum(spacing * (weight_a[:, None] * cubed)[None], 1))
    return (jnp.concatenate([potential_a[None], accel_a], 0), jnp.concatenate([potential_b[None], accel_b], 0))

def self_block(places, weight_row):
    slot_count = weight_row.shape[0]
    spacing = places[:, :, None] - places[:, None, :]
    apart = lax.broadcasted_iota(jnp.int32, (slot_count, slot_count), 0) != lax.broadcasted_iota(jnp.int32, (slot_count, slot_count), 1)
    inverse = jnp.where(apart, lax.rsqrt(lax.optimization_barrier(jnp.sum(spacing * spacing, 0)) + soft_square), 0.0)
    cubed = inverse * inverse * inverse
    potential = -lax.optimization_barrier(jnp.sum(weight_row[None, :] * inverse, 1))
    accel = -lax.optimization_barrier(jnp.sum(spacing * (weight_row[None, :] * cubed)[None], 2))
    return jnp.concatenate([potential[None], accel], 0)

def self_work(body_data):
    leaf_total = body_data.shape[1]
    leaf_size = body_data.shape[2]
    grouped = body_data.reshape(4, leaf_total // 8, 8, leaf_size).transpose(1, 0, 2, 3)

    def one_group(bundle):
        return jax.vmap(self_block, in_axes=(1, 0))(bundle[:3], bundle[3])
    fields = lax.map(one_group, grouped)
    return fields.reshape(leaf_total, 4, leaf_size).transpose(1, 0, 2)

def near_work(table_bodies, pair_list):
    owned_ids = pair_list[0]
    partner_ids = jnp.maximum(pair_list[1], 0)
    active = pair_list[1] >= 0
    z_lift = pair_list[2].astype(jnp.float32) * CZ
    pair_count = owned_ids.shape[0]

    def one_group(bundle):
        ids_a, ids_b, lifts, actives = bundle
        place_a = jnp.take(table_bodies[:3], ids_a, axis=1)
        place_b = jnp.take(table_bodies[:3], ids_b, axis=1)
        place_b = place_b.at[2].add(lifts[:, None])
        weight_a = jnp.take(table_bodies[3], ids_a, axis=0)
        weight_b = jnp.take(table_bodies[3], ids_b, axis=0)
        part_a, part_b = jax.vmap(pair_block, in_axes=(1, 0, 1, 0))(place_a, weight_a, place_b, weight_b)
        keeper = actives[:, None, None]
        return (jnp.where(keeper, part_a, 0.0), jnp.where(keeper, part_b, 0.0))

    def shaped(values):
        return values.reshape(pair_count // 8, 8)
    part_a, part_b = lax.map(one_group, (shaped(owned_ids), shaped(partner_ids), shaped(z_lift), shaped(active)))
    part_a = part_a.reshape(pair_count, 4, -1).transpose(1, 0, 2)
    part_b = part_b.reshape(pair_count, 4, -1).transpose(1, 0, 2)
    summed = jnp.zeros(table_bodies.shape, jnp.float32)
    return summed.at[:, owned_ids].add(part_a).at[:, partner_ids].add(part_b)

def far_work(table_cells, pair_list):
    owned_ids = pair_list[0]
    partner_ids = jnp.maximum(pair_list[1], 0)
    active = pair_list[1] >= 0
    z_lift = pair_list[2].astype(jnp.float32) * CZ
    centre_a = jnp.take(table_cells[121:], owned_ids, axis=1)
    centre_b = jnp.take(table_cells[121:], partner_ids, axis=1)
    centre_b = centre_b.at[2].add(z_lift)
    separation = jnp.where(active[None], centre_a - centre_b, 3.0).T
    moments_a = jnp.take(table_cells[:121], owned_ids, axis=1).T
    moments_b = jnp.take(table_cells[:121], partner_ids, axis=1).T
    locals_a, locals_b = mutual_locals(moments_a, moments_b, separation)
    locals_a = jnp.where(active[:, None], locals_a, 0.0)
    locals_b = jnp.where(active[:, None], locals_b, 0.0)
    summed = jnp.zeros((121, table_cells.shape[1]), jnp.float32)
    return summed.at[:, owned_ids].add(locals_a.T).at[:, partner_ids].add(locals_b.T)

def geometry(slab_at, sub_at):
    leaf_ids = jnp.arange(CX * CY * CZ, dtype=jnp.int32)
    cell_x = leaf_ids // (CY * CZ)
    cell_y = leaf_ids // CZ % CY
    cell_z = leaf_ids % CZ
    base_x = slab_at * CX
    base_y = sub_at * CY
    centres = jnp.stack([base_x + cell_x, base_y + cell_y, cell_z]).astype(jnp.float32) + 0.5
    half_y = CY // 2
    half_z = CZ // 2
    parent_of = (cell_x // 2 * half_y + cell_y // 2) * half_z + cell_z // 2
    parent_ids = jnp.arange(CX // 2 * half_y * half_z, dtype=jnp.int32)
    parent_x = parent_ids // (half_y * half_z)
    parent_y = parent_ids // half_z % half_y
    parent_z = parent_ids % half_z
    parent_centres = jnp.stack([base_x + 2 * parent_x, base_y + 2 * parent_y, 2 * parent_z]).astype(jnp.float32) + 1.0
    return (centres, parent_centres, parent_of)

def image_shift(slab_at, sub_at, slab_count, sub_count):
    rows_out = []
    for direction in range(4):
        reach_x = slab_at + slab_steps[direction]
        reach_y = sub_at + sub_steps[direction]
        jump_x = (reach_x - reach_x % slab_count) * CX
        jump_y = (reach_y - reach_y % sub_count) * CY
        rows_out.append(jnp.stack([jump_x, jump_y, jnp.zeros_like(jump_x)]))
    return jnp.stack(rows_out).astype(jnp.float32)

def neighbour_ranks(slab_at, sub_at, slab_count, sub_count, facing):
    return jnp.stack([(slab_at + facing * slab_steps[direction]) % slab_count * sub_count + (sub_at + facing * sub_steps[direction]) % sub_count for direction in range(4)]).astype(jnp.int32)

def device_front(positions, masses, leaf_counts, send_leaves, send_parents, slab_at, sub_at):
    leaf_total = leaf_counts.shape[0]
    leaf_size = masses.shape[0] // leaf_total
    places = positions.reshape(3, leaf_total, leaf_size)
    filled = lax.broadcasted_iota(jnp.int32, (leaf_total, leaf_size), 1) < leaf_counts[:, None]
    weights = jnp.where(filled, masses.reshape(leaf_total, leaf_size), 0.0)
    centres, parent_centres, parent_of = geometry(slab_at, sub_at)
    parent_total = parent_centres.shape[1]
    leaf_powers = outer_powers(places - centres[:, :, None])
    moments = lax.optimization_barrier(jnp.sum(jnp.concatenate(leaf_powers, 0) * weights[None], 2))
    parent_powers = jnp.concatenate(outer_powers(places - jnp.take(parent_centres, parent_of, axis=1)[:, :, None]), 0)
    per_leaf = lax.optimization_barrier(jnp.sum(parent_powers * weights[None], 2))
    belongs = (parent_of[:, None] == jnp.arange(parent_total, dtype=jnp.int32)[None, :]).astype(jnp.float32)
    parent_moments = jnp.dot(per_leaf, belongs, precision=lax.Precision.HIGHEST)
    body_data = jnp.concatenate([places, weights[None]], 0)
    leaf_rows = jnp.concatenate([moments, centres], 0)
    parent_rows = jnp.concatenate([parent_moments, parent_centres], 0)
    sent_leaf = send_leaves.reshape(4, -1)
    sent_parent = send_parents.reshape(4, -1)
    out_bodies = jnp.take(body_data, sent_leaf, axis=1).transpose(1, 0, 2, 3).reshape(4, -1)
    out_leaf = jnp.take(leaf_rows, sent_leaf, axis=1).transpose(1, 0, 2).reshape(4, -1)
    out_parent = jnp.take(parent_rows, sent_parent, axis=1).transpose(1, 0, 2).reshape(4, -1)
    outgoing = jnp.concatenate([out_bodies, out_leaf, out_parent], 1)
    return (filled, leaf_powers, body_data, leaf_rows, parent_rows, centres, parent_centres, parent_of, sent_leaf, sent_parent, outgoing)

def device_middle(body_data, leaf_rows, parent_rows, incoming, image, near_list, far_list, parent_list):
    leaf_total = body_data.shape[1]
    leaf_size = body_data.shape[2]
    parent_total = parent_rows.shape[1]
    slots = leaf_total // 4
    parent_slots = parent_total // 2
    cut_a = 4 * slots * leaf_size
    cut_b = cut_a + 124 * slots
    body_lift = jnp.concatenate([image, jnp.zeros((4, 1), jnp.float32)], 1)
    cell_lift = jnp.concatenate([jnp.zeros((4, 121), jnp.float32), image], 1)
    in_bodies = incoming[:, :cut_a].reshape(4, 4, slots, leaf_size) + body_lift[:, :, None, None]
    in_leaf = incoming[:, cut_a:cut_b].reshape(4, 124, slots) + cell_lift[:, :, None]
    in_parent = incoming[:, cut_b:].reshape(4, 124, parent_slots) + cell_lift[:, :, None]
    table_bodies = jnp.concatenate([body_data, in_bodies.transpose(1, 0, 2, 3).reshape(4, 4 * slots, leaf_size)], 1)
    table_leaf = jnp.concatenate([leaf_rows, in_leaf.transpose(1, 0, 2).reshape(124, 4 * slots)], 1)
    table_parent = jnp.concatenate([parent_rows, in_parent.transpose(1, 0, 2).reshape(124, 4 * parent_slots)], 1)
    near_table = near_work(table_bodies, near_list)
    local_near = near_table[:, :leaf_total] + self_work(body_data)
    leaf_table = far_work(table_leaf, far_list)
    parent_table = far_work(table_parent, parent_list)
    back_bodies = near_table[:, leaf_total:].reshape(4, 4, slots, leaf_size).transpose(1, 0, 2, 3).reshape(4, -1)
    back_leaf = leaf_table[:, leaf_total:].reshape(121, 4, slots).transpose(1, 0, 2).reshape(4, -1)
    back_parent = parent_table[:, parent_total:].reshape(121, 4, parent_slots).transpose(1, 0, 2).reshape(4, -1)
    returning = jnp.concatenate([back_bodies, back_leaf, back_parent], 1)
    return (returning, local_near, leaf_table[:, :leaf_total], parent_table[:, :parent_total])

def device_back(local_near, leaf_terms, parent_terms, arrived, sent_leaf, sent_parent, leaf_powers, centres, parent_centres, parent_of, filled):
    leaf_size = local_near.shape[2]
    slots = sent_leaf.shape[1]
    cut_a = 4 * slots * leaf_size
    cut_b = cut_a + 121 * slots
    flat_leaf = sent_leaf.reshape(-1)
    flat_parent = sent_parent.reshape(-1)
    got_bodies = arrived[:, :cut_a].reshape(4, 4, slots, leaf_size).transpose(1, 0, 2, 3).reshape(4, 4 * slots, leaf_size)
    got_leaf = arrived[:, cut_a:cut_b].reshape(4, 121, slots).transpose(1, 0, 2).reshape(121, -1)
    got_parent = arrived[:, cut_b:].reshape(4, 121, -1).transpose(1, 0, 2).reshape(121, -1)
    local_near = local_near.at[:, flat_leaf].add(got_bodies)
    leaf_terms = leaf_terms.at[:, flat_leaf].add(got_leaf)
    parent_terms = parent_terms.at[:, flat_parent].add(got_parent)
    leaf_terms = leaf_terms + shift_locals(jnp.take(parent_terms, parent_of, axis=1), centres - jnp.take(parent_centres, parent_of, axis=1))
    result = evaluate_locals(leaf_terms, leaf_powers) + local_near
    result = jnp.where(filled[None], result, 0.0)
    return result.reshape(4, -1)

def reference(positions, masses, leaf_counts, send_leaves, send_parents, near_pairs, far_pairs, parent_pairs):
    devices = N_SLAB * N_SUB
    per_device = masses.shape[0] // devices
    leaf_total = leaf_counts.shape[0] // devices
    place_blocks = positions.reshape(3, devices, per_device).transpose(1, 0, 2)
    mass_blocks = masses.reshape(devices, per_device)
    count_blocks = leaf_counts.reshape(devices, leaf_total)
    device_ids = jnp.arange(devices, dtype=jnp.int32)
    directions = jnp.arange(4, dtype=jnp.int32)

    def front(device_id):
        slab_at = device_id // N_SUB
        sub_at = device_id % N_SUB
        return device_front(place_blocks[device_id], mass_blocks[device_id], count_blocks[device_id], send_leaves[device_id], send_parents[device_id], slab_at, sub_at)

    def front_outgoing(device_id):
        return front(device_id)[-1]
    outgoing_all = lax.map(front_outgoing, device_ids)

    def middle(device_id):
        parts = front(device_id)
        slab_at = device_id // N_SUB
        sub_at = device_id % N_SUB
        sources = neighbour_ranks(slab_at, sub_at, N_SLAB, N_SUB, 1)
        incoming = outgoing_all[sources, directions]
        image = image_shift(slab_at, sub_at, N_SLAB, N_SUB)
        return device_middle(parts[2], parts[3], parts[4], incoming, image, near_pairs[device_id], far_pairs[device_id], parent_pairs[device_id])
    returning_all, near_all, leaf_all, parent_all = lax.map(middle, device_ids)

    def back(device_id):
        parts = front(device_id)
        slab_at = device_id // N_SUB
        sub_at = device_id % N_SUB
        targets = neighbour_ranks(slab_at, sub_at, N_SLAB, N_SUB, -1)
        arrived = returning_all[targets, directions]
        return device_back(near_all[device_id], leaf_all[device_id], parent_all[device_id], arrived, parts[8], parts[9], parts[1], parts[5], parts[6], parts[7], parts[0])
    fields = lax.map(back, device_ids)
    return fields.transpose(1, 0, 2).reshape(4, -1)
```

```python
import jax
import jax.numpy as jnp
from jax import lax
from jax.experimental import pallas as pl
from jax.experimental.pallas import tpu as pltpu
from jax.sharding import PartitionSpec as P

CX = 2
CY = 4
CZ = 32
LEAVES = 256
LEAF = 256
PARENTS = 32
SLOTS = 64
PSLOTS = 16
NEAR = 256
FAR = 1024
PFAR = 64
PAY = SLOTS + 5
SOFT = 0.0025
slab_steps = (1, 0, 1, 1)
sub_steps = (0, 1, 1, -1)
f32 = jnp.float32
bf16 = jnp.bfloat16

ALPHAS = [
    (i, j, d - i - j) for d in range(5) for i in range(d, -1, -1) for j in range(d - i, -1, -1)
]
AT = {a: n for n, a in enumerate(ALPHAS)}
FACT = (1.0, 1.0, 2.0, 6.0, 24.0)
TABLE = LEAVES + 4 * 128 + 128


def afact(alpha):
    return FACT[alpha[0]] * FACT[alpha[1]] * FACT[alpha[2]]


def add(a, b):
    return (a[0] + b[0], a[1] + b[1], a[2] + b[2])


def unit(axis):
    return tuple(1 if k == axis else 0 for k in range(3))


def split3(value):
    one = value.astype(bf16)
    rest = value - one.astype(f32)
    two = rest.astype(bf16)
    three = (rest - two.astype(f32)).astype(bf16)
    return one, two, three


def dot_nn(a, b):
    return lax.dot_general(a, b, (((1,), (0,)), ((), ())), preferred_element_type=f32)


def dot_nt(a, b):
    return lax.dot_general(a, b, (((1,), (1,)), ((), ())), preferred_element_type=f32)


def dot_tn(a, b):
    return lax.dot_general(a, b, (((0,), (0,)), ((), ())), preferred_element_type=f32)


def pick(values, onehot, transposed=False):
    parts = jnp.concatenate([part.astype(f32) for part in split3(values)], 0).astype(bf16)
    out = dot_nt(parts, onehot) if transposed else dot_nn(parts, onehot)
    rows = values.shape[0]
    return out[:rows] + out[rows : 2 * rows] + out[2 * rows :]


def iota(shape, dim):
    return lax.broadcasted_iota(jnp.int32, shape, dim)


def onehot_rows(count, ids):
    hit = iota((count, ids.shape[1]), 0) == ids
    return jnp.where(hit, 1.0, 0.0).astype(bf16)


def put_slab(slab_ref, c, slab):
    wide = jnp.concatenate([slab, jnp.zeros((4, LEAF), f32)], 0)
    for half in range(2):
        rows = pl.ds(pl.multiple_of(half * LEAVES * 8 + c * 8, 8), 8)
        slab_ref[rows, :] = wide[:, half * 128 : half * 128 + 128]


def get_rows(slab_ref, comp):
    return jnp.concatenate(
        [slab_ref[pl.ds(half * LEAVES * 8 + comp, LEAVES, stride=8), :] for half in range(2)], 1
    )


def monomials(x, y, z, w):
    made = {(0, 0, 0): w}
    for alpha in ALPHAS[1:]:
        for axis, value in ((2, z), (1, y), (0, x)):
            if alpha[axis]:
                lower = tuple(alpha[k] - (k == axis) for k in range(3))
                made[alpha] = made[lower] * value
                break
    return made


def shift_moments(moments, offsets):
    choose = ((1,), (1, 1), (1, 2, 1), (1, 3, 3, 1), (1, 4, 6, 4, 1))
    for axis in range(3):
        powers = [None, offsets[axis]]
        for _ in range(3):
            powers.append(powers[-1] * offsets[axis])
        moved = {}
        for alpha in ALPHAS:
            total = moments[alpha]
            for k in range(alpha[axis]):
                lower = tuple(k if q == axis else alpha[q] for q in range(3))
                total = total + moments[lower] * powers[alpha[axis] - k] * float(
                    choose[alpha[axis]][k]
                )
            moved[alpha] = total
        moments = moved
    return moments


def leaf_lanes():
    lane = iota((1, LEAVES), 1)
    return lane // (CY * CZ), lane // CZ % CY, lane % CZ


def parent_offsets():
    cell_x, cell_y, cell_z = leaf_lanes()
    return [(cell % 2).astype(f32) - 0.5 for cell in (cell_x, cell_y, cell_z)]


def front_kernel(
    at_ref, counts_ref, send_ref, ids_ref, pos_ref, mass_ref,
    own_ref, cells_ref, pcells_ref, pay0, pay1, pay2, pay3, slab_ref, turned_ref,
):
    pays = (pay0, pay1, pay2, pay3)
    base_x = at_ref[0] * CX
    base_y = at_ref[1] * CY
    row4 = iota((4, LEAF), 0)
    lane = iota((1, LEAF), 1)

    def one_leaf(c, _):
        start = pl.multiple_of(c * LEAF, LEAF)
        place = pos_ref[:, pl.ds(start, LEAF)]
        mass = jnp.concatenate(
            [mass_ref[pl.ds(2 * c, 1), :], mass_ref[pl.ds(2 * c + 1, 1), :]], 1
        )
        weight = jnp.where(lane < counts_ref[c], mass, 0.0)
        centre_x = (base_x + c // (CY * CZ)).astype(f32) + 0.5
        centre_y = (base_y + c // CZ % CY).astype(f32) + 0.5
        centre_z = (c % CZ).astype(f32) + 0.5
        centre = jnp.where(row4 == 1, centre_x, jnp.where(row4 == 2, centre_y, centre_z))
        centre = jnp.where(row4 == 0, 0.0, centre)
        slab = jnp.concatenate([weight, place], 0) - centre
        own_ref[c] = slab
        put_slab(slab_ref, c, slab)
        return 0

    lax.fori_loop(0, LEAVES, one_leaf, 0, unroll=8)

    for comp in range(4):
        turned_ref[comp] = get_rows(slab_ref, comp).T

    for half in range(2):
        lanes = slice(half * 128, half * 128 + 128)

        def chunk(step, totals):
            rows = pl.ds(pl.multiple_of(step * 8, 8), 8)
            w, x, y, z = [turned_ref[comp, rows, lanes] for comp in range(4)]
            made = monomials(x, y, z, w)
            return tuple(total + made[alpha] for total, alpha in zip(totals, ALPHAS))

        totals = lax.fori_loop(
            0, LEAF // 8, chunk, tuple(jnp.zeros((8, 128), f32) for _ in ALPHAS)
        )
        for n, total in enumerate(totals):
            cells_ref[n : n + 1, lanes] = jnp.sum(total, 0, keepdims=True)

    cell_x, cell_y, cell_z = leaf_lanes()
    cells_ref[35:36, :] = (base_x + cell_x).astype(f32) + 0.5
    cells_ref[36:37, :] = (base_y + cell_y).astype(f32) + 0.5
    cells_ref[37:38, :] = cell_z.astype(f32) + 0.5
    cells_ref[38:40, :] = jnp.zeros((2, LEAVES), f32)

    moments = {alpha: cells_ref[n : n + 1, :] for n, alpha in enumerate(ALPHAS)}
    moved = shift_moments(moments, parent_offsets())
    moved = jnp.concatenate(
        [moved[alpha] for alpha in ALPHAS] + [jnp.zeros((5, LEAVES), f32)], 0
    )
    parent_of = (iota((LEAVES, 128), 0) // CZ % CY // 2) * (CZ // 2) + iota(
        (LEAVES, 128), 0
    ) % CZ // 2
    belongs = jnp.where(parent_of == iota((LEAVES, 128), 1), 1.0, 0.0).astype(bf16)
    pcells = pick(moved, belongs)
    plane = iota((40, 128), 1)
    prow = iota((40, 128), 0)
    pcells = jnp.where(prow == 35, (base_x + 1).astype(f32), pcells)
    pcells = jnp.where(
        prow == 36, (base_y + 2 * (plane // (CZ // 2))).astype(f32) + 1.0, pcells
    )
    pcells = jnp.where(prow == 37, (2 * (plane % (CZ // 2))).astype(f32) + 1.0, pcells)
    pcells_ref[...] = pcells

    lane128 = iota((1, 128), 1)
    for q in range(4):
        pay = pays[q]

        def copy_leaf(k, _, pay=pay, q=q):
            pay[k] = own_ref[send_ref[q * SLOTS + k]]
            return 0

        lax.fori_loop(0, SLOTS, copy_leaf, 0, unroll=8)
        ids = ids_ref[q : q + 1, :]
        leaf_hot = onehot_rows(LEAVES, jnp.where(lane128 < SLOTS, ids, -1))
        parent_hot = onehot_rows(128, jnp.where(lane128 >= SLOTS, ids, -1))
        block = pick(cells_ref[...], leaf_hot) + pick(pcells, parent_hot)
        put_block(pay, block)


def put_block(pay, block):
    for s in range(5):
        pay[SLOTS + s, :, 0:128] = block[4 * s : 4 * s + 4]
        pay[SLOTS + s, :, 128:256] = block[20 + 4 * s : 24 + 4 * s]


def get_block(tail):
    return jnp.concatenate(
        [tail(s)[:, 0:128] for s in range(5)] + [tail(s)[:, 128:256] for s in range(5)], 0
    )


VM = pl.BlockSpec(memory_space=pltpu.VMEM)
SM = pl.BlockSpec(memory_space=pltpu.SMEM)
HB = pl.BlockSpec(memory_space=pl.ANY)
PARAMS = dict(vmem_limit_bytes=48 * 1024 * 1024)


def shaped(*shape):
    return jax.ShapeDtypeStruct(shape, f32)


def front(at, counts, send, ids, positions, masses):
    return pl.pallas_call(
        front_kernel,
        name="front",
        out_shape=[
            shaped(LEAVES, 4, LEAF), shaped(40, LEAVES), shaped(40, 128),
        ] + [shaped(PAY, 4, LEAF)] * 4,
        in_specs=[SM, SM, SM, VM, VM, VM],
        out_specs=[VM] * 7,
        scratch_shapes=[
            pltpu.VMEM((LEAVES * 16, 128), f32),
            pltpu.VMEM((4, LEAF, LEAVES), f32),
        ],
        compiler_params=pltpu.CompilerParams(**PARAMS),
    )(at, counts, send, ids, positions, masses)


def slab8(slab):
    return jnp.concatenate([slab, jnp.zeros((4, LEAF), f32)], 0)


def b_form(points):
    row = iota(points.shape, 0)
    square = jnp.sum(jnp.where(row == 0, 0.0, points * points), 0, keepdims=True)
    return jnp.where(row == 4, square, points)


def a_form(points):
    row = iota(points.shape, 0)
    square = jnp.sum(jnp.where(row == 0, 0.0, points * points), 0, keepdims=True)
    value = jnp.where(row == 0, square + SOFT, -2.0 * points)
    return jnp.where(row == 4, 1.0, value)


def widen(value):
    one = value.astype(bf16).astype(f32)
    rest = value - one
    two = rest.astype(bf16).astype(f32)
    return one, two, rest - two


def squares(a_points, b_points):
    a1, a2, a3 = widen(a_form(a_points))
    b1, b2, b3 = widen(b_form(b_points))
    left = jnp.concatenate([a1, a1, a2, a2, a1, a3], 0).astype(bf16)
    right = jnp.concatenate([b1, b2, b1, b2, b3, b1], 0).astype(bf16)
    return dot_tn(left, right)


def sources(points, weight):
    row = iota(points.shape, 0)
    loaded = points * weight
    one, two, _ = widen(loaded)
    third = jnp.concatenate([one, two], 0).astype(bf16)
    one, two, _ = widen(jnp.where(row == 4, weight, 0.0))
    first = jnp.concatenate([one, two], 0).astype(bf16)
    return third, first


def summed(sides, third, first, dot):
    out = dot(sides[0], third) + dot(sides[1], first)
    return out[0:8] + out[8:16]


def finish(total, points):
    row = iota((8, LEAF), 0)
    value = jnp.where(row == 0, -total[4:5], total - points * total[0:1])
    return value[0:4]


def load_points(slab):
    wide = slab8(slab)
    row = iota((8, LEAF), 0)
    return jnp.where(row == 0, 1.0, wide), slab[0:1]


def self_kernel(own_ref, out_ref):
    apart = jnp.where(iota((LEAF, LEAF), 0) == iota((LEAF, LEAF), 1), 0.0, 1.0)

    def one_leaf(c, _):
        points, weight = load_points(own_ref[c])
        inverse = lax.rsqrt(squares(points, points)) * apart
        cubed = inverse * inverse * inverse
        total = summed(
            sources(points, weight), cubed.astype(bf16), inverse.astype(bf16), dot_nn
        )
        out_ref[c] = finish(total, points)
        return 0

    lax.fori_loop(0, own_ref.shape[0], one_leaf, 0, unroll=4)


def self_part(own, first, count):
    block = 16
    return pl.pallas_call(
        self_kernel,
        name="self_part",
        grid=(count // block,),
        out_shape=shaped(count, 4, LEAF),
        in_specs=[pl.BlockSpec((block, 4, LEAF), lambda i: (i + first // block, 0, 0))],
        out_specs=pl.BlockSpec((block, 4, LEAF), lambda i: (i, 0, 0)),
        cost_estimate=pl.CostEstimate(
            flops=count * 40_000_000, bytes_accessed=count * 8192, transcendentals=0
        ),
        compiler_params=pltpu.CompilerParams(**PARAMS),
    )(own)


def near_kernel(
    pairs_ref, moved_ref, own_ref, in0, in1, in2, in3, backs_ref,
    out_ref, pay0, pay1, pay2, pay3, table, total, sem,
):
    pays = (pay0, pay1, pay2, pay3)
    copies = [pltpu.make_async_copy(own_ref, table.at[pl.ds(0, LEAVES)], sem.at[0])]
    for q, part in enumerate((in0, in1, in2, in3)):
        copies.append(
            pltpu.make_async_copy(
                part.at[pl.ds(0, SLOTS)],
                table.at[pl.ds(LEAVES + q * SLOTS, SLOTS)],
                sem.at[1 + q],
            )
        )
    for copy in copies:
        copy.start()

    def clear(c, _):
        total[c] = jnp.zeros((8, LEAF), f32)
        return 0

    lax.fori_loop(0, 2 * LEAVES, clear, 0, unroll=8)
    for copy in copies:
        copy.wait()

    row = iota((8, LEAF), 0)

    def one_pair(p):
        a = pairs_ref[0, p]
        listed = pairs_ref[1, p]
        b = jnp.maximum(listed, 0)
        used = jnp.where(listed >= 0, 1.0, 0.0)
        points_a, weight_a = load_points(table[a])
        points_b, weight_b = load_points(table[b])
        shift = jnp.where(
            row == 1,
            moved_ref[0, p],
            jnp.where(row == 2, moved_ref[1, p], jnp.where(row == 3, moved_ref[2, p], 0.0)),
        )
        from_b = points_a + shift
        from_a = points_b - shift
        inverse = lax.rsqrt(squares(from_b, points_b))
        cubed = (inverse * inverse * inverse).astype(bf16)
        inverse = inverse.astype(bf16)
        to_b = summed(sources(from_b, weight_a * used), cubed, inverse, dot_nn)
        to_a = summed(sources(from_a, weight_b * used), cubed, inverse, dot_nt)
        return a, b, to_a, to_b

    width = 4

    def some_pairs(step, _):
        done = [one_pair(step * width + k) for k in range(width)]
        for a, b, to_a, to_b in done:
            total[a] = total[a] + to_a
            total[b] = total[b] + to_b
        return 0

    def count_used(p, n):
        return n + jnp.where(pairs_ref[1, p] >= 0, 1, 0)

    used_pairs = lax.fori_loop(0, NEAR, count_used, 0)
    lax.fori_loop(0, (used_pairs + width - 1) // width, some_pairs, 0)

    def finish_own(c, _):
        points, _ = load_points(table[c])
        out_ref[c] = finish(total[c], points)
        return 0

    lax.fori_loop(0, LEAVES, finish_own, 0, unroll=8)
    for q in range(4):

        def finish_other(k, _, q=q):
            points, _ = load_points(table[LEAVES + q * SLOTS + k])
            pays[q][k] = finish(total[LEAVES + q * SLOTS + k], points)
            return 0

        lax.fori_loop(0, SLOTS, finish_other, 0, unroll=8)
        put_block(pays[q], backs_ref[q])


def near_part(pairs, moved, own, incoming, backs):
    return pl.pallas_call(
        near_kernel,
        name="near_part",
        out_shape=[shaped(LEAVES, 4, LEAF)] + [shaped(PAY, 4, LEAF)] * 4,
        in_specs=[SM, SM, HB, HB, HB, HB, HB, VM],
        out_specs=[VM] * 5,
        scratch_shapes=[
            pltpu.VMEM((2 * LEAVES, 4, LEAF), f32),
            pltpu.VMEM((2 * LEAVES, 8, LEAF), f32),
            pltpu.SemaphoreType.DMA((5,)),
        ],
        cost_estimate=pl.CostEstimate(
            flops=NEAR * 80_000_000, bytes_accessed=4_000_000, transcendentals=0
        ),
        compiler_params=pltpu.CompilerParams(**PARAMS),
    )(pairs, moved, own, *incoming, backs)


def derivatives(x, y, z):
    square = x * x + y * y + z * z
    inverse = 1.0 / jnp.sqrt(square)
    inverse2 = inverse * inverse
    table = {(0, (0, 0, 0)): inverse}
    for m in range(1, 5):
        table[(m, (0, 0, 0))] = table[(m - 1, (0, 0, 0))] * inverse2 * float(-(2 * m - 1))
    place = (x, y, z)

    def entry(m, alpha):
        key = (m, alpha)
        if key not in table:
            axis = [k for k in range(3) if alpha[k]][0]
            lower = tuple(alpha[k] - (k == axis) for k in range(3))
            value = place[axis] * entry(m + 1, lower)
            if lower[axis]:
                lowest = tuple(lower[k] - (k == axis) for k in range(3))
                value = value + float(lower[axis]) * entry(m + 1, lowest)
            table[key] = value
        return table[key]

    return {alpha: entry(0, alpha) for alpha in ALPHAS}


def mutual(a_ref, b_ref, to_a, to_b):
    def rows(n):
        return pl.ds(n * 8, 8)

    lift = a_ref[rows(38), :]
    live = a_ref[rows(39), :] > 0.5
    gap = [
        jnp.where(live, a_ref[rows(35 + k), :] - b_ref[rows(35 + k), :] - (lift if k == 2 else 0.0), 3.0)
        for k in range(3)
    ]
    made = derivatives(*gap)
    for beta in ALPHAS:
        sum_a = None
        sum_b = None
        for alpha in ALPHAS:
            if sum(alpha) + sum(beta) > 4:
                continue
            tensor = made[add(alpha, beta)]
            scale = 1.0 / afact(alpha)
            sign_a = -((-1.0) ** sum(alpha)) * scale
            sign_b = -((-1.0) ** sum(beta)) * scale
            term_a = b_ref[rows(AT[alpha]), :] * sign_a * tensor
            term_b = a_ref[rows(AT[alpha]), :] * sign_b * tensor
            sum_a = term_a if sum_a is None else sum_a + term_a
            sum_b = term_b if sum_b is None else sum_b + term_b
        to_a[rows(AT[beta]), :] = jnp.where(live, sum_a, 0.0)
        to_b[rows(AT[beta]), :] = jnp.where(live, sum_b, 0.0)


def far_kernel(
    image_ref, far_ref, parent_ref, near_ref, cells_ref, pcells_ref, in0, in1, in2, in3,
    leaf_ref, par_ref, backs_ref, moved_ref, tails, table, left, right, to_a, to_b, total, sem,
):
    copies = []
    for q, part in enumerate((in0, in1, in2, in3)):
        copies.append(
            pltpu.make_async_copy(part.at[pl.ds(SLOTS, 5)], tails.at[q], sem.at[q])
        )
    for copy in copies:
        copy.start()
    table[:, 0:LEAVES] = cells_ref[...]
    table[:, LEAVES + 512 :] = pcells_ref[...]
    row = iota((40, 128), 0)
    to_a[...] = jnp.zeros_like(to_a)
    to_b[...] = jnp.zeros_like(to_b)
    left[...] = jnp.zeros_like(left)
    right[...] = jnp.zeros_like(right)
    for copy in copies:
        copy.wait()
    for q in range(4):
        block = get_block(lambda s, q=q: tails[q, s])
        block = block + jnp.where(
            row == 35, image_ref[q, 0], jnp.where(row == 36, image_ref[q, 1], 0.0)
        )
        table[:, LEAVES + q * 128 : LEAVES + q * 128 + 128] = block
    parts = jnp.concatenate([part.astype(f32) for part in split3(table[...])], 0).astype(bf16)
    total[...] = jnp.zeros_like(total)

    def gathered(hot, first, count):
        out = dot_nn(parts[:, first : first + count], hot)
        return out[0:40] + out[40:80] + out[80:120]

    def leaf_entry(ids):
        other = ids - LEAVES
        return jnp.where(ids < LEAVES, ids, LEAVES + other // SLOTS * 128 + other % SLOTS)

    def parent_entry(ids):
        other = ids - PARENTS
        return jnp.where(
            ids < PARENTS, LEAVES + 512 + ids, LEAVES + other // PSLOTS * 128 + SLOTS + other % PSLOTS
        )

    def hots(ids_a, ids_b, parents):
        if parents:
            return (
                onehot_rows(128, ids_a), LEAVES + 512, 128,
                onehot_rows(640, parent_entry(ids_b) - LEAVES), LEAVES, 640,
            )
        return (
            onehot_rows(LEAVES, ids_a), 0, LEAVES,
            onehot_rows(768, leaf_entry(ids_b)), 0, 768,
        )

    def load(ids_a, ids_b, lifts, g, parents):
        hot_a, first_a, count_a, hot_b, first_b, count_b = hots(ids_a, ids_b, parents)
        from_a = gathered(hot_a, first_a, count_a)
        from_b = gathered(hot_b, first_b, count_b)
        live = jnp.where(ids_b >= 0, 1.0, 0.0)
        from_a = jnp.where(row == 38, lifts.astype(f32) * float(CZ), from_a)
        from_a = jnp.where(row == 39, live, from_a)
        left[pl.ds(g, 40, stride=8), :] = from_a
        right[pl.ds(g, 40, stride=8), :] = from_b

    def store(ids_a, ids_b, g, parents):
        hot_a, first_a, count_a, hot_b, first_b, count_b = hots(ids_a, ids_b, parents)
        sum_a = pick(to_a[pl.ds(g, 40, stride=8), :], hot_a, True)
        sum_b = pick(to_b[pl.ds(g, 40, stride=8), :], hot_b, True)
        total[:, first_a : first_a + count_a] += sum_a
        total[:, first_b : first_b + count_b] += sum_b

    for g in range(FAR // 128):
        lanes = slice(g * 128, g * 128 + 128)
        load(far_ref[0:1, lanes], far_ref[1:2, lanes], far_ref[2:3, lanes], g, False)
    mutual(left, right, to_a, to_b)
    for g in range(FAR // 128):
        lanes = slice(g * 128, g * 128 + 128)
        store(far_ref[0:1, lanes], far_ref[1:2, lanes], g, False)
    load(parent_ref[0:1, :], parent_ref[1:2, :], parent_ref[2:3, :], 0, True)
    mutual(left, right, to_a, to_b)
    store(parent_ref[0:1, :], parent_ref[1:2, :], 0, True)

    for g in range(NEAR // 128):
        lanes = slice(g * 128, g * 128 + 128)
        hot_a, _, _, hot_b, _, _ = hots(near_ref[0:1, lanes], near_ref[1:2, lanes], False)
        apart = gathered(hot_a, 0, LEAVES) - gathered(hot_b, 0, 768)
        apart = jnp.where(row == 37, apart - near_ref[2:3, lanes].astype(f32) * float(CZ), apart)
        for k in range(3):
            moved_ref[k : k + 1, lanes] = apart[35 + k : 36 + k, :]

    leaf_ref[...] = total[:, 0:LEAVES]
    par_ref[...] = total[:, LEAVES + 512 :]
    for q in range(4):
        backs_ref[q] = total[:, LEAVES + q * 128 : LEAVES + q * 128 + 128]


def far_part(image, far, parent, near, cells, pcells, incoming):
    return pl.pallas_call(
        far_kernel,
        name="far_part",
        out_shape=[
            shaped(40, LEAVES), shaped(40, 128), shaped(4, 40, 128), shaped(3, NEAR),
        ],
        in_specs=[SM, VM, VM, VM, VM, VM, HB, HB, HB, HB],
        out_specs=[VM] * 4,
        scratch_shapes=[
            pltpu.VMEM((4, 5, 4, LEAF), f32),
            pltpu.VMEM((40, TABLE), f32),
        ] + [pltpu.VMEM((320, 128), f32)] * 4 + [
            pltpu.VMEM((40, TABLE), f32),
            pltpu.SemaphoreType.DMA((4,)),
        ],
        compiler_params=pltpu.CompilerParams(**PARAMS),
    )(image, far, parent, near, cells, pcells, *incoming)


def shift_terms(terms, offsets):
    for axis in range(3):
        powers = [None, offsets[axis]]
        for _ in range(3):
            powers.append(powers[-1] * offsets[axis])
        moved = {}
        for alpha in ALPHAS:
            total = terms[alpha]
            for k in range(1, 5 - sum(alpha)):
                upper = tuple(alpha[q] + k * (q == axis) for q in range(3))
                total = total + terms[upper] * powers[k] * (1.0 / FACT[k])
            moved[alpha] = total
        terms = moved
    return terms


def horner(get, degree, x, y, z):
    over_x = None
    for i in range(degree, -1, -1):
        over_y = None
        for j in range(degree - i, -1, -1):
            over_z = None
            for k in range(degree - i - j, -1, -1):
                value = get((i, j, k))
                over_z = value if over_z is None else over_z * z + value
            over_y = over_z if over_y is None else over_y * y + over_z
        over_x = over_y if over_x is None else over_x * x + over_y
    return over_x


def last_kernel(
    counts_ref, send_ref, ids_ref, own_ref, near_ref, self0_ref, self1_ref, leaf_ref, par_ref,
    in0, in1, in2, in3, out_ref, slab_ref, turned_ref, terms_ref, field_ref, near_sum,
):
    incoming = (in0, in1, in2, in3)
    lane128 = iota((1, 128), 1)

    def copy_leaf(c, _):
        put_slab(slab_ref, c, own_ref[c])
        return 0

    lax.fori_loop(0, LEAVES, copy_leaf, 0, unroll=8)

    def both(c, _):
        near_sum[c] = near_ref[c] + self0_ref[c]
        near_sum[c + LEAVES // 2] = near_ref[c + LEAVES // 2] + self1_ref[c]
        return 0

    lax.fori_loop(0, LEAVES // 2, both, 0, unroll=8)

    leaf = leaf_ref[...]
    par = par_ref[...]
    for q in range(4):
        block = get_block(lambda s, q=q: incoming[q][SLOTS + s])
        ids = ids_ref[q : q + 1, :]
        leaf_hot = onehot_rows(LEAVES, jnp.where(lane128 < SLOTS, ids, -1))
        parent_hot = onehot_rows(128, jnp.where(lane128 >= SLOTS, ids, -1))
        leaf = leaf + pick(block, leaf_hot, True)
        par = par + pick(block, parent_hot, True)

        def arrive(k, _, q=q):
            c = send_ref[q * SLOTS + k]
            near_sum[c] = near_sum[c] + incoming[q][k]
            return 0

        lax.fori_loop(0, SLOTS, arrive, 0, unroll=4)
    lane_parent = (iota((128, LEAVES), 1) // CZ % CY // 2) * (CZ // 2) + iota(
        (128, LEAVES), 1
    ) % CZ // 2
    above = pick(par, jnp.where(lane_parent == iota((128, LEAVES), 0), 1.0, 0.0).astype(bf16))
    terms = {alpha: above[n : n + 1, :] for n, alpha in enumerate(ALPHAS)}
    terms = shift_terms(terms, parent_offsets())
    for n, alpha in enumerate(ALPHAS):
        terms_ref[n : n + 1, :] = leaf[n : n + 1, :] + terms[alpha]

    for comp in range(1, 4):
        turned_ref[comp] = get_rows(slab_ref, comp).T

    for half in range(2):
        lanes = slice(half * 128, half * 128 + 128)

        def term(alpha):
            return terms_ref[AT[alpha] : AT[alpha] + 1, lanes]

        def potential_at(alpha):
            return term(alpha) * (1.0 / afact(alpha))

        coefs = [{alpha: potential_at(alpha) for alpha in ALPHAS}]
        for axis in range(3):
            coefs.append(
                {
                    alpha: term(add(alpha, unit(axis))) * (-1.0 / afact(alpha))
                    for alpha in ALPHAS
                    if sum(alpha) <= 3
                }
            )

        def chunk(step, _):
            rows = pl.ds(pl.multiple_of(step * 32, 32), 32)
            x, y, z = [turned_ref[comp, rows, lanes] for comp in range(1, 4)]
            for comp in range(4):
                field_ref[comp, rows, lanes] = horner(
                    lambda alpha, comp=comp: coefs[comp][alpha], 3 if comp else 4, x, y, z
                )
            return 0

        lax.fori_loop(0, LEAF // 32, chunk, 0)

    for comp in range(4):
        turned = field_ref[comp].T
        for half in range(2):
            slab_ref[pl.ds(half * LEAVES * 8 + comp, LEAVES, stride=8), :] = turned[
                :, half * 128 : half * 128 + 128
            ]

    lane = iota((4, LEAF), 1)

    def write(c, _):
        value = jnp.concatenate(
            [
                slab_ref[pl.ds(pl.multiple_of(half * LEAVES * 8 + c * 8, 8), 8), :]
                for half in range(2)
            ],
            1,
        )[0:4] + near_sum[c]
        start = pl.multiple_of(c * LEAF, LEAF)
        out_ref[:, pl.ds(start, LEAF)] = jnp.where(lane < counts_ref[c], value, 0.0)
        return 0

    lax.fori_loop(0, LEAVES, write, 0, unroll=8)


def last(counts, send, ids, own, near, self0, self1, leaf, par, arrived):
    return pl.pallas_call(
        last_kernel,
        name="last",
        out_shape=shaped(4, LEAVES * LEAF),
        in_specs=[SM, SM] + [VM] * 11,
        out_specs=VM,
        scratch_shapes=[
            pltpu.VMEM((LEAVES * 16, 128), f32),
            pltpu.VMEM((4, LEAF, LEAVES), f32),
            pltpu.VMEM((40, LEAVES), f32),
            pltpu.VMEM((4, LEAF, LEAVES), f32),
            pltpu.VMEM((LEAVES, 4, LEAF), f32),
        ],
        compiler_params=pltpu.CompilerParams(**PARAMS),
    )(counts, send, ids, own, near, self0, self1, leaf, par, *arrived)


def image_shift(slab_at, sub_at, slab_count, sub_count):
    rows_out = []
    for direction in range(4):
        reach_x = slab_at + slab_steps[direction]
        reach_y = sub_at + sub_steps[direction]
        jump_x = (reach_x - reach_x % slab_count) * CX
        jump_y = (reach_y - reach_y % sub_count) * CY
        rows_out.append(jnp.stack([jump_x, jump_y]))
    return jnp.stack(rows_out).astype(f32)


def moved_by(value, slab_step, sub_step, slab_count, sub_count):
    pairs = []
    for slab_at in range(slab_count):
        for sub_at in range(sub_count):
            target = (slab_at + slab_step) % slab_count * sub_count + (sub_at + sub_step) % sub_count
            pairs.append((slab_at * sub_count + sub_at, target))
    return lax.ppermute(value, ("slab", "sub"), pairs)


def id_table(send_leaves, send_parents):
    return jnp.concatenate(
        [
            send_leaves.reshape(4, SLOTS),
            send_parents.reshape(4, PSLOTS),
            jnp.full((4, 128 - SLOTS - PSLOTS), -1, jnp.int32),
        ],
        1,
    )


def pad_pairs(pairs):
    filler = jnp.broadcast_to(
        jnp.array([[0], [-1], [0]], jnp.int32), (3, 128 - pairs.shape[1])
    )
    return jnp.concatenate([pairs, filler], 1)


def on_device(
    positions, masses, leaf_counts, send_leaves, send_parents, near_pairs, far_pairs, parent_pairs
):
    slab_count = lax.axis_size("slab")
    sub_count = lax.axis_size("sub")
    slab_at = lax.axis_index("slab")
    sub_at = lax.axis_index("sub")
    at = jnp.stack([slab_at, sub_at]).astype(jnp.int32)
    send = send_leaves[0]
    ids = id_table(send, send_parents[0])
    own, cells, pcells, *outgoing = front(
        at, leaf_counts, send, ids, positions, masses.reshape(-1, 128)
    )
    incoming = [
        moved_by(outgoing[q], -slab_steps[q], -sub_steps[q], slab_count, sub_count)
        for q in range(4)
    ]
    image = image_shift(slab_at, sub_at, slab_count, sub_count)
    self0 = self_part(own, 0, LEAVES // 2)
    leaf, par, backs, moved = far_part(
        image, far_pairs[0], pad_pairs(parent_pairs[0]), near_pairs[0], cells, pcells, incoming
    )
    near, *returning = near_part(near_pairs[0], moved, own, incoming, backs)
    arrived = [
        moved_by(returning[q], slab_steps[q], sub_steps[q], slab_count, sub_count)
        for q in range(4)
    ]
    self1 = self_part(own, LEAVES // 2, LEAVES // 2)
    return last(leaf_counts, send, ids, own, near, self0, self1, leaf, par, arrived)


def solution(mesh):
    return jax.shard_map(
        on_device,
        mesh=mesh,
        in_specs=(
            P(None, ("slab", "sub")),
            P(("slab", "sub")),
            P(("slab", "sub")),
            P(("slab", "sub"), None),
            P(("slab", "sub"), None),
            P(("slab", "sub"), None, None),
            P(("slab", "sub"), None, None),
            P(("slab", "sub"), None, None),
        ),
        out_specs=P(None, ("slab", "sub")),
        check_vma=False,
    )
```

```python
import jax
import jax.numpy as jnp
from jax import lax
from jax.experimental import pallas as pl
from jax.experimental.pallas import tpu as pltpu
from jax.sharding import PartitionSpec as P

CX = 2
CY = 4
CZ = 32
LEAVES = 256
LEAF = 256
PARENTS = 32
SLOTS = 64
PSLOTS = 16
NEAR = 256
FAR = 1024
PFAR = 64
PAY = SLOTS + 5
SOFT = 0.0025
WIDTH = 8
slab_steps = (1, 0, 1, 1)
sub_steps = (0, 1, 1, -1)
f32 = jnp.float32
bf16 = jnp.bfloat16

ALPHAS = [
    (i, j, d - i - j) for d in range(5) for i in range(d, -1, -1) for j in range(d - i, -1, -1)
]
AT = {a: n for n, a in enumerate(ALPHAS)}
FACT = (1.0, 1.0, 2.0, 6.0, 24.0)
TABLE = LEAVES + 4 * 128 + 128


def afact(alpha):
    return FACT[alpha[0]] * FACT[alpha[1]] * FACT[alpha[2]]


def add(a, b):
    return (a[0] + b[0], a[1] + b[1], a[2] + b[2])


def unit(axis):
    return tuple(1 if k == axis else 0 for k in range(3))


def split3(value):
    one = value.astype(bf16)
    rest = value - one.astype(f32)
    two = rest.astype(bf16)
    three = (rest - two.astype(f32)).astype(bf16)
    return one, two, three


def dot_nn(a, b):
    return lax.dot_general(a, b, (((1,), (0,)), ((), ())), preferred_element_type=f32)


def dot_nt(a, b):
    return lax.dot_general(a, b, (((1,), (1,)), ((), ())), preferred_element_type=f32)


def dot_tn(a, b):
    return lax.dot_general(a, b, (((0,), (0,)), ((), ())), preferred_element_type=f32)


def pick(values, onehot, transposed=False):
    parts = jnp.concatenate([part.astype(f32) for part in split3(values)], 0).astype(bf16)
    out = dot_nt(parts, onehot) if transposed else dot_nn(parts, onehot)
    rows = values.shape[0]
    return out[:rows] + out[rows : 2 * rows] + out[2 * rows :]


def iota(shape, dim):
    return lax.broadcasted_iota(jnp.int32, shape, dim)


def onehot_rows(count, ids):
    hit = iota((count, ids.shape[1]), 0) == ids
    return jnp.where(hit, 1.0, 0.0).astype(bf16)


def put_slab(slab_ref, c, slab):
    wide = jnp.concatenate([slab, jnp.zeros((4, LEAF), f32)], 0)
    for half in range(2):
        rows = pl.ds(pl.multiple_of(half * LEAVES * 8 + c * 8, 8), 8)
        slab_ref[rows, :] = wide[:, half * 128 : half * 128 + 128]


def get_rows(slab_ref, comp):
    return jnp.concatenate(
        [slab_ref[pl.ds(half * LEAVES * 8 + comp, LEAVES, stride=8), :] for half in range(2)], 1
    )


def monomials(x, y, z, w):
    made = {(0, 0, 0): w}
    for alpha in ALPHAS[1:]:
        for axis, value in ((2, z), (1, y), (0, x)):
            if alpha[axis]:
                lower = tuple(alpha[k] - (k == axis) for k in range(3))
                made[alpha] = made[lower] * value
                break
    return made


def shift_moments(moments, offsets):
    choose = ((1,), (1, 1), (1, 2, 1), (1, 3, 3, 1), (1, 4, 6, 4, 1))
    for axis in range(3):
        powers = [None, offsets[axis]]
        for _ in range(3):
            powers.append(powers[-1] * offsets[axis])
        moved = {}
        for alpha in ALPHAS:
            total = moments[alpha]
            for k in range(alpha[axis]):
                lower = tuple(k if q == axis else alpha[q] for q in range(3))
                total = total + moments[lower] * powers[alpha[axis] - k] * float(
                    choose[alpha[axis]][k]
                )
            moved[alpha] = total
        moments = moved
    return moments


def leaf_lanes():
    lane = iota((1, LEAVES), 1)
    return lane // (CY * CZ), lane // CZ % CY, lane % CZ


def parent_offsets():
    cell_x, cell_y, cell_z = leaf_lanes()
    return [(cell % 2).astype(f32) - 0.5 for cell in (cell_x, cell_y, cell_z)]


def front_kernel(
    at_ref, counts_ref, send_ref, ids_ref, pos_ref, mass_ref,
    own_ref, cells_ref, pcells_ref, pay0, pay1, pay2, pay3, slab_ref, turned_ref,
):
    pays = (pay0, pay1, pay2, pay3)
    base_x = at_ref[0] * CX
    base_y = at_ref[1] * CY
    row4 = iota((4, LEAF), 0)
    lane = iota((1, LEAF), 1)

    def one_leaf(c, _):
        start = pl.multiple_of(c * LEAF, LEAF)
        place = pos_ref[:, pl.ds(start, LEAF)]
        mass = jnp.concatenate(
            [mass_ref[pl.ds(2 * c, 1), :], mass_ref[pl.ds(2 * c + 1, 1), :]], 1
        )
        weight = jnp.where(lane < counts_ref[c], mass, 0.0)
        centre_x = (base_x + c // (CY * CZ)).astype(f32) + 0.5
        centre_y = (base_y + c // CZ % CY).astype(f32) + 0.5
        centre_z = (c % CZ).astype(f32) + 0.5
        centre = jnp.where(row4 == 1, centre_x, jnp.where(row4 == 2, centre_y, centre_z))
        centre = jnp.where(row4 == 0, 0.0, centre)
        slab = jnp.concatenate([weight, place], 0) - centre
        own_ref[c] = slab
        put_slab(slab_ref, c, slab)
        return 0

    lax.fori_loop(0, LEAVES, one_leaf, 0, unroll=8)

    for comp in range(4):
        turned_ref[comp] = get_rows(slab_ref, comp).T

    for half in range(2):
        lanes = slice(half * 128, half * 128 + 128)

        def chunk(step, totals):
            rows = pl.ds(pl.multiple_of(step * 8, 8), 8)
            w, x, y, z = [turned_ref[comp, rows, lanes] for comp in range(4)]
            made = monomials(x, y, z, w)
            return tuple(total + made[alpha] for total, alpha in zip(totals, ALPHAS))

        totals = lax.fori_loop(
            0, LEAF // 8, chunk, tuple(jnp.zeros((8, 128), f32) for _ in ALPHAS)
        )
        for n, total in enumerate(totals):
            cells_ref[n : n + 1, lanes] = jnp.sum(total, 0, keepdims=True)

    cell_x, cell_y, cell_z = leaf_lanes()
    cells_ref[35:36, :] = (base_x + cell_x).astype(f32) + 0.5
    cells_ref[36:37, :] = (base_y + cell_y).astype(f32) + 0.5
    cells_ref[37:38, :] = cell_z.astype(f32) + 0.5
    cells_ref[38:40, :] = jnp.zeros((2, LEAVES), f32)

    moments = {alpha: cells_ref[n : n + 1, :] for n, alpha in enumerate(ALPHAS)}
    moved = shift_moments(moments, parent_offsets())
    moved = jnp.concatenate(
        [moved[alpha] for alpha in ALPHAS] + [jnp.zeros((5, LEAVES), f32)], 0
    )
    parent_of = (iota((LEAVES, 128), 0) // CZ % CY // 2) * (CZ // 2) + iota(
        (LEAVES, 128), 0
    ) % CZ // 2
    belongs = jnp.where(parent_of == iota((LEAVES, 128), 1), 1.0, 0.0).astype(bf16)
    pcells = pick(moved, belongs)
    plane = iota((40, 128), 1)
    prow = iota((40, 128), 0)
    pcells = jnp.where(prow == 35, (base_x + 1).astype(f32), pcells)
    pcells = jnp.where(
        prow == 36, (base_y + 2 * (plane // (CZ // 2))).astype(f32) + 1.0, pcells
    )
    pcells = jnp.where(prow == 37, (2 * (plane % (CZ // 2))).astype(f32) + 1.0, pcells)
    pcells_ref[...] = pcells

    lane128 = iota((1, 128), 1)
    for q in range(4):
        pay = pays[q]

        def copy_leaf(k, _, pay=pay, q=q):
            pay[k] = own_ref[send_ref[q * SLOTS + k]]
            return 0

        lax.fori_loop(0, SLOTS, copy_leaf, 0, unroll=8)
        ids = ids_ref[q : q + 1, :]
        leaf_hot = onehot_rows(LEAVES, jnp.where(lane128 < SLOTS, ids, -1))
        parent_hot = onehot_rows(128, jnp.where(lane128 >= SLOTS, ids, -1))
        block = pick(cells_ref[...], leaf_hot) + pick(pcells, parent_hot)
        put_block(pay, block)


def put_block(pay, block):
    for s in range(5):
        pay[SLOTS + s, :, 0:128] = block[4 * s : 4 * s + 4]
        pay[SLOTS + s, :, 128:256] = block[20 + 4 * s : 24 + 4 * s]


def get_block(tail):
    return jnp.concatenate(
        [tail(s)[:, 0:128] for s in range(5)] + [tail(s)[:, 128:256] for s in range(5)], 0
    )


VM = pl.BlockSpec(memory_space=pltpu.VMEM)
SM = pl.BlockSpec(memory_space=pltpu.SMEM)
HB = pl.BlockSpec(memory_space=pl.ANY)
PARAMS = dict(vmem_limit_bytes=48 * 1024 * 1024)


def shaped(*shape):
    return jax.ShapeDtypeStruct(shape, f32)


def front(at, counts, send, ids, positions, masses):
    return pl.pallas_call(
        front_kernel,
        name="front",
        out_shape=[
            shaped(LEAVES, 4, LEAF), shaped(40, LEAVES), shaped(40, 128),
        ] + [shaped(PAY, 4, LEAF)] * 4,
        in_specs=[SM, SM, SM, VM, VM, VM],
        out_specs=[VM] * 7,
        scratch_shapes=[
            pltpu.VMEM((LEAVES * 16, 128), f32),
            pltpu.VMEM((4, LEAF, LEAVES), f32),
        ],
        compiler_params=pltpu.CompilerParams(**PARAMS),
    )(at, counts, send, ids, positions, masses)


def slab8(slab):
    return jnp.concatenate([slab, jnp.zeros((4, LEAF), f32)], 0)


def b_form(points):
    row = iota(points.shape, 0)
    square = jnp.sum(jnp.where(row == 0, 0.0, points * points), 0, keepdims=True)
    return jnp.where(row == 4, square, points)


def a_form(points):
    row = iota(points.shape, 0)
    square = jnp.sum(jnp.where(row == 0, 0.0, points * points), 0, keepdims=True)
    value = jnp.where(row == 0, square + SOFT, -2.0 * points)
    return jnp.where(row == 4, 1.0, value)


def widen(value):
    one = value.astype(bf16).astype(f32)
    rest = value - one
    two = rest.astype(bf16).astype(f32)
    return one, two, rest - two


def squares(a_points, b_points):
    a1, a2, a3 = widen(a_form(a_points))
    b1, b2, b3 = widen(b_form(b_points))
    left = jnp.concatenate([a1, a1, a2, a2, a1, a3], 0).astype(bf16)
    right = jnp.concatenate([b1, b2, b1, b2, b3, b1], 0).astype(bf16)
    return dot_tn(left, right)


def sources(points, weight):
    parts = widen(b_form(points) * weight)
    return jnp.concatenate(parts + (jnp.zeros_like(parts[0]),), 0).astype(bf16)


def fold(out):
    total = out[0:8]
    for first in range(8, out.shape[0] // 8 * 8, 8):
        total = total + out[first : first + 8]
    return total


def finish(total, points):
    row = iota(points.shape, 0)
    mass = total[0:1]
    square = b_form(points)[4:5]
    along = jnp.sum(jnp.where((row >= 1) & (row <= 3), points * total, 0.0), 0, keepdims=True)
    potential = total[4:5] + (square + SOFT) * mass - 2.0 * along
    return jnp.where(row == 0, -potential, total - points * mass)[0:4]


def load_points(slab):
    wide = slab8(slab)
    row = iota((8, LEAF), 0)
    return jnp.where(row == 0, 1.0, wide), slab[0:1]


def self_kernel(own_ref, out_ref):
    apart = jnp.where(iota((LEAF, LEAF), 0) == iota((LEAF, LEAF), 1), 0.0, 1.0)

    def some_leaves(step, _):
        first = step * WIDTH
        loaded = [load_points(own_ref[first + k]) for k in range(WIDTH)]
        spaced = [squares(points, points) for points, _ in loaded]
        cubes = []
        for value in spaced:
            inverse = lax.rsqrt(value) * apart
            cubes.append(inverse * inverse * inverse)
        high = [cube.astype(bf16) for cube in cubes]
        for k, (points, weight) in enumerate(loaded):
            low = (cubes[k] - high[k].astype(f32)).astype(bf16)
            side = sources(points, weight)
            total = fold(dot_nn(side, high[k])) + fold(dot_nn(side[0:16], low))
            out_ref[first + k] = finish(total, points)
        return 0

    lax.fori_loop(0, own_ref.shape[0] // WIDTH, some_leaves, 0)


def self_part(own, first, count):
    block = 32
    return pl.pallas_call(
        self_kernel,
        name="self_part",
        grid=(count // block,),
        out_shape=shaped(count, 4, LEAF),
        in_specs=[pl.BlockSpec((block, 4, LEAF), lambda i: (i + first // block, 0, 0))],
        out_specs=pl.BlockSpec((block, 4, LEAF), lambda i: (i, 0, 0)),
        cost_estimate=pl.CostEstimate(
            flops=count * 40_000_000, bytes_accessed=count * 8192, transcendentals=0
        ),
        compiler_params=pltpu.CompilerParams(**PARAMS),
    )(own)


def near_kernel(
    pairs_ref, moved_ref, own_ref, in0, in1, in2, in3, backs_ref,
    out_ref, pay0, pay1, pay2, pay3, table, total, sem,
):
    pays = (pay0, pay1, pay2, pay3)
    copies = [pltpu.make_async_copy(own_ref, table.at[pl.ds(0, LEAVES)], sem.at[0])]
    for q, part in enumerate((in0, in1, in2, in3)):
        copies.append(
            pltpu.make_async_copy(
                part.at[pl.ds(0, SLOTS)],
                table.at[pl.ds(LEAVES + q * SLOTS, SLOTS)],
                sem.at[1 + q],
            )
        )
    for copy in copies:
        copy.start()

    def clear(c, _):
        total[c] = jnp.zeros((8, LEAF), f32)
        return 0

    lax.fori_loop(0, 2 * LEAVES, clear, 0, unroll=8)
    for copy in copies:
        copy.wait()

    row = iota((8, LEAF), 0)

    def some_pairs(step, _):
        first = step * WIDTH
        ends, loaded = [], []
        for k in range(WIDTH):
            p = first + k
            a = pairs_ref[0, p]
            listed = pairs_ref[1, p]
            b = jnp.maximum(listed, 0)
            used = jnp.where(listed >= 0, 1.0, 0.0)
            points_a, weight_a = load_points(table[a])
            points_b, weight_b = load_points(table[b])
            shift = jnp.where(
                row == 1,
                moved_ref[0, p],
                jnp.where(row == 2, moved_ref[1, p], jnp.where(row == 3, moved_ref[2, p], 0.0)),
            )
            ends.append((a, b))
            loaded.append((points_a + shift, weight_a * used, points_b, weight_b * used, shift))
        spaced = [squares(from_b, points_b) for from_b, _, points_b, _, _ in loaded]
        high = []
        for value in spaced:
            inverse = lax.rsqrt(value)
            high.append((inverse * inverse * inverse).astype(bf16))
        done = []
        for (from_b, weight_a, points_b, weight_b, shift), cube in zip(loaded, high):
            to_b = fold(dot_nn(sources(from_b, weight_a), cube))
            to_a = fold(dot_nt(sources(points_b - shift, weight_b), cube))
            done.append((to_a, to_b))
        for (a, b), (to_a, to_b) in zip(ends, done):
            total[a] = total[a] + to_a
            total[b] = total[b] + to_b
        return 0

    def count_used(p, n):
        return n + jnp.where(pairs_ref[1, p] >= 0, 1, 0)

    used_pairs = lax.fori_loop(0, NEAR, count_used, 0)
    lax.fori_loop(0, (used_pairs + WIDTH - 1) // WIDTH, some_pairs, 0)

    def finish_own(c, _):
        points, _ = load_points(table[c])
        out_ref[c] = finish(total[c], points)
        return 0

    lax.fori_loop(0, LEAVES, finish_own, 0, unroll=8)
    for q in range(4):

        def finish_other(k, _, q=q):
            points, _ = load_points(table[LEAVES + q * SLOTS + k])
            pays[q][k] = finish(total[LEAVES + q * SLOTS + k], points)
            return 0

        lax.fori_loop(0, SLOTS, finish_other, 0, unroll=8)
        put_block(pays[q], backs_ref[q])


def near_part(pairs, moved, own, incoming, backs):
    return pl.pallas_call(
        near_kernel,
        name="near_part",
        out_shape=[shaped(LEAVES, 4, LEAF)] + [shaped(PAY, 4, LEAF)] * 4,
        in_specs=[SM, SM, HB, HB, HB, HB, HB, VM],
        out_specs=[VM] * 5,
        scratch_shapes=[
            pltpu.VMEM((2 * LEAVES, 4, LEAF), f32),
            pltpu.VMEM((2 * LEAVES, 8, LEAF), f32),
            pltpu.SemaphoreType.DMA((5,)),
        ],
        cost_estimate=pl.CostEstimate(
            flops=NEAR * 80_000_000, bytes_accessed=4_000_000, transcendentals=0
        ),
        compiler_params=pltpu.CompilerParams(**PARAMS),
    )(pairs, moved, own, *incoming, backs)


def derivatives(x, y, z):
    square = x * x + y * y + z * z
    inverse = 1.0 / jnp.sqrt(square)
    inverse2 = inverse * inverse
    table = {(0, (0, 0, 0)): inverse}
    for m in range(1, 5):
        table[(m, (0, 0, 0))] = table[(m - 1, (0, 0, 0))] * inverse2 * float(-(2 * m - 1))
    place = (x, y, z)

    def entry(m, alpha):
        key = (m, alpha)
        if key not in table:
            axis = [k for k in range(3) if alpha[k]][0]
            lower = tuple(alpha[k] - (k == axis) for k in range(3))
            value = place[axis] * entry(m + 1, lower)
            if lower[axis]:
                lowest = tuple(lower[k] - (k == axis) for k in range(3))
                value = value + float(lower[axis]) * entry(m + 1, lowest)
            table[key] = value
        return table[key]

    return {alpha: entry(0, alpha) for alpha in ALPHAS}


def mutual(a_ref, b_ref, to_a, to_b):
    def rows(n):
        return pl.ds(n * 8, 8)

    lift = a_ref[rows(38), :]
    live = a_ref[rows(39), :] > 0.5
    gap = [
        jnp.where(live, a_ref[rows(35 + k), :] - b_ref[rows(35 + k), :] - (lift if k == 2 else 0.0), 3.0)
        for k in range(3)
    ]
    made = derivatives(*gap)
    for beta in ALPHAS:
        sum_a = None
        sum_b = None
        for alpha in ALPHAS:
            if sum(alpha) + sum(beta) > 4:
                continue
            tensor = made[add(alpha, beta)]
            scale = 1.0 / afact(alpha)
            sign_a = -((-1.0) ** sum(alpha)) * scale
            sign_b = -((-1.0) ** sum(beta)) * scale
            term_a = b_ref[rows(AT[alpha]), :] * sign_a * tensor
            term_b = a_ref[rows(AT[alpha]), :] * sign_b * tensor
            sum_a = term_a if sum_a is None else sum_a + term_a
            sum_b = term_b if sum_b is None else sum_b + term_b
        to_a[rows(AT[beta]), :] = jnp.where(live, sum_a, 0.0)
        to_b[rows(AT[beta]), :] = jnp.where(live, sum_b, 0.0)


def far_kernel(
    image_ref, far_ref, parent_ref, near_ref, cells_ref, pcells_ref, in0, in1, in2, in3,
    leaf_ref, par_ref, backs_ref, moved_ref, tails, table, left, right, to_a, to_b, total, sem,
):
    copies = []
    for q, part in enumerate((in0, in1, in2, in3)):
        copies.append(
            pltpu.make_async_copy(part.at[pl.ds(SLOTS, 5)], tails.at[q], sem.at[q])
        )
    for copy in copies:
        copy.start()
    table[:, 0:LEAVES] = cells_ref[...]
    table[:, LEAVES + 512 :] = pcells_ref[...]
    row = iota((40, 128), 0)
    to_a[...] = jnp.zeros_like(to_a)
    to_b[...] = jnp.zeros_like(to_b)
    left[...] = jnp.zeros_like(left)
    right[...] = jnp.zeros_like(right)
    for copy in copies:
        copy.wait()
    for q in range(4):
        block = get_block(lambda s, q=q: tails[q, s])
        block = block + jnp.where(
            row == 35, image_ref[q, 0], jnp.where(row == 36, image_ref[q, 1], 0.0)
        )
        table[:, LEAVES + q * 128 : LEAVES + q * 128 + 128] = block
    parts = jnp.concatenate([part.astype(f32) for part in split3(table[...])], 0).astype(bf16)
    total[...] = jnp.zeros_like(total)

    def gathered(hot, first, count):
        out = dot_nn(parts[:, first : first + count], hot)
        return out[0:40] + out[40:80] + out[80:120]

    def leaf_entry(ids):
        other = ids - LEAVES
        return jnp.where(ids < LEAVES, ids, LEAVES + other // SLOTS * 128 + other % SLOTS)

    def parent_entry(ids):
        other = ids - PARENTS
        return jnp.where(
            ids < PARENTS, LEAVES + 512 + ids, LEAVES + other // PSLOTS * 128 + SLOTS + other % PSLOTS
        )

    def hots(ids_a, ids_b, parents):
        if parents:
            return (
                onehot_rows(128, ids_a), LEAVES + 512, 128,
                onehot_rows(640, parent_entry(ids_b) - LEAVES), LEAVES, 640,
            )
        return (
            onehot_rows(LEAVES, ids_a), 0, LEAVES,
            onehot_rows(768, leaf_entry(ids_b)), 0, 768,
        )

    def load(ids_a, ids_b, lifts, g, parents):
        hot_a, first_a, count_a, hot_b, first_b, count_b = hots(ids_a, ids_b, parents)
        from_a = gathered(hot_a, first_a, count_a)
        from_b = gathered(hot_b, first_b, count_b)
        live = jnp.where(ids_b >= 0, 1.0, 0.0)
        from_a = jnp.where(row == 38, lifts.astype(f32) * float(CZ), from_a)
        from_a = jnp.where(row == 39, live, from_a)
        left[pl.ds(g, 40, stride=8), :] = from_a
        right[pl.ds(g, 40, stride=8), :] = from_b

    def store(ids_a, ids_b, g, parents):
        hot_a, first_a, count_a, hot_b, first_b, count_b = hots(ids_a, ids_b, parents)
        sum_a = pick(to_a[pl.ds(g, 40, stride=8), :], hot_a, True)
        sum_b = pick(to_b[pl.ds(g, 40, stride=8), :], hot_b, True)
        total[:, first_a : first_a + count_a] += sum_a
        total[:, first_b : first_b + count_b] += sum_b

    for g in range(FAR // 128):
        lanes = slice(g * 128, g * 128 + 128)
        load(far_ref[0:1, lanes], far_ref[1:2, lanes], far_ref[2:3, lanes], g, False)
    mutual(left, right, to_a, to_b)
    for g in range(FAR // 128):
        lanes = slice(g * 128, g * 128 + 128)
        store(far_ref[0:1, lanes], far_ref[1:2, lanes], g, False)
    load(parent_ref[0:1, :], parent_ref[1:2, :], parent_ref[2:3, :], 0, True)
    mutual(left, right, to_a, to_b)
    store(parent_ref[0:1, :], parent_ref[1:2, :], 0, True)

    for g in range(NEAR // 128):
        lanes = slice(g * 128, g * 128 + 128)
        hot_a, _, _, hot_b, _, _ = hots(near_ref[0:1, lanes], near_ref[1:2, lanes], False)
        apart = gathered(hot_a, 0, LEAVES) - gathered(hot_b, 0, 768)
        apart = jnp.where(row == 37, apart - near_ref[2:3, lanes].astype(f32) * float(CZ), apart)
        for k in range(3):
            moved_ref[k : k + 1, lanes] = apart[35 + k : 36 + k, :]

    leaf_ref[...] = total[:, 0:LEAVES]
    par_ref[...] = total[:, LEAVES + 512 :]
    for q in range(4):
        backs_ref[q] = total[:, LEAVES + q * 128 : LEAVES + q * 128 + 128]


def far_part(image, far, parent, near, cells, pcells, incoming):
    return pl.pallas_call(
        far_kernel,
        name="far_part",
        out_shape=[
            shaped(40, LEAVES), shaped(40, 128), shaped(4, 40, 128), shaped(3, NEAR),
        ],
        in_specs=[SM, VM, VM, VM, VM, VM, HB, HB, HB, HB],
        out_specs=[VM] * 4,
        scratch_shapes=[
            pltpu.VMEM((4, 5, 4, LEAF), f32),
            pltpu.VMEM((40, TABLE), f32),
        ] + [pltpu.VMEM((320, 128), f32)] * 4 + [
            pltpu.VMEM((40, TABLE), f32),
            pltpu.SemaphoreType.DMA((4,)),
        ],
        compiler_params=pltpu.CompilerParams(**PARAMS),
    )(image, far, parent, near, cells, pcells, *incoming)


def shift_terms(terms, offsets):
    for axis in range(3):
        powers = [None, offsets[axis]]
        for _ in range(3):
            powers.append(powers[-1] * offsets[axis])
        moved = {}
        for alpha in ALPHAS:
            total = terms[alpha]
            for k in range(1, 5 - sum(alpha)):
                upper = tuple(alpha[q] + k * (q == axis) for q in range(3))
                total = total + terms[upper] * powers[k] * (1.0 / FACT[k])
            moved[alpha] = total
        terms = moved
    return terms


def horner(get, degree, x, y, z):
    over_x = None
    for i in range(degree, -1, -1):
        over_y = None
        for j in range(degree - i, -1, -1):
            over_z = None
            for k in range(degree - i - j, -1, -1):
                value = get((i, j, k))
                over_z = value if over_z is None else over_z * z + value
            over_y = over_z if over_y is None else over_y * y + over_z
        over_x = over_y if over_x is None else over_x * x + over_y
    return over_x


def last_kernel(
    counts_ref, send_ref, ids_ref, own_ref, near_ref, self0_ref, self1_ref, leaf_ref, par_ref,
    in0, in1, in2, in3, out_ref, slab_ref, turned_ref, terms_ref, field_ref, near_sum,
):
    incoming = (in0, in1, in2, in3)
    lane128 = iota((1, 128), 1)

    def copy_leaf(c, _):
        put_slab(slab_ref, c, own_ref[c])
        return 0

    lax.fori_loop(0, LEAVES, copy_leaf, 0, unroll=8)

    def both(c, _):
        near_sum[c] = near_ref[c] + self0_ref[c]
        near_sum[c + LEAVES // 2] = near_ref[c + LEAVES // 2] + self1_ref[c]
        return 0

    lax.fori_loop(0, LEAVES // 2, both, 0, unroll=8)

    leaf = leaf_ref[...]
    par = par_ref[...]
    for q in range(4):
        block = get_block(lambda s, q=q: incoming[q][SLOTS + s])
        ids = ids_ref[q : q + 1, :]
        leaf_hot = onehot_rows(LEAVES, jnp.where(lane128 < SLOTS, ids, -1))
        parent_hot = onehot_rows(128, jnp.where(lane128 >= SLOTS, ids, -1))
        leaf = leaf + pick(block, leaf_hot, True)
        par = par + pick(block, parent_hot, True)

        def arrive(k, _, q=q):
            c = send_ref[q * SLOTS + k]
            near_sum[c] = near_sum[c] + incoming[q][k]
            return 0

        lax.fori_loop(0, SLOTS, arrive, 0, unroll=4)
    lane_parent = (iota((128, LEAVES), 1) // CZ % CY // 2) * (CZ // 2) + iota(
        (128, LEAVES), 1
    ) % CZ // 2
    above = pick(par, jnp.where(lane_parent == iota((128, LEAVES), 0), 1.0, 0.0).astype(bf16))
    terms = {alpha: above[n : n + 1, :] for n, alpha in enumerate(ALPHAS)}
    terms = shift_terms(terms, parent_offsets())
    for n, alpha in enumerate(ALPHAS):
        terms_ref[n : n + 1, :] = leaf[n : n + 1, :] + terms[alpha]

    for comp in range(1, 4):
        turned_ref[comp] = get_rows(slab_ref, comp).T

    for half in range(2):
        lanes = slice(half * 128, half * 128 + 128)

        def term(alpha):
            return terms_ref[AT[alpha] : AT[alpha] + 1, lanes]

        def potential_at(alpha):
            return term(alpha) * (1.0 / afact(alpha))

        coefs = [{alpha: potential_at(alpha) for alpha in ALPHAS}]
        for axis in range(3):
            coefs.append(
                {
                    alpha: term(add(alpha, unit(axis))) * (-1.0 / afact(alpha))
                    for alpha in ALPHAS
                    if sum(alpha) <= 3
                }
            )

        def chunk(step, _):
            rows = pl.ds(pl.multiple_of(step * 32, 32), 32)
            x, y, z = [turned_ref[comp, rows, lanes] for comp in range(1, 4)]
            for comp in range(4):
                field_ref[comp, rows, lanes] = horner(
                    lambda alpha, comp=comp: coefs[comp][alpha], 3 if comp else 4, x, y, z
                )
            return 0

        lax.fori_loop(0, LEAF // 32, chunk, 0)

    for comp in range(4):
        turned = field_ref[comp].T
        for half in range(2):
            slab_ref[pl.ds(half * LEAVES * 8 + comp, LEAVES, stride=8), :] = turned[
                :, half * 128 : half * 128 + 128
            ]

    lane = iota((4, LEAF), 1)

    def write(c, _):
        value = jnp.concatenate(
            [
                slab_ref[pl.ds(pl.multiple_of(half * LEAVES * 8 + c * 8, 8), 8), :]
                for half in range(2)
            ],
            1,
        )[0:4] + near_sum[c]
        start = pl.multiple_of(c * LEAF, LEAF)
        out_ref[:, pl.ds(start, LEAF)] = jnp.where(lane < counts_ref[c], value, 0.0)
        return 0

    lax.fori_loop(0, LEAVES, write, 0, unroll=8)


def last(counts, send, ids, own, near, self0, self1, leaf, par, arrived):
    return pl.pallas_call(
        last_kernel,
        name="last",
        out_shape=shaped(4, LEAVES * LEAF),
        in_specs=[SM, SM] + [VM] * 11,
        out_specs=VM,
        scratch_shapes=[
            pltpu.VMEM((LEAVES * 16, 128), f32),
            pltpu.VMEM((4, LEAF, LEAVES), f32),
            pltpu.VMEM((40, LEAVES), f32),
            pltpu.VMEM((4, LEAF, LEAVES), f32),
            pltpu.VMEM((LEAVES, 4, LEAF), f32),
        ],
        compiler_params=pltpu.CompilerParams(**PARAMS),
    )(counts, send, ids, own, near, self0, self1, leaf, par, *arrived)


def image_shift(slab_at, sub_at, slab_count, sub_count):
    rows_out = []
    for direction in range(4):
        reach_x = slab_at + slab_steps[direction]
        reach_y = sub_at + sub_steps[direction]
        jump_x = (reach_x - reach_x % slab_count) * CX
        jump_y = (reach_y - reach_y % sub_count) * CY
        rows_out.append(jnp.stack([jump_x, jump_y]))
    return jnp.stack(rows_out).astype(f32)


def moved_by(value, slab_step, sub_step, slab_count, sub_count):
    pairs = []
    for slab_at in range(slab_count):
        for sub_at in range(sub_count):
            target = (slab_at + slab_step) % slab_count * sub_count + (sub_at + sub_step) % sub_count
            pairs.append((slab_at * sub_count + sub_at, target))
    return lax.ppermute(value, ("slab", "sub"), pairs)


def id_table(send_leaves, send_parents):
    return jnp.concatenate(
        [
            send_leaves.reshape(4, SLOTS),
            send_parents.reshape(4, PSLOTS),
            jnp.full((4, 128 - SLOTS - PSLOTS), -1, jnp.int32),
        ],
        1,
    )


def pad_pairs(pairs):
    filler = jnp.broadcast_to(
        jnp.array([[0], [-1], [0]], jnp.int32), (3, 128 - pairs.shape[1])
    )
    return jnp.concatenate([pairs, filler], 1)


def on_device(
    positions, masses, leaf_counts, send_leaves, send_parents, near_pairs, far_pairs, parent_pairs
):
    slab_count = lax.axis_size("slab")
    sub_count = lax.axis_size("sub")
    slab_at = lax.axis_index("slab")
    sub_at = lax.axis_index("sub")
    at = jnp.stack([slab_at, sub_at]).astype(jnp.int32)
    send = send_leaves[0]
    ids = id_table(send, send_parents[0])
    own, cells, pcells, *outgoing = front(
        at, leaf_counts, send, ids, positions, masses.reshape(-1, 128)
    )
    incoming = [
        moved_by(outgoing[q], -slab_steps[q], -sub_steps[q], slab_count, sub_count)
        for q in range(4)
    ]
    image = image_shift(slab_at, sub_at, slab_count, sub_count)
    self0 = self_part(own, 0, LEAVES // 2)
    leaf, par, backs, moved = far_part(
        image, far_pairs[0], pad_pairs(parent_pairs[0]), near_pairs[0], cells, pcells, incoming
    )
    near, *returning = near_part(near_pairs[0], moved, own, incoming, backs)
    arrived = [
        moved_by(returning[q], slab_steps[q], sub_steps[q], slab_count, sub_count)
        for q in range(4)
    ]
    self1 = self_part(own, LEAVES // 2, LEAVES // 2)
    return last(leaf_counts, send, ids, own, near, self0, self1, leaf, par, arrived)


def solution(mesh):
    return jax.shard_map(
        on_device,
        mesh=mesh,
        in_specs=(
            P(None, ("slab", "sub")),
            P(("slab", "sub")),
            P(("slab", "sub")),
            P(("slab", "sub"), None),
            P(("slab", "sub"), None),
            P(("slab", "sub"), None, None),
            P(("slab", "sub"), None, None),
            P(("slab", "sub"), None, None),
        ),
        out_specs=P(None, ("slab", "sub")),
        check_vma=False,
    )
```

```python
import jax
import jax.numpy as jnp
from jax import lax
from jax.experimental import pallas as pl
from jax.experimental.pallas import tpu as pltpu
from jax.sharding import PartitionSpec as P

CX = 2
CY = 4
CZ = 32
LEAVES = 256
LEAF = 256
PARENTS = 32
SLOTS = 64
PSLOTS = 16
NEAR = 256
FAR = 1024
PFAR = 64
PAY = SLOTS + 5
SOFT = 0.0025
WIDTH = 8
CLASSES = (128, 192, 256)
SORTED = 384
slab_steps = (1, 0, 1, 1)
sub_steps = (0, 1, 1, -1)
f32 = jnp.float32
bf16 = jnp.bfloat16

ALPHAS = [
    (i, j, d - i - j) for d in range(5) for i in range(d, -1, -1) for j in range(d - i, -1, -1)
]
AT = {a: n for n, a in enumerate(ALPHAS)}
FACT = (1.0, 1.0, 2.0, 6.0, 24.0)
TABLE = LEAVES + 4 * 128 + 128


def afact(alpha):
    return FACT[alpha[0]] * FACT[alpha[1]] * FACT[alpha[2]]


def add(a, b):
    return (a[0] + b[0], a[1] + b[1], a[2] + b[2])


def unit(axis):
    return tuple(1 if k == axis else 0 for k in range(3))


def split3(value):
    one = value.astype(bf16)
    rest = value - one.astype(f32)
    two = rest.astype(bf16)
    three = (rest - two.astype(f32)).astype(bf16)
    return one, two, three


def dot_nn(a, b):
    return lax.dot_general(a, b, (((1,), (0,)), ((), ())), preferred_element_type=f32)


def dot_nt(a, b):
    return lax.dot_general(a, b, (((1,), (1,)), ((), ())), preferred_element_type=f32)


def dot_tn(a, b):
    return lax.dot_general(a, b, (((0,), (0,)), ((), ())), preferred_element_type=f32)


def pick(values, onehot, transposed=False):
    parts = jnp.concatenate([part.astype(f32) for part in split3(values)], 0).astype(bf16)
    out = dot_nt(parts, onehot) if transposed else dot_nn(parts, onehot)
    rows = values.shape[0]
    return out[:rows] + out[rows : 2 * rows] + out[2 * rows :]


def iota(shape, dim):
    return lax.broadcasted_iota(jnp.int32, shape, dim)


def onehot_rows(count, ids):
    hit = iota((count, ids.shape[1]), 0) == ids
    return jnp.where(hit, 1.0, 0.0).astype(bf16)


def fetch_all(moves, sem):
    copies = [
        pltpu.make_async_copy(source, target, sem.at[n])
        for n, (source, target) in enumerate(moves)
    ]
    for copy in copies:
        copy.start()
    for copy in copies:
        copy.wait()


def id_row(sent_leaves, sent_parents, q):
    return jnp.concatenate(
        [
            sent_leaves[:, q * SLOTS : (q + 1) * SLOTS],
            sent_parents[:, q * PSLOTS : (q + 1) * PSLOTS],
            jnp.full((1, 128 - SLOTS - PSLOTS), -1, jnp.int32),
        ],
        1,
    )


def put_slab(slab_ref, c, slab):
    wide = jnp.concatenate([slab, jnp.zeros((4, LEAF), f32)], 0)
    for half in range(2):
        rows = pl.ds(pl.multiple_of(half * LEAVES * 8 + c * 8, 8), 8)
        slab_ref[rows, :] = wide[:, half * 128 : half * 128 + 128]


def get_rows(slab_ref, comp):
    return jnp.concatenate(
        [slab_ref[pl.ds(half * LEAVES * 8 + comp, LEAVES, stride=8), :] for half in range(2)], 1
    )


def monomials(x, y, z, w):
    made = {(0, 0, 0): w}
    for alpha in ALPHAS[1:]:
        for axis, value in ((2, z), (1, y), (0, x)):
            if alpha[axis]:
                lower = tuple(alpha[k] - (k == axis) for k in range(3))
                made[alpha] = made[lower] * value
                break
    return made


def shift_moments(moments, offsets):
    choose = ((1,), (1, 1), (1, 2, 1), (1, 3, 3, 1), (1, 4, 6, 4, 1))
    for axis in range(3):
        powers = [None, offsets[axis]]
        for _ in range(3):
            powers.append(powers[-1] * offsets[axis])
        moved = {}
        for alpha in ALPHAS:
            total = moments[alpha]
            for k in range(alpha[axis]):
                lower = tuple(k if q == axis else alpha[q] for q in range(3))
                total = total + moments[lower] * powers[alpha[axis] - k] * float(
                    choose[alpha[axis]][k]
                )
            moved[alpha] = total
        moments = moved
    return moments


def leaf_lanes():
    lane = iota((1, LEAVES), 1)
    return lane // (CY * CZ), lane // CZ % CY, lane % CZ


def parent_offsets():
    cell_x, cell_y, cell_z = leaf_lanes()
    return [(cell % 2).astype(f32) - 0.5 for cell in (cell_x, cell_y, cell_z)]


def front_kernel(
    at_ref, counts_row, sent_leaves, sent_parents, counts_hbm, send_hbm, pos_hbm, mass_hbm,
    own_ref, cells_ref, pcells_ref, pay0, pay1, pay2, pay3,
    slab_ref, turned_ref, pos_ref, mass_ref, counts_ref, send_ref, sem,
):
    pays = (pay0, pay1, pay2, pay3)
    fetch_all(
        ((counts_hbm, counts_ref), (send_hbm, send_ref), (pos_hbm, pos_ref), (mass_hbm, mass_ref)),
        sem,
    )
    base_x = at_ref[0] * CX
    base_y = at_ref[1] * CY
    row4 = iota((4, LEAF), 0)
    lane = iota((1, LEAF), 1)

    def one_leaf(c, _):
        start = pl.multiple_of(c * LEAF, LEAF)
        place = pos_ref[:, pl.ds(start, LEAF)]
        mass = jnp.concatenate(
            [mass_ref[pl.ds(2 * c, 1), :], mass_ref[pl.ds(2 * c + 1, 1), :]], 1
        )
        weight = jnp.where(lane < counts_ref[c], mass, 0.0)
        centre_x = (base_x + c // (CY * CZ)).astype(f32) + 0.5
        centre_y = (base_y + c // CZ % CY).astype(f32) + 0.5
        centre_z = (c % CZ).astype(f32) + 0.5
        centre = jnp.where(row4 == 1, centre_x, jnp.where(row4 == 2, centre_y, centre_z))
        centre = jnp.where(row4 == 0, 0.0, centre)
        slab = jnp.concatenate([weight, place], 0) - centre
        own_ref[c] = slab
        put_slab(slab_ref, c, slab)
        return 0

    lax.fori_loop(0, LEAVES, one_leaf, 0, unroll=8)

    for comp in range(4):
        turned_ref[comp] = get_rows(slab_ref, comp).T

    for half in range(2):
        lanes = slice(half * 128, half * 128 + 128)

        def chunk(step, totals):
            rows = pl.ds(pl.multiple_of(step * 8, 8), 8)
            w, x, y, z = [turned_ref[comp, rows, lanes] for comp in range(4)]
            made = monomials(x, y, z, w)
            return tuple(total + made[alpha] for total, alpha in zip(totals, ALPHAS))

        totals = lax.fori_loop(
            0, LEAF // 8, chunk, tuple(jnp.zeros((8, 128), f32) for _ in ALPHAS)
        )
        for n, total in enumerate(totals):
            cells_ref[n : n + 1, lanes] = jnp.sum(total, 0, keepdims=True)

    cell_x, cell_y, cell_z = leaf_lanes()
    cells_ref[35:36, :] = (base_x + cell_x).astype(f32) + 0.5
    cells_ref[36:37, :] = (base_y + cell_y).astype(f32) + 0.5
    cells_ref[37:38, :] = cell_z.astype(f32) + 0.5
    cells_ref[38:39, :] = counts_row[...].astype(f32)
    cells_ref[39:40, :] = jnp.zeros((1, LEAVES), f32)

    moments = {alpha: cells_ref[n : n + 1, :] for n, alpha in enumerate(ALPHAS)}
    moved = shift_moments(moments, parent_offsets())
    moved = jnp.concatenate(
        [moved[alpha] for alpha in ALPHAS] + [jnp.zeros((5, LEAVES), f32)], 0
    )
    parent_of = (iota((LEAVES, 128), 0) // CZ % CY // 2) * (CZ // 2) + iota(
        (LEAVES, 128), 0
    ) % CZ // 2
    belongs = jnp.where(parent_of == iota((LEAVES, 128), 1), 1.0, 0.0).astype(bf16)
    pcells = pick(moved, belongs)
    plane = iota((40, 128), 1)
    prow = iota((40, 128), 0)
    pcells = jnp.where(prow == 35, (base_x + 1).astype(f32), pcells)
    pcells = jnp.where(
        prow == 36, (base_y + 2 * (plane // (CZ // 2))).astype(f32) + 1.0, pcells
    )
    pcells = jnp.where(prow == 37, (2 * (plane % (CZ // 2))).astype(f32) + 1.0, pcells)
    pcells_ref[...] = pcells

    lane128 = iota((1, 128), 1)
    for q in range(4):
        pay = pays[q]

        def copy_leaf(k, _, pay=pay, q=q):
            pay[k] = own_ref[send_ref[0, q * SLOTS + k]]
            return 0

        lax.fori_loop(0, SLOTS, copy_leaf, 0, unroll=8)
        ids = id_row(sent_leaves, sent_parents, q)
        leaf_hot = onehot_rows(LEAVES, jnp.where(lane128 < SLOTS, ids, -1))
        parent_hot = onehot_rows(128, jnp.where(lane128 >= SLOTS, ids, -1))
        block = pick(cells_ref[...], leaf_hot) + pick(pcells, parent_hot)
        put_block(pay, block)


def put_block(pay, block):
    for s in range(5):
        pay[SLOTS + s, :, 0:128] = block[4 * s : 4 * s + 4]
        pay[SLOTS + s, :, 128:256] = block[20 + 4 * s : 24 + 4 * s]


def get_block(tail):
    return jnp.concatenate(
        [tail(s)[:, 0:128] for s in range(5)] + [tail(s)[:, 128:256] for s in range(5)], 0
    )


VM = pl.BlockSpec(memory_space=pltpu.VMEM)
SM = pl.BlockSpec(memory_space=pltpu.SMEM)
HB = pl.BlockSpec(memory_space=pl.ANY)
HBM = pl.BlockSpec(memory_space=pltpu.MemorySpace.HBM)
PARAMS = dict(vmem_limit_bytes=48 * 1024 * 1024)


def shaped(*shape):
    return jax.ShapeDtypeStruct(shape, f32)


def front(at, counts, send_leaves, send_parents, positions, masses):
    return pl.pallas_call(
        front_kernel,
        name="front",
        out_shape=[
            shaped(LEAVES, 4, LEAF), shaped(40, LEAVES), shaped(40, 128),
        ] + [shaped(PAY, 4, LEAF)] * 4,
        in_specs=[SM, VM, VM, VM, HBM, HBM, HBM, HBM],
        out_specs=[VM] * 7,
        scratch_shapes=[
            pltpu.VMEM((LEAVES * 16, 128), f32),
            pltpu.VMEM((4, LEAF, LEAVES), f32),
            pltpu.VMEM((3, LEAVES * LEAF), f32),
            pltpu.VMEM((LEAVES * 2, 128), f32),
            pltpu.SMEM((LEAVES,), jnp.int32),
            pltpu.SMEM((1, 4 * SLOTS), jnp.int32),
            pltpu.SemaphoreType.DMA((4,)),
        ],
        compiler_params=pltpu.CompilerParams(**PARAMS),
    )(
        at, counts.reshape(1, LEAVES), send_leaves, send_parents, counts, send_leaves, positions,
        masses.reshape(-1, 128),
    )


def slab8(slab):
    return jnp.concatenate([slab, jnp.zeros((4, LEAF), f32)], 0)


def b_form(points):
    row = iota(points.shape, 0)
    square = jnp.sum(jnp.where(row == 0, 0.0, points * points), 0, keepdims=True)
    return jnp.where(row == 4, square, points)


def a_form(points):
    row = iota(points.shape, 0)
    square = jnp.sum(jnp.where(row == 0, 0.0, points * points), 0, keepdims=True)
    value = jnp.where(row == 0, square + SOFT, -2.0 * points)
    return jnp.where(row == 4, 1.0, value)


def widen(value):
    one = value.astype(bf16).astype(f32)
    rest = value - one
    two = rest.astype(bf16).astype(f32)
    return one, two, rest - two


def squares(a_points, b_points):
    a1, a2, a3 = widen(a_form(a_points))
    b1, b2, b3 = widen(b_form(b_points))
    left = jnp.concatenate([a1, a1, a2, a2, a1, a3], 0).astype(bf16)
    right = jnp.concatenate([b1, b2, b1, b2, b3, b1], 0).astype(bf16)
    return dot_tn(left, right)


def sources(points, weight):
    parts = widen(b_form(points) * weight)
    return jnp.concatenate(parts + (jnp.zeros_like(parts[0]),), 0).astype(bf16)


def fold(out):
    total = out[0:8]
    for first in range(8, out.shape[0] // 8 * 8, 8):
        total = total + out[first : first + 8]
    return total


def finish(total, points):
    row = iota(points.shape, 0)
    mass = total[0:1]
    pushed = points * mass
    terms = jnp.where(row == 0, SOFT * total, points * (pushed - 2.0 * total))
    terms = jnp.where(row == 4, total, terms)
    potential = jnp.sum(terms, 0, keepdims=True)
    return jnp.where(row == 0, -potential, total - pushed)[0:4]


def load_points(slab):
    wide = slab8(slab)
    row = iota((8, LEAF), 0)
    return jnp.where(row == 0, 1.0, wide), slab[0:1]


def self_kernel(own_ref, out_ref):
    apart = jnp.where(iota((LEAF, LEAF), 0) == iota((LEAF, LEAF), 1), 0.0, 1.0)

    def some_leaves(step, _):
        first = step * WIDTH
        loaded = [load_points(own_ref[first + k]) for k in range(WIDTH)]
        spaced = [squares(points, points) for points, _ in loaded]
        cubes = []
        for value in spaced:
            inverse = lax.rsqrt(value) * apart
            cubes.append(inverse * inverse * inverse)
        high = [cube.astype(bf16) for cube in cubes]
        for k, (points, weight) in enumerate(loaded):
            low = (cubes[k] - high[k].astype(f32)).astype(bf16)
            side = sources(points, weight)
            total = fold(dot_nn(side, high[k])) + fold(dot_nn(side[0:16], low))
            out_ref[first + k] = finish(total, points)
        return 0

    lax.fori_loop(0, own_ref.shape[0] // WIDTH, some_leaves, 0)


def self_part(own, first, count):
    block = 32
    return pl.pallas_call(
        self_kernel,
        name="self_part",
        grid=(count // block,),
        out_shape=shaped(count, 4, LEAF),
        in_specs=[pl.BlockSpec((block, 4, LEAF), lambda i: (i + first // block, 0, 0))],
        out_specs=pl.BlockSpec((block, 4, LEAF), lambda i: (i, 0, 0)),
        cost_estimate=pl.CostEstimate(
            flops=count * 40_000_000, bytes_accessed=count * 8192, transcendentals=0
        ),
        compiler_params=pltpu.CompilerParams(**PARAMS),
    )(own)


def near_kernel(
    list_ref, own_ref, in0, in1, in2, in3, backs_ref,
    out_ref, pay0, pay1, pay2, pay3, table, total, shifts, sem, *held,
):
    pays = (pay0, pay1, pay2, pay3)
    copies = [pltpu.make_async_copy(own_ref, table.at[pl.ds(0, LEAVES)], sem.at[0])]
    for q, part in enumerate((in0, in1, in2, in3)):
        copies.append(
            pltpu.make_async_copy(
                part.at[pl.ds(0, SLOTS)],
                table.at[pl.ds(LEAVES + q * SLOTS, SLOTS)],
                sem.at[1 + q],
            )
        )
    for copy in copies:
        copy.start()

    def clear(c, _):
        total[c] = jnp.zeros((8, LEAF), f32)
        return 0

    lax.fori_loop(0, 2 * LEAVES + 8, clear, 0, unroll=8)
    row = iota((8, 128), 0)
    for code in range(27):
        step = (code % 3 - 1, code // 3 % 3 - 1, code // 9 - 1)
        value = jnp.zeros((8, 128), f32)
        for k in range(3):
            value = jnp.where(row == k + 1, float(step[k]), value)
        shifts[code] = value
    for copy in copies:
        copy.wait()

    def decode(group, k):
        code = list_ref[0, group * WIDTH + k]
        value = jnp.maximum(code - 1, 0)
        return value & 511, (value >> 9) & 511, value >> 18, code > 0

    def shift_of(code):
        half = shifts[code]
        return jnp.concatenate([half, half], 1)

    def spaced(group, k, rows):
        r, c, code, _ = decode(group, k)
        points_r, _ = load_points(table[r])
        points_c, _ = load_points(table[c])
        return squares((points_r + shift_of(code))[:, :rows], points_c)

    def keep(k, rows, value):
        inverse = lax.rsqrt(value)
        held[k][0:rows, :] = (inverse * inverse * inverse).astype(bf16)

    def products(group, k, rows):
        r, c, code, live = decode(group, k)
        points_r, weight_r = load_points(table[r])
        points_c, weight_c = load_points(table[c])
        shift = shift_of(code)
        cube = held[k][0:rows, :]
        side_r = sources((points_r + shift)[:, :rows], weight_r[:, :rows])
        to_c = fold(dot_nn(side_r, cube))
        to_r = fold(dot_nt(sources(points_c - shift, weight_c), cube))
        return jnp.where(live, r, 2 * LEAVES), jnp.where(live, c, 2 * LEAVES), to_r, to_c

    def settle(done, rows):
        for r, c, to_r, to_c in done:
            total[r, :, 0:rows] = total[r, :, 0:rows] + to_r
            total[c] = total[c] + to_c

    for n, rows in enumerate(CLASSES):
        first = list_ref[1, n]
        end = list_ref[1, n + 1]

        @pl.when(end > first)
        def _(first=first, end=end, rows=rows):
            for k in range(WIDTH):
                keep(k, rows, spaced(first, k, rows))

            def advance(group, _):
                done = []
                for k in range(WIDTH):
                    done.append(products(group, k, rows))
                    keep(k, rows, spaced(group + 1, k, rows))
                settle(done, rows)
                return 0

            lax.fori_loop(first, end - 1, advance, 0)
            settle([products(end - 1, k, rows) for k in range(WIDTH)], rows)

    def finish_own(c, _):
        points, _ = load_points(table[c])
        out_ref[c] = finish(total[c], points)
        return 0

    lax.fori_loop(0, LEAVES, finish_own, 0, unroll=8)
    for q in range(4):

        def finish_other(k, _, q=q):
            points, _ = load_points(table[LEAVES + q * SLOTS + k])
            pays[q][k] = finish(total[LEAVES + q * SLOTS + k], points)
            return 0

        lax.fori_loop(0, SLOTS, finish_other, 0, unroll=8)
        put_block(pays[q], backs_ref[q])


def near_part(ordered, own, incoming, backs):
    return pl.pallas_call(
        near_kernel,
        name="near_part",
        out_shape=[shaped(LEAVES, 4, LEAF)] + [shaped(PAY, 4, LEAF)] * 4,
        in_specs=[SM, HB, HB, HB, HB, HB, VM],
        out_specs=[VM] * 5,
        scratch_shapes=[
            pltpu.VMEM((2 * LEAVES, 4, LEAF), f32),
            pltpu.VMEM((2 * LEAVES + 8, 8, LEAF), f32),
            pltpu.VMEM((27, 8, 128), f32),
            pltpu.SemaphoreType.DMA((5,)),
        ] + [pltpu.VMEM((LEAF, LEAF), bf16)] * WIDTH,
        cost_estimate=pl.CostEstimate(
            flops=NEAR * 80_000_000, bytes_accessed=4_000_000, transcendentals=0
        ),
        compiler_params=pltpu.CompilerParams(**PARAMS),
    )(ordered, own, *incoming, backs)


def sort_lists(code, group, out_ref):
    count = code.shape[1]
    hot = jnp.where(iota((8, count), 0) == group, 1.0, 0.0)
    earlier = jnp.where(iota((count, count), 0) < iota((count, count), 1), 1.0, 0.0).astype(bf16)
    before = dot_nn(hot.astype(bf16), earlier)
    members = jnp.sum(hot, 1, keepdims=True)
    lane = iota((1, SORTED), 1)
    place = jnp.zeros((1, count), f32)
    groups = jnp.zeros((1, 1), f32)
    ends = jnp.zeros((1, SORTED), f32)
    for n in range(len(CLASSES)):
        place = place + hot[n : n + 1] * (before[n : n + 1] + groups * WIDTH)
        groups = groups + jnp.floor((members[n : n + 1] + (WIDTH - 1)) * (1.0 / WIDTH))
        ends = jnp.where(lane == n + 1, groups, ends)
    place = jnp.where(group >= 0, place, -1.0).astype(jnp.int32)
    ordered = pick(jnp.broadcast_to(code, (8, count)), onehot_rows(SORTED, place), True)
    out_ref[0:1, :] = ordered[0:1].astype(jnp.int32)
    out_ref[1:2, :] = ends.astype(jnp.int32)


def derivatives(x, y, z):
    square = x * x + y * y + z * z
    inverse = 1.0 / jnp.sqrt(square)
    inverse2 = inverse * inverse
    table = {(0, (0, 0, 0)): inverse}
    for m in range(1, 5):
        table[(m, (0, 0, 0))] = table[(m - 1, (0, 0, 0))] * inverse2 * float(-(2 * m - 1))
    place = (x, y, z)

    def entry(m, alpha):
        key = (m, alpha)
        if key not in table:
            axis = [k for k in range(3) if alpha[k]][0]
            lower = tuple(alpha[k] - (k == axis) for k in range(3))
            value = place[axis] * entry(m + 1, lower)
            if lower[axis]:
                lowest = tuple(lower[k] - (k == axis) for k in range(3))
                value = value + float(lower[axis]) * entry(m + 1, lowest)
            table[key] = value
        return table[key]

    return {alpha: entry(0, alpha) for alpha in ALPHAS}


def mutual(a_ref, b_ref, to_a, to_b):
    def rows(n):
        return pl.ds(n * 8, 8)

    lift = a_ref[rows(38), :]
    live = a_ref[rows(39), :] > 0.5
    gap = [
        jnp.where(live, a_ref[rows(35 + k), :] - b_ref[rows(35 + k), :] - (lift if k == 2 else 0.0), 3.0)
        for k in range(3)
    ]
    made = derivatives(*gap)
    for beta in ALPHAS:
        sum_a = None
        sum_b = None
        for alpha in ALPHAS:
            if sum(alpha) + sum(beta) > 4:
                continue
            tensor = made[add(alpha, beta)]
            scale = 1.0 / afact(alpha)
            sign_a = -((-1.0) ** sum(alpha)) * scale
            sign_b = -((-1.0) ** sum(beta)) * scale
            term_a = b_ref[rows(AT[alpha]), :] * sign_a * tensor
            term_b = a_ref[rows(AT[alpha]), :] * sign_b * tensor
            sum_a = term_a if sum_a is None else sum_a + term_a
            sum_b = term_b if sum_b is None else sum_b + term_b
        to_a[rows(AT[beta]), :] = jnp.where(live, sum_a, 0.0)
        to_b[rows(AT[beta]), :] = jnp.where(live, sum_b, 0.0)


def far_kernel(
    image_ref, far_ref, parent_ref, near_ref, cells_ref, pcells_ref, in0, in1, in2, in3,
    leaf_ref, par_ref, backs_ref, ordered_ref, tails, table, left, right, to_a, to_b, total, sem,
):
    copies = []
    for q, part in enumerate((in0, in1, in2, in3)):
        copies.append(
            pltpu.make_async_copy(part.at[pl.ds(SLOTS, 5)], tails.at[q], sem.at[q])
        )
    for copy in copies:
        copy.start()
    table[:, 0:LEAVES] = cells_ref[...]
    table[:, LEAVES + 512 :] = pcells_ref[...]
    row = iota((40, 128), 0)
    to_a[...] = jnp.zeros_like(to_a)
    to_b[...] = jnp.zeros_like(to_b)
    left[...] = jnp.zeros_like(left)
    right[...] = jnp.zeros_like(right)
    for copy in copies:
        copy.wait()
    for q in range(4):
        block = get_block(lambda s, q=q: tails[q, s])
        block = block + jnp.where(
            row == 35, image_ref[q, 0], jnp.where(row == 36, image_ref[q, 1], 0.0)
        )
        table[:, LEAVES + q * 128 : LEAVES + q * 128 + 128] = block
    parts = jnp.concatenate([part.astype(f32) for part in split3(table[...])], 0).astype(bf16)
    total[...] = jnp.zeros_like(total)

    def gathered(hot, first, count):
        out = dot_nn(parts[:, first : first + count], hot)
        return out[0:40] + out[40:80] + out[80:120]

    def leaf_entry(ids):
        other = ids - LEAVES
        return jnp.where(ids < LEAVES, ids, LEAVES + other // SLOTS * 128 + other % SLOTS)

    def parent_entry(ids):
        other = ids - PARENTS
        return jnp.where(
            ids < PARENTS, LEAVES + 512 + ids, LEAVES + other // PSLOTS * 128 + SLOTS + other % PSLOTS
        )

    def hots(ids_a, ids_b, parents):
        if parents:
            return (
                onehot_rows(128, ids_a), LEAVES + 512, 128,
                onehot_rows(640, parent_entry(ids_b) - LEAVES), LEAVES, 640,
            )
        return (
            onehot_rows(LEAVES, ids_a), 0, LEAVES,
            onehot_rows(768, leaf_entry(ids_b)), 0, 768,
        )

    def load(ids_a, ids_b, lifts, g, parents):
        hot_a, first_a, count_a, hot_b, first_b, count_b = hots(ids_a, ids_b, parents)
        from_a = gathered(hot_a, first_a, count_a)
        from_b = gathered(hot_b, first_b, count_b)
        live = jnp.where(ids_b >= 0, 1.0, 0.0)
        from_a = jnp.where(row == 38, lifts.astype(f32) * float(CZ), from_a)
        from_a = jnp.where(row == 39, live, from_a)
        left[pl.ds(g, 40, stride=8), :] = from_a
        right[pl.ds(g, 40, stride=8), :] = from_b

    def store(ids_a, ids_b, g, parents):
        hot_a, first_a, count_a, hot_b, first_b, count_b = hots(ids_a, ids_b, parents)
        sum_a = pick(to_a[pl.ds(g, 40, stride=8), :], hot_a, True)
        sum_b = pick(to_b[pl.ds(g, 40, stride=8), :], hot_b, True)
        total[:, first_a : first_a + count_a] += sum_a
        total[:, first_b : first_b + count_b] += sum_b

    for g in range(FAR // 128):
        lanes = slice(g * 128, g * 128 + 128)
        load(far_ref[0, :, lanes], far_ref[1, :, lanes], far_ref[2, :, lanes], g, False)
    mutual(left, right, to_a, to_b)
    for g in range(FAR // 128):
        lanes = slice(g * 128, g * 128 + 128)
        store(far_ref[0, :, lanes], far_ref[1, :, lanes], g, False)
    ids_a, ids_b, lifts = [
        jnp.concatenate([parent_ref[k], jnp.full((1, 128 - PFAR), -(k == 1), jnp.int32)], 1)
        for k in range(3)
    ]
    load(ids_a, ids_b, lifts, 0, True)
    mutual(left, right, to_a, to_b)
    store(ids_a, ids_b, 0, True)

    ids_a, ids_b, lifts = near_ref[0], near_ref[1], near_ref[2]
    hot_a, _, _, hot_b, _, _ = hots(ids_a, ids_b, False)
    from_a = gathered(hot_a, 0, LEAVES)[35:39]
    from_b = gathered(hot_b, 0, 768)[35:39]
    count_a, count_b = from_a[3:4], from_b[3:4]
    fewer = jnp.minimum(count_a, count_b)
    swap = count_b < count_a
    group = jnp.where(fewer <= 128.0, 0, jnp.where(fewer <= 192.0, 1, 2))
    group = jnp.where(ids_b >= 0, group, -1)
    moved = jnp.zeros((1, NEAR), f32)
    for k in range(3):
        apart = from_a[k : k + 1] - from_b[k : k + 1]
        if k == 2:
            apart = apart - lifts.astype(f32) * float(CZ)
        apart = jnp.where(swap, -apart, apart)
        moved = moved + (apart + 1.0) * float(3**k)
    rows = jnp.where(swap, ids_b, ids_a)
    columns = jnp.where(swap, ids_a, ids_b)
    code = 1.0 + rows.astype(f32) + columns.astype(f32) * 512.0 + moved * 262144.0
    sort_lists(jnp.where(ids_b >= 0, code, 0.0), group, ordered_ref)

    leaf_ref[...] = total[:, 0:LEAVES]
    par_ref[...] = total[:, LEAVES + 512 :]
    for q in range(4):
        backs_ref[q] = total[:, LEAVES + q * 128 : LEAVES + q * 128 + 128]


def far_part(image, far, parent, near, cells, pcells, incoming):
    return pl.pallas_call(
        far_kernel,
        name="far_part",
        out_shape=[
            shaped(40, LEAVES), shaped(40, 128), shaped(4, 40, 128),
            jax.ShapeDtypeStruct((2, SORTED), jnp.int32),
        ],
        in_specs=[SM, VM, VM, VM, VM, VM, HB, HB, HB, HB],
        out_specs=[VM] * 4,
        scratch_shapes=[
            pltpu.VMEM((4, 5, 4, LEAF), f32),
            pltpu.VMEM((40, TABLE), f32),
        ] + [pltpu.VMEM((320, 128), f32)] * 4 + [
            pltpu.VMEM((40, TABLE), f32),
            pltpu.SemaphoreType.DMA((4,)),
        ],
        compiler_params=pltpu.CompilerParams(**PARAMS),
    )(
        image, far.transpose(1, 0, 2), parent.transpose(1, 0, 2), near.transpose(1, 0, 2),
        cells, pcells, *incoming,
    )


def shift_terms(terms, offsets):
    for axis in range(3):
        powers = [None, offsets[axis]]
        for _ in range(3):
            powers.append(powers[-1] * offsets[axis])
        moved = {}
        for alpha in ALPHAS:
            total = terms[alpha]
            for k in range(1, 5 - sum(alpha)):
                upper = tuple(alpha[q] + k * (q == axis) for q in range(3))
                total = total + terms[upper] * powers[k] * (1.0 / FACT[k])
            moved[alpha] = total
        terms = moved
    return terms


def horner(get, degree, x, y, z):
    over_x = None
    for i in range(degree, -1, -1):
        over_y = None
        for j in range(degree - i, -1, -1):
            over_z = None
            for k in range(degree - i - j, -1, -1):
                value = get((i, j, k))
                over_z = value if over_z is None else over_z * z + value
            over_y = over_z if over_y is None else over_y * y + over_z
        over_x = over_y if over_x is None else over_x * x + over_y
    return over_x


def last_kernel(
    counts_ref, send_ref, sent_leaves, sent_parents, own_ref, near_ref, self0_ref, self1_ref, leaf_ref, par_ref,
    in0, in1, in2, in3, out_ref, slab_ref, turned_ref, terms_ref, field_ref, near_sum,
):
    incoming = (in0, in1, in2, in3)
    lane128 = iota((1, 128), 1)

    def copy_leaf(c, _):
        put_slab(slab_ref, c, own_ref[c])
        return 0

    lax.fori_loop(0, LEAVES, copy_leaf, 0, unroll=8)

    def both(c, _):
        near_sum[c] = near_ref[c] + self0_ref[c]
        near_sum[c + LEAVES // 2] = near_ref[c + LEAVES // 2] + self1_ref[c]
        return 0

    lax.fori_loop(0, LEAVES // 2, both, 0, unroll=8)

    leaf = leaf_ref[...]
    par = par_ref[...]
    for q in range(4):
        block = get_block(lambda s, q=q: incoming[q][SLOTS + s])
        ids = id_row(sent_leaves, sent_parents, q)
        leaf_hot = onehot_rows(LEAVES, jnp.where(lane128 < SLOTS, ids, -1))
        parent_hot = onehot_rows(128, jnp.where(lane128 >= SLOTS, ids, -1))
        leaf = leaf + pick(block, leaf_hot, True)
        par = par + pick(block, parent_hot, True)

        def arrive(k, _, q=q):
            c = send_ref[0, q * SLOTS + k]
            near_sum[c] = near_sum[c] + incoming[q][k]
            return 0

        lax.fori_loop(0, SLOTS, arrive, 0, unroll=4)
    lane_parent = (iota((128, LEAVES), 1) // CZ % CY // 2) * (CZ // 2) + iota(
        (128, LEAVES), 1
    ) % CZ // 2
    above = pick(par, jnp.where(lane_parent == iota((128, LEAVES), 0), 1.0, 0.0).astype(bf16))
    terms = {alpha: above[n : n + 1, :] for n, alpha in enumerate(ALPHAS)}
    terms = shift_terms(terms, parent_offsets())
    for n, alpha in enumerate(ALPHAS):
        terms_ref[n : n + 1, :] = leaf[n : n + 1, :] + terms[alpha]

    for comp in range(1, 4):
        turned_ref[comp] = get_rows(slab_ref, comp).T

    for half in range(2):
        lanes = slice(half * 128, half * 128 + 128)

        def term(alpha):
            return terms_ref[AT[alpha] : AT[alpha] + 1, lanes]

        def potential_at(alpha):
            return term(alpha) * (1.0 / afact(alpha))

        coefs = [{alpha: potential_at(alpha) for alpha in ALPHAS}]
        for axis in range(3):
            coefs.append(
                {
                    alpha: term(add(alpha, unit(axis))) * (-1.0 / afact(alpha))
                    for alpha in ALPHAS
                    if sum(alpha) <= 3
                }
            )

        def chunk(step, _):
            rows = pl.ds(pl.multiple_of(step * 32, 32), 32)
            x, y, z = [turned_ref[comp, rows, lanes] for comp in range(1, 4)]
            for comp in range(4):
                field_ref[comp, rows, lanes] = horner(
                    lambda alpha, comp=comp: coefs[comp][alpha], 3 if comp else 4, x, y, z
                )
            return 0

        lax.fori_loop(0, LEAF // 32, chunk, 0)

    for comp in range(4):
        turned = field_ref[comp].T
        for half in range(2):
            slab_ref[pl.ds(half * LEAVES * 8 + comp, LEAVES, stride=8), :] = turned[
                :, half * 128 : half * 128 + 128
            ]

    lane = iota((4, LEAF), 1)

    def write(c, _):
        value = jnp.concatenate(
            [
                slab_ref[pl.ds(pl.multiple_of(half * LEAVES * 8 + c * 8, 8), 8), :]
                for half in range(2)
            ],
            1,
        )[0:4] + near_sum[c]
        start = pl.multiple_of(c * LEAF, LEAF)
        out_ref[:, pl.ds(start, LEAF)] = jnp.where(lane < counts_ref[c], value, 0.0)
        return 0

    lax.fori_loop(0, LEAVES, write, 0, unroll=8)


def last(counts, send_leaves, send_parents, own, near, self0, self1, leaf, par, arrived):
    return pl.pallas_call(
        last_kernel,
        name="last",
        out_shape=shaped(4, LEAVES * LEAF),
        in_specs=[SM, SM] + [VM] * 12,
        out_specs=VM,
        scratch_shapes=[
            pltpu.VMEM((LEAVES * 16, 128), f32),
            pltpu.VMEM((4, LEAF, LEAVES), f32),
            pltpu.VMEM((40, LEAVES), f32),
            pltpu.VMEM((4, LEAF, LEAVES), f32),
            pltpu.VMEM((LEAVES, 4, LEAF), f32),
        ],
        compiler_params=pltpu.CompilerParams(**PARAMS),
    )(
        counts, send_leaves, send_leaves, send_parents, own, near, self0, self1, leaf, par, *arrived
    )


def image_shift(slab_at, sub_at, slab_count, sub_count):
    rows_out = []
    for direction in range(4):
        reach_x = slab_at + slab_steps[direction]
        reach_y = sub_at + sub_steps[direction]
        jump_x = (reach_x - reach_x % slab_count) * CX
        jump_y = (reach_y - reach_y % sub_count) * CY
        rows_out.append(jnp.stack([jump_x, jump_y]))
    return jnp.stack(rows_out).astype(f32)


def moved_by(value, slab_step, sub_step, slab_count, sub_count):
    pairs = []
    for slab_at in range(slab_count):
        for sub_at in range(sub_count):
            target = (slab_at + slab_step) % slab_count * sub_count + (sub_at + sub_step) % sub_count
            pairs.append((slab_at * sub_count + sub_at, target))
    return lax.ppermute(value, ("slab", "sub"), pairs)


def on_device(
    positions, masses, leaf_counts, send_leaves, send_parents, near_pairs, far_pairs, parent_pairs
):
    slab_count = lax.axis_size("slab")
    sub_count = lax.axis_size("sub")
    slab_at = lax.axis_index("slab")
    sub_at = lax.axis_index("sub")
    at = jnp.stack([slab_at, sub_at]).astype(jnp.int32)
    own, cells, pcells, *outgoing = front(
        at, leaf_counts, send_leaves, send_parents, positions, masses
    )
    incoming = [
        moved_by(outgoing[q], -slab_steps[q], -sub_steps[q], slab_count, sub_count)
        for q in range(4)
    ]
    image = image_shift(slab_at, sub_at, slab_count, sub_count)
    self0 = self_part(own, 0, LEAVES // 2)
    leaf, par, backs, ordered = far_part(
        image, far_pairs, parent_pairs, near_pairs, cells, pcells, incoming
    )
    near, *returning = near_part(ordered, own, incoming, backs)
    arrived = [
        moved_by(returning[q], slab_steps[q], sub_steps[q], slab_count, sub_count)
        for q in range(4)
    ]
    self1 = self_part(own, LEAVES // 2, LEAVES // 2)
    return last(leaf_counts, send_leaves, send_parents, own, near, self0, self1, leaf, par, arrived)


def solution(mesh):
    return jax.shard_map(
        on_device,
        mesh=mesh,
        in_specs=(
            P(None, ("slab", "sub")),
            P(("slab", "sub")),
            P(("slab", "sub")),
            P(("slab", "sub"), None),
            P(("slab", "sub"), None),
            P(("slab", "sub"), None, None),
            P(("slab", "sub"), None, None),
            P(("slab", "sub"), None, None),
        ),
        out_specs=P(None, ("slab", "sub")),
        check_vma=False,
    )
```

```python
import jax
import jax.numpy as jnp
from jax import lax
from jax.experimental import pallas as pl
from jax.experimental.pallas import tpu as pltpu
from jax.sharding import PartitionSpec as P

CX = 2
CY = 4
CZ = 32
LEAVES = 256
LEAF = 256
PARENTS = 32
SLOTS = 64
PSLOTS = 16
NEAR = 256
FAR = 1024
PFAR = 64
PAY = SLOTS + 5
SOFT = 0.0025
WIDTH = 8
CLASSES = (128, 192, 256)
SORTED = 384
slab_steps = (1, 0, 1, 1)
sub_steps = (0, 1, 1, -1)
f32 = jnp.float32
bf16 = jnp.bfloat16

ALPHAS = [
    (i, j, d - i - j) for d in range(5) for i in range(d, -1, -1) for j in range(d - i, -1, -1)
]
AT = {a: n for n, a in enumerate(ALPHAS)}
FACT = (1.0, 1.0, 2.0, 6.0, 24.0)
TABLE = LEAVES + 4 * 128 + 128


def afact(alpha):
    return FACT[alpha[0]] * FACT[alpha[1]] * FACT[alpha[2]]


def add(a, b):
    return (a[0] + b[0], a[1] + b[1], a[2] + b[2])


def unit(axis):
    return tuple(1 if k == axis else 0 for k in range(3))


def split3(value):
    one = value.astype(bf16)
    rest = value - one.astype(f32)
    two = rest.astype(bf16)
    three = (rest - two.astype(f32)).astype(bf16)
    return one, two, three


def dot_nn(a, b):
    return lax.dot_general(a, b, (((1,), (0,)), ((), ())), preferred_element_type=f32)


def dot_nt(a, b):
    return lax.dot_general(a, b, (((1,), (1,)), ((), ())), preferred_element_type=f32)


def dot_tn(a, b):
    return lax.dot_general(a, b, (((0,), (0,)), ((), ())), preferred_element_type=f32)


def pick(values, onehot, transposed=False):
    parts = jnp.concatenate([part.astype(f32) for part in split3(values)], 0).astype(bf16)
    out = dot_nt(parts, onehot) if transposed else dot_nn(parts, onehot)
    rows = values.shape[0]
    return out[:rows] + out[rows : 2 * rows] + out[2 * rows :]


def iota(shape, dim):
    return lax.broadcasted_iota(jnp.int32, shape, dim)


def onehot_rows(count, ids):
    hit = iota((count, ids.shape[1]), 0) == ids
    return jnp.where(hit, 1.0, 0.0).astype(bf16)


def fetch_all(moves, sem):
    copies = [
        pltpu.make_async_copy(source, target, sem.at[n])
        for n, (source, target) in enumerate(moves)
    ]
    for copy in copies:
        copy.start()
    for copy in copies:
        copy.wait()


def id_row(sent_leaves, sent_parents, q):
    return jnp.concatenate(
        [
            sent_leaves[:, q * SLOTS : (q + 1) * SLOTS],
            sent_parents[:, q * PSLOTS : (q + 1) * PSLOTS],
            jnp.full((1, 128 - SLOTS - PSLOTS), -1, jnp.int32),
        ],
        1,
    )


def put_slab(slab_ref, c, slab):
    wide = jnp.concatenate([slab, jnp.zeros((4, LEAF), f32)], 0)
    for half in range(2):
        rows = pl.ds(pl.multiple_of(half * LEAVES * 8 + c * 8, 8), 8)
        slab_ref[rows, :] = wide[:, half * 128 : half * 128 + 128]


def get_rows(slab_ref, comp):
    return jnp.concatenate(
        [slab_ref[pl.ds(half * LEAVES * 8 + comp, LEAVES, stride=8), :] for half in range(2)], 1
    )


def monomials(x, y, z, w):
    made = {(0, 0, 0): w}
    for alpha in ALPHAS[1:]:
        for axis, value in ((2, z), (1, y), (0, x)):
            if alpha[axis]:
                lower = tuple(alpha[k] - (k == axis) for k in range(3))
                made[alpha] = made[lower] * value
                break
    return made


def shift_moments(moments, offsets):
    choose = ((1,), (1, 1), (1, 2, 1), (1, 3, 3, 1), (1, 4, 6, 4, 1))
    for axis in range(3):
        powers = [None, offsets[axis]]
        for _ in range(3):
            powers.append(powers[-1] * offsets[axis])
        moved = {}
        for alpha in ALPHAS:
            total = moments[alpha]
            for k in range(alpha[axis]):
                lower = tuple(k if q == axis else alpha[q] for q in range(3))
                total = total + moments[lower] * powers[alpha[axis] - k] * float(
                    choose[alpha[axis]][k]
                )
            moved[alpha] = total
        moments = moved
    return moments


def leaf_lanes():
    lane = iota((1, LEAVES), 1)
    return lane // (CY * CZ), lane // CZ % CY, lane % CZ


def parent_offsets():
    cell_x, cell_y, cell_z = leaf_lanes()
    return [(cell % 2).astype(f32) - 0.5 for cell in (cell_x, cell_y, cell_z)]


def front_kernel(
    at_ref, counts_row, sent_leaves, sent_parents, counts_hbm, send_hbm, pos_hbm, mass_hbm,
    own_ref, cells_ref, pcells_ref, pay0, pay1, pay2, pay3, turned_ref,
    slab_ref, pos_ref, mass_ref, counts_ref, send_ref, sem,
):
    pays = (pay0, pay1, pay2, pay3)
    fetch_all(
        ((counts_hbm, counts_ref), (send_hbm, send_ref), (pos_hbm, pos_ref), (mass_hbm, mass_ref)),
        sem,
    )
    base_x = at_ref[0] * CX
    base_y = at_ref[1] * CY
    row4 = iota((4, LEAF), 0)
    lane = iota((1, LEAF), 1)
    batch = 8

    for x in range(CX):
        for y in range(CY):
            centre = jnp.where(row4 == 1, (base_x + x).astype(f32) + 0.5, 0.0)
            centre = jnp.where(row4 == 2, (base_y + y).astype(f32) + 0.5, centre)

            def some_leaves(step, _, x=x, y=y, centre=centre):
                low = step * batch
                first = (x * CY + y) * CZ + low
                from_z = jnp.where(row4 == 3, low.astype(f32) + 0.5, centre)
                for k in range(batch):
                    c = first + k
                    start = pl.multiple_of(c * LEAF, LEAF)
                    place = pos_ref[:, pl.ds(start, LEAF)]
                    mass = jnp.concatenate(
                        [mass_ref[pl.ds(2 * c, 1), :], mass_ref[pl.ds(2 * c + 1, 1), :]], 1
                    )
                    weight = jnp.where(lane < counts_ref[c], mass, 0.0)
                    slab = jnp.concatenate([weight, place], 0) - (
                        from_z + jnp.where(row4 == 3, float(k), 0.0)
                    )
                    own_ref[c] = slab
                    put_slab(slab_ref, c, slab)
                return 0

            lax.fori_loop(0, CZ // batch, some_leaves, 0)

    for comp in range(4):
        turned_ref[comp] = get_rows(slab_ref, comp).T

    for half in range(2):
        lanes = slice(half * 128, half * 128 + 128)

        def chunk(step, totals):
            rows = pl.ds(pl.multiple_of(step * 8, 8), 8)
            w, x, y, z = [turned_ref[comp, rows, lanes] for comp in range(4)]
            made = monomials(x, y, z, w)
            return tuple(total + made[alpha] for total, alpha in zip(totals, ALPHAS))

        totals = lax.fori_loop(
            0, LEAF // 8, chunk, tuple(jnp.zeros((8, 128), f32) for _ in ALPHAS)
        )
        for n, total in enumerate(totals):
            cells_ref[n : n + 1, lanes] = jnp.sum(total, 0, keepdims=True)

    cell_x, cell_y, cell_z = leaf_lanes()
    cells_ref[35:36, :] = (base_x + cell_x).astype(f32) + 0.5
    cells_ref[36:37, :] = (base_y + cell_y).astype(f32) + 0.5
    cells_ref[37:38, :] = cell_z.astype(f32) + 0.5
    cells_ref[38:39, :] = counts_row[...].astype(f32)
    cells_ref[39:40, :] = jnp.zeros((1, LEAVES), f32)

    moments = {alpha: cells_ref[n : n + 1, :] for n, alpha in enumerate(ALPHAS)}
    moved = shift_moments(moments, parent_offsets())
    moved = jnp.concatenate(
        [moved[alpha] for alpha in ALPHAS] + [jnp.zeros((5, LEAVES), f32)], 0
    )
    parent_of = (iota((LEAVES, 128), 0) // CZ % CY // 2) * (CZ // 2) + iota(
        (LEAVES, 128), 0
    ) % CZ // 2
    belongs = jnp.where(parent_of == iota((LEAVES, 128), 1), 1.0, 0.0).astype(bf16)
    pcells = pick(moved, belongs)
    plane = iota((40, 128), 1)
    prow = iota((40, 128), 0)
    pcells = jnp.where(prow == 35, (base_x + 1).astype(f32), pcells)
    pcells = jnp.where(
        prow == 36, (base_y + 2 * (plane // (CZ // 2))).astype(f32) + 1.0, pcells
    )
    pcells = jnp.where(prow == 37, (2 * (plane % (CZ // 2))).astype(f32) + 1.0, pcells)
    pcells_ref[...] = pcells

    lane128 = iota((1, 128), 1)
    for q in range(4):
        pay = pays[q]

        def copy_leaf(k, _, pay=pay, q=q):
            pay[k] = own_ref[send_ref[0, q * SLOTS + k]]
            return 0

        lax.fori_loop(0, SLOTS, copy_leaf, 0, unroll=8)
        ids = id_row(sent_leaves, sent_parents, q)
        leaf_hot = onehot_rows(LEAVES, jnp.where(lane128 < SLOTS, ids, -1))
        parent_hot = onehot_rows(128, jnp.where(lane128 >= SLOTS, ids, -1))
        block = pick(cells_ref[...], leaf_hot) + pick(pcells, parent_hot)
        put_block(pay, block)


def put_block(pay, block):
    for s in range(5):
        pay[SLOTS + s, :, 0:128] = block[4 * s : 4 * s + 4]
        pay[SLOTS + s, :, 128:256] = block[20 + 4 * s : 24 + 4 * s]


def get_block(tail):
    return jnp.concatenate(
        [tail(s)[:, 0:128] for s in range(5)] + [tail(s)[:, 128:256] for s in range(5)], 0
    )


VM = pl.BlockSpec(memory_space=pltpu.VMEM)
SM = pl.BlockSpec(memory_space=pltpu.SMEM)
HB = pl.BlockSpec(memory_space=pl.ANY)
HBM = pl.BlockSpec(memory_space=pltpu.MemorySpace.HBM)
PARAMS = dict(vmem_limit_bytes=48 * 1024 * 1024)


def shaped(*shape):
    return jax.ShapeDtypeStruct(shape, f32)


def front(at, counts, send_leaves, send_parents, positions, masses):
    return pl.pallas_call(
        front_kernel,
        name="front",
        out_shape=[
            shaped(LEAVES, 4, LEAF), shaped(40, LEAVES), shaped(40, 128),
        ] + [shaped(PAY, 4, LEAF)] * 4 + [shaped(4, LEAF, LEAVES)],
        in_specs=[SM, VM, VM, VM, HBM, HBM, HBM, HBM],
        out_specs=[VM] * 8,
        scratch_shapes=[
            pltpu.VMEM((LEAVES * 16, 128), f32),
            pltpu.VMEM((3, LEAVES * LEAF), f32),
            pltpu.VMEM((LEAVES * 2, 128), f32),
            pltpu.SMEM((LEAVES,), jnp.int32),
            pltpu.SMEM((1, 4 * SLOTS), jnp.int32),
            pltpu.SemaphoreType.DMA((4,)),
        ],
        compiler_params=pltpu.CompilerParams(vmem_limit_bytes=63 * 1024 * 1024),
    )(
        at, counts.reshape(1, LEAVES), send_leaves, send_parents, counts, send_leaves, positions,
        masses.reshape(-1, 128),
    )


def slab8(slab):
    return jnp.concatenate([slab, jnp.zeros((4, LEAF), f32)], 0)


def b_form(points):
    row = iota(points.shape, 0)
    square = jnp.sum(jnp.where(row == 0, 0.0, points * points), 0, keepdims=True)
    return jnp.where(row == 4, square, points)


def a_form(points):
    row = iota(points.shape, 0)
    square = jnp.sum(jnp.where(row == 0, 0.0, points * points), 0, keepdims=True)
    value = jnp.where(row == 0, square + SOFT, -2.0 * points)
    return jnp.where(row == 4, 1.0, value)


def widen(value):
    one = value.astype(bf16).astype(f32)
    rest = value - one
    two = rest.astype(bf16).astype(f32)
    return one, two, rest - two


def squares(a_points, b_points):
    a1, a2, a3 = widen(a_form(a_points))
    b1, b2, b3 = widen(b_form(b_points))
    left = jnp.concatenate([a1, a1, a2, a2, a1, a3], 0).astype(bf16)
    right = jnp.concatenate([b1, b2, b1, b2, b3, b1], 0).astype(bf16)
    return dot_tn(left, right)


def sources(points, weight):
    parts = widen(b_form(points) * weight)
    return jnp.concatenate(parts + (jnp.zeros_like(parts[0]),), 0).astype(bf16)


def fold(out):
    total = out[0:8]
    for first in range(8, out.shape[0] // 8 * 8, 8):
        total = total + out[first : first + 8]
    return total


def finish(total, points):
    row = iota(points.shape, 0)
    mass = total[0:1]
    pushed = points * mass
    terms = jnp.where(row == 0, SOFT * total, points * (pushed - 2.0 * total))
    terms = jnp.where(row == 4, total, terms)
    potential = jnp.sum(terms, 0, keepdims=True)
    return jnp.where(row == 0, -potential, total - pushed)[0:4]


def load_points(slab):
    wide = slab8(slab)
    row = iota((8, LEAF), 0)
    return jnp.where(row == 0, 1.0, wide), slab[0:1]


def self_kernel(own_ref, *refs):
    out_ref = refs[-1]
    apart = jnp.where(iota((LEAF, LEAF), 0) == iota((LEAF, LEAF), 1), 0.0, 1.0)

    def some_leaves(step, _):
        first = step * WIDTH
        loaded = [load_points(own_ref[first + k]) for k in range(WIDTH)]
        spaced = [squares(points, points) for points, _ in loaded]
        cubes = []
        for value in spaced:
            inverse = lax.rsqrt(value) * apart
            cubes.append(inverse * inverse * inverse)
        high = [cube.astype(bf16) for cube in cubes]
        for k, (points, weight) in enumerate(loaded):
            low = (cubes[k] - high[k].astype(f32)).astype(bf16)
            side = sources(points, weight)
            total = fold(dot_nn(side, high[k])) + fold(dot_nn(side[0:16], low))
            value = finish(total, points)
            out_ref[first + k] = value + refs[0][first + k] if len(refs) > 1 else value
        return 0

    lax.fori_loop(0, own_ref.shape[0] // WIDTH, some_leaves, 0)


def self_part(own, first, count, others=()):
    block = 32
    spec = pl.BlockSpec((block, 4, LEAF), lambda i: (i + first // block, 0, 0))
    return pl.pallas_call(
        self_kernel,
        name="self_part",
        grid=(count // block,),
        out_shape=shaped(count, 4, LEAF),
        in_specs=[spec] * (1 + len(others)),
        out_specs=pl.BlockSpec((block, 4, LEAF), lambda i: (i, 0, 0)),
        cost_estimate=pl.CostEstimate(
            flops=count * 40_000_000, bytes_accessed=count * 8192, transcendentals=0
        ),
        compiler_params=pltpu.CompilerParams(**PARAMS),
    )(own, *others)


def near_kernel(
    list_ref, own_ref, in0, in1, in2, in3, backs_ref, self_ref,
    out_ref, pay0, pay1, pay2, pay3, table, total, shifts, sem, *held,
):
    pays = (pay0, pay1, pay2, pay3)
    copies = [pltpu.make_async_copy(own_ref, table.at[pl.ds(0, LEAVES)], sem.at[0])]
    for q, part in enumerate((in0, in1, in2, in3)):
        copies.append(
            pltpu.make_async_copy(
                part.at[pl.ds(0, SLOTS)],
                table.at[pl.ds(LEAVES + q * SLOTS, SLOTS)],
                sem.at[1 + q],
            )
        )
    for copy in copies:
        copy.start()

    def clear(c, _):
        total[c] = jnp.zeros((8, LEAF), f32)
        return 0

    lax.fori_loop(0, 2 * LEAVES + 8, clear, 0, unroll=8)
    row = iota((8, 128), 0)
    for code in range(27):
        step = (code % 3 - 1, code // 3 % 3 - 1, code // 9 - 1)
        value = jnp.zeros((8, 128), f32)
        for k in range(3):
            value = jnp.where(row == k + 1, float(step[k]), value)
        shifts[code] = value
    for copy in copies:
        copy.wait()

    def decode(group, k):
        code = list_ref[0, group * WIDTH + k]
        value = jnp.maximum(code - 1, 0)
        return value & 511, (value >> 9) & 511, value >> 18, code > 0

    def shift_of(code):
        half = shifts[code]
        return jnp.concatenate([half, half], 1)

    def spaced(group, k, rows):
        r, c, code, _ = decode(group, k)
        points_r, _ = load_points(table[r])
        points_c, _ = load_points(table[c])
        return squares((points_r + shift_of(code))[:, :rows], points_c)

    def keep(k, rows, value):
        inverse = lax.rsqrt(value)
        held[k][0:rows, :] = (inverse * inverse * inverse).astype(bf16)

    def products(group, k, rows):
        r, c, code, live = decode(group, k)
        points_r, weight_r = load_points(table[r])
        points_c, weight_c = load_points(table[c])
        shift = shift_of(code)
        cube = held[k][0:rows, :]
        side_r = sources((points_r + shift)[:, :rows], weight_r[:, :rows])
        to_c = fold(dot_nn(side_r, cube))
        to_r = fold(dot_nt(sources(points_c - shift, weight_c), cube))
        return jnp.where(live, r, 2 * LEAVES), jnp.where(live, c, 2 * LEAVES), to_r, to_c

    def settle(done, rows):
        for r, c, to_r, to_c in done:
            total[r, :, 0:rows] = total[r, :, 0:rows] + to_r
            total[c] = total[c] + to_c

    for n, rows in enumerate(CLASSES):
        first = list_ref[1, n]
        end = list_ref[1, n + 1]

        @pl.when(end > first)
        def _(first=first, end=end, rows=rows):
            for k in range(WIDTH):
                keep(k, rows, spaced(first, k, rows))

            def advance(group, _):
                done = []
                for k in range(WIDTH):
                    done.append(products(group, k, rows))
                    keep(k, rows, spaced(group + 1, k, rows))
                settle(done, rows)
                return 0

            lax.fori_loop(first, end - 1, advance, 0)
            settle([products(end - 1, k, rows) for k in range(WIDTH)], rows)

    def finish_own(c, _):
        points, _ = load_points(table[c])
        out_ref[c] = finish(total[c], points)
        return 0

    def finish_both(c, _):
        points, _ = load_points(table[c])
        out_ref[c] = finish(total[c], points) + self_ref[c]
        return 0

    lax.fori_loop(0, LEAVES // 2, finish_both, 0, unroll=8)
    lax.fori_loop(LEAVES // 2, LEAVES, finish_own, 0, unroll=8)
    for q in range(4):

        def finish_other(k, _, q=q):
            points, _ = load_points(table[LEAVES + q * SLOTS + k])
            pays[q][k] = finish(total[LEAVES + q * SLOTS + k], points)
            return 0

        lax.fori_loop(0, SLOTS, finish_other, 0, unroll=8)
        put_block(pays[q], backs_ref[q])


def near_part(ordered, own, incoming, backs, self0):
    return pl.pallas_call(
        near_kernel,
        name="near_part",
        out_shape=[shaped(LEAVES, 4, LEAF)] + [shaped(PAY, 4, LEAF)] * 4,
        in_specs=[SM, HB, HB, HB, HB, HB, VM, VM],
        out_specs=[VM] * 5,
        scratch_shapes=[
            pltpu.VMEM((2 * LEAVES, 4, LEAF), f32),
            pltpu.VMEM((2 * LEAVES + 8, 8, LEAF), f32),
            pltpu.VMEM((27, 8, 128), f32),
            pltpu.SemaphoreType.DMA((5,)),
        ] + [pltpu.VMEM((LEAF, LEAF), bf16)] * WIDTH,
        cost_estimate=pl.CostEstimate(
            flops=NEAR * 80_000_000, bytes_accessed=4_000_000, transcendentals=0
        ),
        compiler_params=pltpu.CompilerParams(**PARAMS),
    )(ordered, own, *incoming, backs, self0)


def sort_lists(code, group, out_ref):
    count = code.shape[1]
    hot = jnp.where(iota((8, count), 0) == group, 1.0, 0.0)
    earlier = jnp.where(iota((count, count), 0) < iota((count, count), 1), 1.0, 0.0).astype(bf16)
    before = dot_nn(hot.astype(bf16), earlier)
    members = jnp.sum(hot, 1, keepdims=True)
    lane = iota((1, SORTED), 1)
    place = jnp.zeros((1, count), f32)
    groups = jnp.zeros((1, 1), f32)
    ends = jnp.zeros((1, SORTED), f32)
    for n in range(len(CLASSES)):
        place = place + hot[n : n + 1] * (before[n : n + 1] + groups * WIDTH)
        groups = groups + jnp.floor((members[n : n + 1] + (WIDTH - 1)) * (1.0 / WIDTH))
        ends = jnp.where(lane == n + 1, groups, ends)
    place = jnp.where(group >= 0, place, -1.0).astype(jnp.int32)
    ordered = pick(jnp.broadcast_to(code, (8, count)), onehot_rows(SORTED, place), True)
    out_ref[0:1, :] = ordered[0:1].astype(jnp.int32)
    out_ref[1:2, :] = ends.astype(jnp.int32)


def derivatives(x, y, z):
    square = x * x + y * y + z * z
    inverse = 1.0 / jnp.sqrt(square)
    inverse2 = inverse * inverse
    table = {(0, (0, 0, 0)): inverse}
    for m in range(1, 5):
        table[(m, (0, 0, 0))] = table[(m - 1, (0, 0, 0))] * inverse2 * float(-(2 * m - 1))
    place = (x, y, z)

    def entry(m, alpha):
        key = (m, alpha)
        if key not in table:
            axis = [k for k in range(3) if alpha[k]][0]
            lower = tuple(alpha[k] - (k == axis) for k in range(3))
            value = place[axis] * entry(m + 1, lower)
            if lower[axis]:
                lowest = tuple(lower[k] - (k == axis) for k in range(3))
                value = value + float(lower[axis]) * entry(m + 1, lowest)
            table[key] = value
        return table[key]

    return {alpha: entry(0, alpha) for alpha in ALPHAS}


def mutual(a_ref, b_ref, to_a, to_b):
    def rows(n):
        return pl.ds(n * 8, 8)

    lift = a_ref[rows(38), :]
    live = a_ref[rows(39), :] > 0.5
    gap = [
        jnp.where(live, a_ref[rows(35 + k), :] - b_ref[rows(35 + k), :] - (lift if k == 2 else 0.0), 3.0)
        for k in range(3)
    ]
    made = derivatives(*gap)
    for beta in ALPHAS:
        sum_a = None
        sum_b = None
        for alpha in ALPHAS:
            if sum(alpha) + sum(beta) > 4:
                continue
            tensor = made[add(alpha, beta)]
            scale = 1.0 / afact(alpha)
            sign_a = -((-1.0) ** sum(alpha)) * scale
            sign_b = -((-1.0) ** sum(beta)) * scale
            term_a = b_ref[rows(AT[alpha]), :] * sign_a * tensor
            term_b = a_ref[rows(AT[alpha]), :] * sign_b * tensor
            sum_a = term_a if sum_a is None else sum_a + term_a
            sum_b = term_b if sum_b is None else sum_b + term_b
        to_a[rows(AT[beta]), :] = jnp.where(live, sum_a, 0.0)
        to_b[rows(AT[beta]), :] = jnp.where(live, sum_b, 0.0)


def far_kernel(
    image_ref, far_ref, parent_ref, near_ref, cells_ref, pcells_ref, in0, in1, in2, in3,
    leaf_ref, par_ref, backs_ref, ordered_ref, tails, table, left, right, to_a, to_b, total, sem,
):
    copies = []
    for q, part in enumerate((in0, in1, in2, in3)):
        copies.append(
            pltpu.make_async_copy(part.at[pl.ds(SLOTS, 5)], tails.at[q], sem.at[q])
        )
    for copy in copies:
        copy.start()
    table[:, 0:LEAVES] = cells_ref[...]
    table[:, LEAVES + 512 :] = pcells_ref[...]
    row = iota((40, 128), 0)
    to_a[...] = jnp.zeros_like(to_a)
    to_b[...] = jnp.zeros_like(to_b)
    left[...] = jnp.zeros_like(left)
    right[...] = jnp.zeros_like(right)
    for copy in copies:
        copy.wait()
    for q in range(4):
        block = get_block(lambda s, q=q: tails[q, s])
        block = block + jnp.where(
            row == 35, image_ref[q, 0], jnp.where(row == 36, image_ref[q, 1], 0.0)
        )
        table[:, LEAVES + q * 128 : LEAVES + q * 128 + 128] = block
    parts = jnp.concatenate([part.astype(f32) for part in split3(table[...])], 0).astype(bf16)
    total[...] = jnp.zeros_like(total)

    def gathered(hot, first, count):
        out = dot_nn(parts[:, first : first + count], hot)
        return out[0:40] + out[40:80] + out[80:120]

    def leaf_entry(ids):
        other = ids - LEAVES
        return jnp.where(ids < LEAVES, ids, LEAVES + other // SLOTS * 128 + other % SLOTS)

    def parent_entry(ids):
        other = ids - PARENTS
        return jnp.where(
            ids < PARENTS, LEAVES + 512 + ids, LEAVES + other // PSLOTS * 128 + SLOTS + other % PSLOTS
        )

    def hots(ids_a, ids_b, parents):
        if parents:
            return (
                onehot_rows(128, ids_a), LEAVES + 512, 128,
                onehot_rows(640, parent_entry(ids_b) - LEAVES), LEAVES, 640,
            )
        return (
            onehot_rows(LEAVES, ids_a), 0, LEAVES,
            onehot_rows(768, leaf_entry(ids_b)), 0, 768,
        )

    def load(ids_a, ids_b, lifts, g, parents):
        hot_a, first_a, count_a, hot_b, first_b, count_b = hots(ids_a, ids_b, parents)
        from_a = gathered(hot_a, first_a, count_a)
        from_b = gathered(hot_b, first_b, count_b)
        live = jnp.where(ids_b >= 0, 1.0, 0.0)
        from_a = jnp.where(row == 38, lifts.astype(f32) * float(CZ), from_a)
        from_a = jnp.where(row == 39, live, from_a)
        left[pl.ds(g, 40, stride=8), :] = from_a
        right[pl.ds(g, 40, stride=8), :] = from_b

    def store(ids_a, ids_b, g, parents):
        hot_a, first_a, count_a, hot_b, first_b, count_b = hots(ids_a, ids_b, parents)
        sum_a = pick(to_a[pl.ds(g, 40, stride=8), :], hot_a, True)
        sum_b = pick(to_b[pl.ds(g, 40, stride=8), :], hot_b, True)
        total[:, first_a : first_a + count_a] += sum_a
        total[:, first_b : first_b + count_b] += sum_b

    for g in range(FAR // 128):
        lanes = slice(g * 128, g * 128 + 128)
        load(far_ref[0, :, lanes], far_ref[1, :, lanes], far_ref[2, :, lanes], g, False)
    mutual(left, right, to_a, to_b)
    for g in range(FAR // 128):
        lanes = slice(g * 128, g * 128 + 128)
        store(far_ref[0, :, lanes], far_ref[1, :, lanes], g, False)
    ids_a, ids_b, lifts = [
        jnp.concatenate([parent_ref[k], jnp.full((1, 128 - PFAR), -(k == 1), jnp.int32)], 1)
        for k in range(3)
    ]
    load(ids_a, ids_b, lifts, 0, True)
    mutual(left, right, to_a, to_b)
    store(ids_a, ids_b, 0, True)

    ids_a, ids_b, lifts = near_ref[0], near_ref[1], near_ref[2]
    hot_a, _, _, hot_b, _, _ = hots(ids_a, ids_b, False)
    from_a = gathered(hot_a, 0, LEAVES)[35:39]
    from_b = gathered(hot_b, 0, 768)[35:39]
    count_a, count_b = from_a[3:4], from_b[3:4]
    fewer = jnp.minimum(count_a, count_b)
    swap = count_b < count_a
    group = jnp.where(fewer <= 128.0, 0, jnp.where(fewer <= 192.0, 1, 2))
    group = jnp.where(ids_b >= 0, group, -1)
    moved = jnp.zeros((1, NEAR), f32)
    for k in range(3):
        apart = from_a[k : k + 1] - from_b[k : k + 1]
        if k == 2:
            apart = apart - lifts.astype(f32) * float(CZ)
        apart = jnp.where(swap, -apart, apart)
        moved = moved + (apart + 1.0) * float(3**k)
    rows = jnp.where(swap, ids_b, ids_a)
    columns = jnp.where(swap, ids_a, ids_b)
    code = 1.0 + rows.astype(f32) + columns.astype(f32) * 512.0 + moved * 262144.0
    sort_lists(jnp.where(ids_b >= 0, code, 0.0), group, ordered_ref)

    leaf_ref[...] = total[:, 0:LEAVES]
    par_ref[...] = total[:, LEAVES + 512 :]
    for q in range(4):
        backs_ref[q] = total[:, LEAVES + q * 128 : LEAVES + q * 128 + 128]


def far_part(image, far, parent, near, cells, pcells, incoming):
    return pl.pallas_call(
        far_kernel,
        name="far_part",
        out_shape=[
            shaped(40, LEAVES), shaped(40, 128), shaped(4, 40, 128),
            jax.ShapeDtypeStruct((2, SORTED), jnp.int32),
        ],
        in_specs=[SM, VM, VM, VM, VM, VM, HB, HB, HB, HB],
        out_specs=[VM] * 4,
        scratch_shapes=[
            pltpu.VMEM((4, 5, 4, LEAF), f32),
            pltpu.VMEM((40, TABLE), f32),
        ] + [pltpu.VMEM((320, 128), f32)] * 4 + [
            pltpu.VMEM((40, TABLE), f32),
            pltpu.SemaphoreType.DMA((4,)),
        ],
        compiler_params=pltpu.CompilerParams(**PARAMS),
    )(
        image, far.transpose(1, 0, 2), parent.transpose(1, 0, 2), near.transpose(1, 0, 2),
        cells, pcells, *incoming,
    )


def shift_terms(terms, offsets):
    for axis in range(3):
        powers = [None, offsets[axis]]
        for _ in range(3):
            powers.append(powers[-1] * offsets[axis])
        moved = {}
        for alpha in ALPHAS:
            total = terms[alpha]
            for k in range(1, 5 - sum(alpha)):
                upper = tuple(alpha[q] + k * (q == axis) for q in range(3))
                total = total + terms[upper] * powers[k] * (1.0 / FACT[k])
            moved[alpha] = total
        terms = moved
    return terms


def horner(get, degree, x, y, z):
    over_x = None
    for i in range(degree, -1, -1):
        over_y = None
        for j in range(degree - i, -1, -1):
            over_z = None
            for k in range(degree - i - j, -1, -1):
                value = get((i, j, k))
                over_z = value if over_z is None else over_z * z + value
            over_y = over_z if over_y is None else over_y * y + over_z
        over_x = over_y if over_x is None else over_x * x + over_y
    return over_x


def last_kernel(
    counts_ref, send_ref, sent_leaves, sent_parents, turned_ref, near_hbm, self_hbm, leaf_ref,
    par_ref, in0, in1, in2, in3, out_ref, slab_ref, terms_ref, field_ref, near_sum, sem,
):
    incoming = (in0, in1, in2, in3)
    lane128 = iota((1, 128), 1)
    half = LEAVES // 2
    fetch_all(
        (
            (near_hbm.at[pl.ds(0, half)], near_sum.at[pl.ds(0, half)]),
            (self_hbm, near_sum.at[pl.ds(half, half)]),
        ),
        sem,
    )
    leaf = leaf_ref[...]
    par = par_ref[...]
    for q in range(4):
        block = get_block(lambda s, q=q: incoming[q][SLOTS + s])
        ids = id_row(sent_leaves, sent_parents, q)
        leaf_hot = onehot_rows(LEAVES, jnp.where(lane128 < SLOTS, ids, -1))
        parent_hot = onehot_rows(128, jnp.where(lane128 >= SLOTS, ids, -1))
        leaf = leaf + pick(block, leaf_hot, True)
        par = par + pick(block, parent_hot, True)

        def arrive(step, _, q=q):
            first = step * 8
            places = [send_ref[0, q * SLOTS + first + k] for k in range(8)]
            values = [near_sum[c] + incoming[q][first + k] for k, c in enumerate(places)]
            for c, value in zip(places, values):
                near_sum[c] = value
            return 0

        lax.fori_loop(0, SLOTS // 8, arrive, 0)
    lane_parent = (iota((128, LEAVES), 1) // CZ % CY // 2) * (CZ // 2) + iota(
        (128, LEAVES), 1
    ) % CZ // 2
    above = pick(par, jnp.where(lane_parent == iota((128, LEAVES), 0), 1.0, 0.0).astype(bf16))
    terms = {alpha: above[n : n + 1, :] for n, alpha in enumerate(ALPHAS)}
    terms = shift_terms(terms, parent_offsets())
    for n, alpha in enumerate(ALPHAS):
        terms_ref[n : n + 1, :] = leaf[n : n + 1, :] + terms[alpha]

    for half in range(2):
        lanes = slice(half * 128, half * 128 + 128)

        def term(alpha):
            return terms_ref[AT[alpha] : AT[alpha] + 1, lanes]

        def potential_at(alpha):
            return term(alpha) * (1.0 / afact(alpha))

        coefs = [{alpha: potential_at(alpha) for alpha in ALPHAS}]
        for axis in range(3):
            coefs.append(
                {
                    alpha: term(add(alpha, unit(axis))) * (-1.0 / afact(alpha))
                    for alpha in ALPHAS
                    if sum(alpha) <= 3
                }
            )

        def chunk(step, _):
            rows = pl.ds(pl.multiple_of(step * 32, 32), 32)
            x, y, z = [turned_ref[comp, rows, lanes] for comp in range(1, 4)]
            for comp in range(4):
                field_ref[comp, rows, lanes] = horner(
                    lambda alpha, comp=comp: coefs[comp][alpha], 3 if comp else 4, x, y, z
                )
            return 0

        lax.fori_loop(0, LEAF // 32, chunk, 0)

    for comp in range(4):
        turned = field_ref[comp].T
        for half in range(2):
            slab_ref[pl.ds(half * LEAVES * 8 + comp, LEAVES, stride=8), :] = turned[
                :, half * 128 : half * 128 + 128
            ]

    lane = iota((4, LEAF), 1)

    def write(c, _):
        value = jnp.concatenate(
            [
                slab_ref[pl.ds(pl.multiple_of(half * LEAVES * 8 + c * 8, 8), 8), :]
                for half in range(2)
            ],
            1,
        )[0:4] + near_sum[c]
        start = pl.multiple_of(c * LEAF, LEAF)
        out_ref[:, pl.ds(start, LEAF)] = jnp.where(lane < counts_ref[c], value, 0.0)
        return 0

    lax.fori_loop(0, LEAVES, write, 0, unroll=8)


def last(counts, send_leaves, send_parents, turned, near, self1, leaf, par, arrived):
    return pl.pallas_call(
        last_kernel,
        name="last",
        out_shape=shaped(4, LEAVES * LEAF),
        in_specs=[SM, SM, VM, VM, VM, HB, HB] + [VM] * 6,
        out_specs=VM,
        scratch_shapes=[
            pltpu.VMEM((LEAVES * 16, 128), f32),
            pltpu.VMEM((40, LEAVES), f32),
            pltpu.VMEM((4, LEAF, LEAVES), f32),
            pltpu.VMEM((LEAVES, 4, LEAF), f32),
            pltpu.SemaphoreType.DMA((2,)),
        ],
        compiler_params=pltpu.CompilerParams(**PARAMS),
    )(
        counts, send_leaves, send_leaves, send_parents, turned, near, self1, leaf, par, *arrived
    )


def image_shift(slab_at, sub_at, slab_count, sub_count):
    rows_out = []
    for direction in range(4):
        reach_x = slab_at + slab_steps[direction]
        reach_y = sub_at + sub_steps[direction]
        jump_x = (reach_x - reach_x % slab_count) * CX
        jump_y = (reach_y - reach_y % sub_count) * CY
        rows_out.append(jnp.stack([jump_x, jump_y]))
    return jnp.stack(rows_out).astype(f32)


def moved_by(value, slab_step, sub_step, slab_count, sub_count):
    pairs = []
    for slab_at in range(slab_count):
        for sub_at in range(sub_count):
            target = (slab_at + slab_step) % slab_count * sub_count + (sub_at + sub_step) % sub_count
            pairs.append((slab_at * sub_count + sub_at, target))
    return lax.ppermute(value, ("slab", "sub"), pairs)


def on_device(
    positions, masses, leaf_counts, send_leaves, send_parents, near_pairs, far_pairs, parent_pairs
):
    slab_count = lax.axis_size("slab")
    sub_count = lax.axis_size("sub")
    slab_at = lax.axis_index("slab")
    sub_at = lax.axis_index("sub")
    at = jnp.stack([slab_at, sub_at]).astype(jnp.int32)
    own, cells, pcells, *outgoing, turned = front(
        at, leaf_counts, send_leaves, send_parents, positions, masses
    )
    incoming = [
        moved_by(outgoing[q], -slab_steps[q], -sub_steps[q], slab_count, sub_count)
        for q in range(4)
    ]
    image = image_shift(slab_at, sub_at, slab_count, sub_count)
    self0 = self_part(own, 0, LEAVES // 2)
    leaf, par, backs, ordered = far_part(
        image, far_pairs, parent_pairs, near_pairs, cells, pcells, incoming
    )
    near, *returning = near_part(ordered, own, incoming, backs, self0)
    arrived = [
        moved_by(returning[q], slab_steps[q], sub_steps[q], slab_count, sub_count)
        for q in range(4)
    ]
    self1 = self_part(own, LEAVES // 2, LEAVES // 2, (near,))
    return last(
        leaf_counts, send_leaves, send_parents, turned, near, self1, leaf, par, arrived
    )


def solution(mesh):
    return jax.shard_map(
        on_device,
        mesh=mesh,
        in_specs=(
            P(None, ("slab", "sub")),
            P(("slab", "sub")),
            P(("slab", "sub")),
            P(("slab", "sub"), None),
            P(("slab", "sub"), None),
            P(("slab", "sub"), None, None),
            P(("slab", "sub"), None, None),
            P(("slab", "sub"), None, None),
        ),
        out_specs=P(None, ("slab", "sub")),
        check_vma=False,
    )
```

```python
import functools

import jax
import jax.numpy as jnp
from jax import lax
from jax.experimental import pallas as pl
from jax.experimental.pallas import tpu as pltpu
from jax.sharding import PartitionSpec as P

CX = 2
CY = 4
CZ = 32
LEAVES = 256
LEAF = 256
PARENTS = 32
SLOTS = 64
PSLOTS = 16
NEAR = 256
FAR = 1024
PFAR = 64
PAY = SLOTS + 5
SOFT = 0.0025
WIDTH = 8
SELF_WIDTH = 16
CLASSES = (128, 192, 256)
SORTED = 384
slab_steps = (1, 0, 1, 1)
sub_steps = (0, 1, 1, -1)
f32 = jnp.float32
bf16 = jnp.bfloat16

ALPHAS = [
    (i, j, d - i - j) for d in range(5) for i in range(d, -1, -1) for j in range(d - i, -1, -1)
]
AT = {a: n for n, a in enumerate(ALPHAS)}
FACT = (1.0, 1.0, 2.0, 6.0, 24.0)
TABLE = LEAVES + 4 * 128 + 128


def afact(alpha):
    return FACT[alpha[0]] * FACT[alpha[1]] * FACT[alpha[2]]


def add(a, b):
    return (a[0] + b[0], a[1] + b[1], a[2] + b[2])


def unit(axis):
    return tuple(1 if k == axis else 0 for k in range(3))


def split3(value):
    one = value.astype(bf16)
    rest = value - one.astype(f32)
    two = rest.astype(bf16)
    three = (rest - two.astype(f32)).astype(bf16)
    return one, two, three


def dot_nn(a, b):
    return lax.dot_general(a, b, (((1,), (0,)), ((), ())), preferred_element_type=f32)


def dot_nt(a, b):
    return lax.dot_general(a, b, (((1,), (1,)), ((), ())), preferred_element_type=f32)


def dot_tn(a, b):
    return lax.dot_general(a, b, (((0,), (0,)), ((), ())), preferred_element_type=f32)


def pick(values, onehot, transposed=False):
    parts = jnp.concatenate([part.astype(f32) for part in split3(values)], 0).astype(bf16)
    out = dot_nt(parts, onehot) if transposed else dot_nn(parts, onehot)
    rows = values.shape[0]
    return out[:rows] + out[rows : 2 * rows] + out[2 * rows :]


def iota(shape, dim):
    return lax.broadcasted_iota(jnp.int32, shape, dim)


def onehot_rows(count, ids):
    hit = iota((count, ids.shape[1]), 0) == ids
    return jnp.where(hit, 1.0, 0.0).astype(bf16)


def fetch_all(moves, sem):
    copies = [
        pltpu.make_async_copy(source, target, sem.at[n])
        for n, (source, target) in enumerate(moves)
    ]
    for copy in copies:
        copy.start()
    for copy in copies:
        copy.wait()


def id_row(sent_leaves, sent_parents, q):
    return jnp.concatenate(
        [
            sent_leaves[:, q * SLOTS : (q + 1) * SLOTS],
            sent_parents[:, q * PSLOTS : (q + 1) * PSLOTS],
            jnp.full((1, 128 - SLOTS - PSLOTS), -1, jnp.int32),
        ],
        1,
    )


def put_slab(slab_ref, c, slab):
    wide = jnp.concatenate([slab, jnp.zeros((4, LEAF), f32)], 0)
    for half in range(2):
        rows = pl.ds(pl.multiple_of(half * LEAVES * 8 + c * 8, 8), 8)
        slab_ref[rows, :] = wide[:, half * 128 : half * 128 + 128]


def get_rows(slab_ref, comp):
    return jnp.concatenate(
        [slab_ref[pl.ds(half * LEAVES * 8 + comp, LEAVES, stride=8), :] for half in range(2)], 1
    )


def monomials(x, y, z, w):
    made = {(0, 0, 0): w}
    for alpha in ALPHAS[1:]:
        for axis, value in ((2, z), (1, y), (0, x)):
            if alpha[axis]:
                lower = tuple(alpha[k] - (k == axis) for k in range(3))
                made[alpha] = made[lower] * value
                break
    return made


def shift_moments(moments, offsets):
    choose = ((1,), (1, 1), (1, 2, 1), (1, 3, 3, 1), (1, 4, 6, 4, 1))
    for axis in range(3):
        powers = [None, offsets[axis]]
        for _ in range(3):
            powers.append(powers[-1] * offsets[axis])
        moved = {}
        for alpha in ALPHAS:
            total = moments[alpha]
            for k in range(alpha[axis]):
                lower = tuple(k if q == axis else alpha[q] for q in range(3))
                total = total + moments[lower] * powers[alpha[axis] - k] * float(
                    choose[alpha[axis]][k]
                )
            moved[alpha] = total
        moments = moved
    return moments


def leaf_lanes():
    lane = iota((1, LEAVES), 1)
    return lane // (CY * CZ), lane // CZ % CY, lane % CZ


def parent_offsets():
    cell_x, cell_y, cell_z = leaf_lanes()
    return [(cell % 2).astype(f32) - 0.5 for cell in (cell_x, cell_y, cell_z)]


def front_kernel(
    at_ref, counts_row, sent_leaves, sent_parents, counts_hbm, send_hbm, pos_hbm, mass_hbm,
    own_ref, cells_ref, pcells_ref, pay0, pay1, pay2, pay3, turned_ref, ordered_ref,
    slab_ref, pos_ref, mass_ref, counts_ref, send_ref, sem,
):
    pays = (pay0, pay1, pay2, pay3)
    fetch_all(
        ((counts_hbm, counts_ref), (send_hbm, send_ref), (pos_hbm, pos_ref), (mass_hbm, mass_ref)),
        sem,
    )
    base_x = at_ref[0] * CX
    base_y = at_ref[1] * CY
    row4 = iota((4, LEAF), 0)
    lane = iota((1, LEAF), 1)
    batch = 8

    for x in range(CX):
        for y in range(CY):
            centre = jnp.where(row4 == 1, (base_x + x).astype(f32) + 0.5, 0.0)
            centre = jnp.where(row4 == 2, (base_y + y).astype(f32) + 0.5, centre)

            def some_leaves(step, _, x=x, y=y, centre=centre):
                low = step * batch
                first = (x * CY + y) * CZ + low
                from_z = jnp.where(row4 == 3, low.astype(f32) + 0.5, centre)
                for k in range(batch):
                    c = first + k
                    start = pl.multiple_of(c * LEAF, LEAF)
                    place = pos_ref[:, pl.ds(start, LEAF)]
                    mass = jnp.concatenate(
                        [mass_ref[pl.ds(2 * c, 1), :], mass_ref[pl.ds(2 * c + 1, 1), :]], 1
                    )
                    weight = jnp.where(lane < counts_ref[c], mass, 0.0)
                    slab = jnp.concatenate([weight, place], 0) - (
                        from_z + jnp.where(row4 == 3, float(k), 0.0)
                    )
                    own_ref[c] = slab
                    put_slab(slab_ref, c, slab)
                return 0

            lax.fori_loop(0, CZ // batch, some_leaves, 0)

    for comp in range(4):
        turned_ref[comp] = get_rows(slab_ref, comp).T

    for half in range(2):
        lanes = slice(half * 128, half * 128 + 128)

        def chunk(step, totals):
            rows = pl.ds(pl.multiple_of(step * 8, 8), 8)
            w, x, y, z = [turned_ref[comp, rows, lanes] for comp in range(4)]
            made = monomials(x, y, z, w)
            return tuple(total + made[alpha] for total, alpha in zip(totals, ALPHAS))

        totals = lax.fori_loop(
            0, LEAF // 8, chunk, tuple(jnp.zeros((8, 128), f32) for _ in ALPHAS)
        )
        for n, total in enumerate(totals):
            cells_ref[n : n + 1, lanes] = jnp.sum(total, 0, keepdims=True)

    cell_x, cell_y, cell_z = leaf_lanes()
    cells_ref[35:36, :] = (base_x + cell_x).astype(f32) + 0.5
    cells_ref[36:37, :] = (base_y + cell_y).astype(f32) + 0.5
    cells_ref[37:38, :] = cell_z.astype(f32) + 0.5
    cells_ref[38:39, :] = counts_row[...].astype(f32)
    cells_ref[39:40, :] = jnp.zeros((1, LEAVES), f32)

    moments = {alpha: cells_ref[n : n + 1, :] for n, alpha in enumerate(ALPHAS)}
    moved = shift_moments(moments, parent_offsets())
    moved = jnp.concatenate(
        [moved[alpha] for alpha in ALPHAS] + [jnp.zeros((5, LEAVES), f32)], 0
    )
    parent_of = (iota((LEAVES, 128), 0) // CZ % CY // 2) * (CZ // 2) + iota(
        (LEAVES, 128), 0
    ) % CZ // 2
    belongs = jnp.where(parent_of == iota((LEAVES, 128), 1), 1.0, 0.0).astype(bf16)
    pcells = pick(moved, belongs)
    plane = iota((40, 128), 1)
    prow = iota((40, 128), 0)
    pcells = jnp.where(prow == 35, (base_x + 1).astype(f32), pcells)
    pcells = jnp.where(
        prow == 36, (base_y + 2 * (plane // (CZ // 2))).astype(f32) + 1.0, pcells
    )
    pcells = jnp.where(prow == 37, (2 * (plane % (CZ // 2))).astype(f32) + 1.0, pcells)
    pcells_ref[...] = pcells

    lane128 = iota((1, 128), 1)
    for q in range(4):
        pay = pays[q]

        def copy_leaf(k, _, pay=pay, q=q):
            pay[k] = own_ref[send_ref[0, q * SLOTS + k]]
            return 0

        lax.fori_loop(0, SLOTS, copy_leaf, 0, unroll=8)
        ids = id_row(sent_leaves, sent_parents, q)
        leaf_hot = onehot_rows(LEAVES, jnp.where(lane128 < SLOTS, ids, -1))
        parent_hot = onehot_rows(128, jnp.where(lane128 >= SLOTS, ids, -1))
        block = pick(cells_ref[...], leaf_hot) + pick(pcells, parent_hot)
        put_block(pay, block)

    counts = counts_row[...]
    group = jnp.where(counts <= 128, 0, jnp.where(counts <= 192, 1, 2))
    sort_lists(iota((1, LEAVES), 1).astype(f32) + 1.0, group, SELF_WIDTH, ordered_ref)


def put_block(pay, block):
    for s in range(5):
        pay[SLOTS + s, :, 0:128] = block[4 * s : 4 * s + 4]
        pay[SLOTS + s, :, 128:256] = block[20 + 4 * s : 24 + 4 * s]


def get_block(tail):
    return jnp.concatenate(
        [tail(s)[:, 0:128] for s in range(5)] + [tail(s)[:, 128:256] for s in range(5)], 0
    )


VM = pl.BlockSpec(memory_space=pltpu.VMEM)
SM = pl.BlockSpec(memory_space=pltpu.SMEM)
HB = pl.BlockSpec(memory_space=pl.ANY)
HBM = pl.BlockSpec(memory_space=pltpu.MemorySpace.HBM)
PARAMS = dict(vmem_limit_bytes=48 * 1024 * 1024)


def shaped(*shape):
    return jax.ShapeDtypeStruct(shape, f32)


def front(at, counts, send_leaves, send_parents, positions, masses):
    return pl.pallas_call(
        front_kernel,
        name="front",
        out_shape=[
            shaped(LEAVES, 4, LEAF), shaped(40, LEAVES), shaped(40, 128),
        ] + [shaped(PAY, 4, LEAF)] * 4 + [
            shaped(4, LEAF, LEAVES), jax.ShapeDtypeStruct((2, SORTED), jnp.int32),
        ],
        in_specs=[SM, VM, VM, VM, HBM, HBM, HBM, HBM],
        out_specs=[VM] * 9,
        scratch_shapes=[
            pltpu.VMEM((LEAVES * 16, 128), f32),
            pltpu.VMEM((3, LEAVES * LEAF), f32),
            pltpu.VMEM((LEAVES * 2, 128), f32),
            pltpu.SMEM((LEAVES,), jnp.int32),
            pltpu.SMEM((1, 4 * SLOTS), jnp.int32),
            pltpu.SemaphoreType.DMA((4,)),
        ],
        compiler_params=pltpu.CompilerParams(vmem_limit_bytes=63 * 1024 * 1024),
    )(
        at, counts.reshape(1, LEAVES), send_leaves, send_parents, counts, send_leaves, positions,
        masses.reshape(-1, 128),
    )


def slab8(slab):
    return jnp.concatenate([slab, jnp.zeros((4, LEAF), f32)], 0)


def b_form(points):
    row = iota(points.shape, 0)
    square = jnp.sum(jnp.where(row == 0, 0.0, points * points), 0, keepdims=True)
    return jnp.where(row == 4, square, points)


def a_form(points):
    row = iota(points.shape, 0)
    square = jnp.sum(jnp.where(row == 0, 0.0, points * points), 0, keepdims=True)
    value = jnp.where(row == 0, square + SOFT, -2.0 * points)
    return jnp.where(row == 4, 1.0, value)


def widen(value):
    one = value.astype(bf16).astype(f32)
    rest = value - one
    two = rest.astype(bf16).astype(f32)
    return one, two, rest - two


def squares(a_points, b_points):
    a1, a2, a3 = widen(a_form(a_points))
    b1, b2, b3 = widen(b_form(b_points))
    left = jnp.concatenate([a1, a1, a2, a2, a1, a3], 0).astype(bf16)
    right = jnp.concatenate([b1, b2, b1, b2, b3, b1], 0).astype(bf16)
    return dot_tn(left, right)


def sources(points, weight):
    parts = widen(b_form(points) * weight)
    return jnp.concatenate(parts + (jnp.zeros_like(parts[0]),), 0).astype(bf16)


def fold(out):
    total = out[0:8]
    for first in range(8, out.shape[0] // 8 * 8, 8):
        total = total + out[first : first + 8]
    return total


def finish(total, points):
    row = iota(points.shape, 0)
    mass = total[0:1]
    pushed = points * mass
    terms = jnp.where(row == 0, SOFT * total, points * (pushed - 2.0 * total))
    terms = jnp.where(row == 4, total, terms)
    potential = jnp.sum(terms, 0, keepdims=True)
    return jnp.where(row == 0, -potential, total - pushed)[0:4]


def load_points(slab):
    wide = slab8(slab)
    row = iota((8, LEAF), 0)
    return jnp.where(row == 0, 1.0, wide), slab[0:1]


def self_kernel(part, list_ref, own_hbm, *refs):
    before_ref = refs[0] if part else None
    out_ref, own_ref, sem = refs[-3:]
    copy = pltpu.make_async_copy(own_hbm, own_ref, sem.at[0])
    copy.start()

    def begin(c, _):
        out_ref[c] = before_ref[c] if part else jnp.zeros((4, LEAF), f32)
        return 0

    lax.fori_loop(0, LEAVES, begin, 0, unroll=8)
    copy.wait()

    def some_leaves(step, rows, lanes):
        places, loaded = [], []
        for k in range(SELF_WIDTH):
            code = list_ref[0, step * SELF_WIDTH + k]
            leaf = jnp.maximum(code - 1, 0)
            points, weight = load_points(own_ref[leaf])
            places.append((leaf, jnp.where(code > 0, leaf, LEAVES)))
            loaded.append((points[:, :rows], weight[:, :rows], points[:, :lanes]))
        spaced = [squares(left, right) for left, _, right in loaded]
        apart = jnp.where(iota((rows, lanes), 0) == iota((rows, lanes), 1), 0.0, 1.0)
        cubes = []
        for value in spaced:
            inverse = lax.rsqrt(value) * apart
            cubes.append(inverse * inverse * inverse)
        high = [cube.astype(bf16) for cube in cubes]
        done = []
        for cube, top, (left, weight, right) in zip(cubes, high, loaded):
            low = (cube - top.astype(f32)).astype(bf16)
            side = sources(left, weight)
            total = fold(dot_nn(side, top)) + fold(dot_nn(side[0:16], low))
            done.append(finish(total, right))
        for (leaf, place), value in zip(places, done):
            if part:
                value = value + before_ref[leaf, :, 0:lanes]
            out_ref[place, :, 0:lanes] = value

    for n, rows in enumerate(CLASSES):
        first = list_ref[1, n]
        end = list_ref[1, n + 1]
        middle = (first + end + n % 2) >> 1
        lanes = 128 if rows == 128 else LEAF

        def body(step, _, rows=rows, lanes=lanes):
            some_leaves(step, rows, lanes)
            return 0

        lax.fori_loop(middle if part else first, end if part else middle, body, 0)


def self_part(part, ordered, own, before=()):
    return pl.pallas_call(
        functools.partial(self_kernel, part),
        name="self_part",
        out_shape=shaped(LEAVES + 8, 4, LEAF),
        in_specs=[SM, HBM] + [VM] * len(before),
        out_specs=VM,
        scratch_shapes=[pltpu.VMEM((LEAVES, 4, LEAF), f32), pltpu.SemaphoreType.DMA((1,))],
        cost_estimate=pl.CostEstimate(
            flops=LEAVES * 20_000_000, bytes_accessed=LEAVES * 8192, transcendentals=0
        ),
        compiler_params=pltpu.CompilerParams(**PARAMS),
    )(ordered, own, *before)


def near_kernel(
    list_ref, own_ref, in0, in1, in2, in3, backs_ref, self_ref,
    out_ref, pay0, pay1, pay2, pay3, table, total, shifts, sem, *held,
):
    pays = (pay0, pay1, pay2, pay3)
    copies = [pltpu.make_async_copy(own_ref, table.at[pl.ds(0, LEAVES)], sem.at[0])]
    for q, part in enumerate((in0, in1, in2, in3)):
        copies.append(
            pltpu.make_async_copy(
                part.at[pl.ds(0, SLOTS)],
                table.at[pl.ds(LEAVES + q * SLOTS, SLOTS)],
                sem.at[1 + q],
            )
        )
    for copy in copies:
        copy.start()

    def clear(c, _):
        total[c] = jnp.zeros((8, LEAF), f32)
        return 0

    lax.fori_loop(0, 2 * LEAVES + 8, clear, 0, unroll=8)
    row = iota((8, 128), 0)
    for code in range(27):
        step = (code % 3 - 1, code // 3 % 3 - 1, code // 9 - 1)
        value = jnp.zeros((8, 128), f32)
        for k in range(3):
            value = jnp.where(row == k + 1, float(step[k]), value)
        shifts[code] = value
    for copy in copies:
        copy.wait()

    def decode(group, k):
        code = list_ref[0, group * WIDTH + k]
        value = jnp.maximum(code - 1, 0)
        return value & 511, (value >> 9) & 511, value >> 18, code > 0

    def shift_of(code):
        half = shifts[code]
        return jnp.concatenate([half, half], 1)

    def spaced(group, k, rows):
        r, c, code, _ = decode(group, k)
        points_r, _ = load_points(table[r])
        points_c, _ = load_points(table[c])
        return squares((points_r + shift_of(code))[:, :rows], points_c)

    def keep(k, rows, value):
        inverse = lax.rsqrt(value)
        held[k][0:rows, :] = (inverse * inverse * inverse).astype(bf16)

    def products(group, k, rows):
        r, c, code, live = decode(group, k)
        points_r, weight_r = load_points(table[r])
        points_c, weight_c = load_points(table[c])
        shift = shift_of(code)
        cube = held[k][0:rows, :]
        side_r = sources((points_r + shift)[:, :rows], weight_r[:, :rows])
        to_c = fold(dot_nn(side_r, cube))
        to_r = fold(dot_nt(sources(points_c - shift, weight_c), cube))
        return jnp.where(live, r, 2 * LEAVES), jnp.where(live, c, 2 * LEAVES), to_r, to_c

    def settle(done, rows):
        for r, c, to_r, to_c in done:
            total[r, :, 0:rows] = total[r, :, 0:rows] + to_r
            total[c] = total[c] + to_c

    for n, rows in enumerate(CLASSES):
        first = list_ref[1, n]
        end = list_ref[1, n + 1]

        @pl.when(end > first)
        def _(first=first, end=end, rows=rows):
            for k in range(WIDTH):
                keep(k, rows, spaced(first, k, rows))

            def advance(group, _):
                done = []
                for k in range(WIDTH):
                    done.append(products(group, k, rows))
                    keep(k, rows, spaced(group + 1, k, rows))
                settle(done, rows)
                return 0

            lax.fori_loop(first, end - 1, advance, 0)
            settle([products(end - 1, k, rows) for k in range(WIDTH)], rows)

    def finish_own(c, _):
        points, _ = load_points(table[c])
        out_ref[c] = finish(total[c], points) + self_ref[c]
        return 0

    lax.fori_loop(0, LEAVES, finish_own, 0, unroll=8)
    for q in range(4):

        def finish_other(k, _, q=q):
            points, _ = load_points(table[LEAVES + q * SLOTS + k])
            pays[q][k] = finish(total[LEAVES + q * SLOTS + k], points)
            return 0

        lax.fori_loop(0, SLOTS, finish_other, 0, unroll=8)
        put_block(pays[q], backs_ref[q])


def near_part(ordered, own, incoming, backs, self0):
    return pl.pallas_call(
        near_kernel,
        name="near_part",
        out_shape=[shaped(LEAVES, 4, LEAF)] + [shaped(PAY, 4, LEAF)] * 4,
        in_specs=[SM, HB, HB, HB, HB, HB, VM, VM],
        out_specs=[VM] * 5,
        scratch_shapes=[
            pltpu.VMEM((2 * LEAVES, 4, LEAF), f32),
            pltpu.VMEM((2 * LEAVES + 8, 8, LEAF), f32),
            pltpu.VMEM((27, 8, 128), f32),
            pltpu.SemaphoreType.DMA((5,)),
        ] + [pltpu.VMEM((LEAF, LEAF), bf16)] * WIDTH,
        cost_estimate=pl.CostEstimate(
            flops=NEAR * 80_000_000, bytes_accessed=4_000_000, transcendentals=0
        ),
        compiler_params=pltpu.CompilerParams(**PARAMS),
    )(ordered, own, *incoming, backs, self0)


def sort_lists(code, group, width, out_ref):
    count = code.shape[1]
    hot = jnp.where(iota((8, count), 0) == group, 1.0, 0.0)
    earlier = jnp.where(iota((count, count), 0) < iota((count, count), 1), 1.0, 0.0).astype(bf16)
    before = dot_nn(hot.astype(bf16), earlier)
    members = jnp.sum(hot, 1, keepdims=True)
    lane = iota((1, SORTED), 1)
    place = jnp.zeros((1, count), f32)
    groups = jnp.zeros((1, 1), f32)
    ends = jnp.zeros((1, SORTED), f32)
    for n in range(len(CLASSES)):
        place = place + hot[n : n + 1] * (before[n : n + 1] + groups * width)
        groups = groups + jnp.floor((members[n : n + 1] + (width - 1)) * (1.0 / width))
        ends = jnp.where(lane == n + 1, groups, ends)
    place = jnp.where(group >= 0, place, -1.0).astype(jnp.int32)
    ordered = pick(jnp.broadcast_to(code, (8, count)), onehot_rows(SORTED, place), True)
    out_ref[0:1, :] = ordered[0:1].astype(jnp.int32)
    out_ref[1:2, :] = ends.astype(jnp.int32)


def derivatives(x, y, z):
    square = x * x + y * y + z * z
    inverse = 1.0 / jnp.sqrt(square)
    inverse2 = inverse * inverse
    table = {(0, (0, 0, 0)): inverse}
    for m in range(1, 5):
        table[(m, (0, 0, 0))] = table[(m - 1, (0, 0, 0))] * inverse2 * float(-(2 * m - 1))
    place = (x, y, z)

    def entry(m, alpha):
        key = (m, alpha)
        if key not in table:
            axis = [k for k in range(3) if alpha[k]][0]
            lower = tuple(alpha[k] - (k == axis) for k in range(3))
            value = place[axis] * entry(m + 1, lower)
            if lower[axis]:
                lowest = tuple(lower[k] - (k == axis) for k in range(3))
                value = value + float(lower[axis]) * entry(m + 1, lowest)
            table[key] = value
        return table[key]

    return {alpha: entry(0, alpha) for alpha in ALPHAS}


def mutual(a_ref, b_ref, to_a, to_b):
    def rows(n):
        return pl.ds(n * 8, 8)

    lift = a_ref[rows(38), :]
    live = a_ref[rows(39), :] > 0.5
    gap = [
        jnp.where(live, a_ref[rows(35 + k), :] - b_ref[rows(35 + k), :] - (lift if k == 2 else 0.0), 3.0)
        for k in range(3)
    ]
    made = derivatives(*gap)
    for beta in ALPHAS:
        sum_a = None
        sum_b = None
        for alpha in ALPHAS:
            if sum(alpha) + sum(beta) > 4:
                continue
            tensor = made[add(alpha, beta)]
            scale = 1.0 / afact(alpha)
            sign_a = -((-1.0) ** sum(alpha)) * scale
            sign_b = -((-1.0) ** sum(beta)) * scale
            term_a = b_ref[rows(AT[alpha]), :] * sign_a * tensor
            term_b = a_ref[rows(AT[alpha]), :] * sign_b * tensor
            sum_a = term_a if sum_a is None else sum_a + term_a
            sum_b = term_b if sum_b is None else sum_b + term_b
        to_a[rows(AT[beta]), :] = jnp.where(live, sum_a, 0.0)
        to_b[rows(AT[beta]), :] = jnp.where(live, sum_b, 0.0)


def far_kernel(
    image_ref, far_ref, parent_ref, near_ref, cells_ref, pcells_ref, in0, in1, in2, in3,
    leaf_ref, par_ref, backs_ref, ordered_ref, tails, table, left, right, to_a, to_b, total, sem,
):
    copies = []
    for q, part in enumerate((in0, in1, in2, in3)):
        copies.append(
            pltpu.make_async_copy(part.at[pl.ds(SLOTS, 5)], tails.at[q], sem.at[q])
        )
    for copy in copies:
        copy.start()
    table[:, 0:LEAVES] = cells_ref[...]
    table[:, LEAVES + 512 :] = pcells_ref[...]
    row = iota((40, 128), 0)
    to_a[...] = jnp.zeros_like(to_a)
    to_b[...] = jnp.zeros_like(to_b)
    left[...] = jnp.zeros_like(left)
    right[...] = jnp.zeros_like(right)
    for copy in copies:
        copy.wait()
    for q in range(4):
        block = get_block(lambda s, q=q: tails[q, s])
        block = block + jnp.where(
            row == 35, image_ref[q, 0], jnp.where(row == 36, image_ref[q, 1], 0.0)
        )
        table[:, LEAVES + q * 128 : LEAVES + q * 128 + 128] = block
    parts = jnp.concatenate([part.astype(f32) for part in split3(table[...])], 0).astype(bf16)
    total[...] = jnp.zeros_like(total)

    def gathered(hot, first, count):
        out = dot_nn(parts[:, first : first + count], hot)
        return out[0:40] + out[40:80] + out[80:120]

    def leaf_entry(ids):
        other = ids - LEAVES
        return jnp.where(ids < LEAVES, ids, LEAVES + other // SLOTS * 128 + other % SLOTS)

    def parent_entry(ids):
        other = ids - PARENTS
        return jnp.where(
            ids < PARENTS, LEAVES + 512 + ids, LEAVES + other // PSLOTS * 128 + SLOTS + other % PSLOTS
        )

    def hots(ids_a, ids_b, parents):
        if parents:
            return (
                onehot_rows(128, ids_a), LEAVES + 512, 128,
                onehot_rows(640, parent_entry(ids_b) - LEAVES), LEAVES, 640,
            )
        return (
            onehot_rows(LEAVES, ids_a), 0, LEAVES,
            onehot_rows(768, leaf_entry(ids_b)), 0, 768,
        )

    def load(ids_a, ids_b, lifts, g, parents):
        hot_a, first_a, count_a, hot_b, first_b, count_b = hots(ids_a, ids_b, parents)
        from_a = gathered(hot_a, first_a, count_a)
        from_b = gathered(hot_b, first_b, count_b)
        live = jnp.where(ids_b >= 0, 1.0, 0.0)
        from_a = jnp.where(row == 38, lifts.astype(f32) * float(CZ), from_a)
        from_a = jnp.where(row == 39, live, from_a)
        left[pl.ds(g, 40, stride=8), :] = from_a
        right[pl.ds(g, 40, stride=8), :] = from_b

    def store(ids_a, ids_b, g, parents):
        hot_a, first_a, count_a, hot_b, first_b, count_b = hots(ids_a, ids_b, parents)
        sum_a = pick(to_a[pl.ds(g, 40, stride=8), :], hot_a, True)
        sum_b = pick(to_b[pl.ds(g, 40, stride=8), :], hot_b, True)
        total[:, first_a : first_a + count_a] += sum_a
        total[:, first_b : first_b + count_b] += sum_b

    for g in range(FAR // 128):
        lanes = slice(g * 128, g * 128 + 128)
        load(far_ref[0, :, lanes], far_ref[1, :, lanes], far_ref[2, :, lanes], g, False)
    mutual(left, right, to_a, to_b)
    for g in range(FAR // 128):
        lanes = slice(g * 128, g * 128 + 128)
        store(far_ref[0, :, lanes], far_ref[1, :, lanes], g, False)
    ids_a, ids_b, lifts = [
        jnp.concatenate([parent_ref[k], jnp.full((1, 128 - PFAR), -(k == 1), jnp.int32)], 1)
        for k in range(3)
    ]
    load(ids_a, ids_b, lifts, 0, True)
    mutual(left, right, to_a, to_b)
    store(ids_a, ids_b, 0, True)

    ids_a, ids_b, lifts = near_ref[0], near_ref[1], near_ref[2]
    hot_a, _, _, hot_b, _, _ = hots(ids_a, ids_b, False)
    from_a = gathered(hot_a, 0, LEAVES)[35:39]
    from_b = gathered(hot_b, 0, 768)[35:39]
    count_a, count_b = from_a[3:4], from_b[3:4]
    fewer = jnp.minimum(count_a, count_b)
    swap = count_b < count_a
    group = jnp.where(fewer <= 128.0, 0, jnp.where(fewer <= 192.0, 1, 2))
    group = jnp.where(ids_b >= 0, group, -1)
    moved = jnp.zeros((1, NEAR), f32)
    for k in range(3):
        apart = from_a[k : k + 1] - from_b[k : k + 1]
        if k == 2:
            apart = apart - lifts.astype(f32) * float(CZ)
        apart = jnp.where(swap, -apart, apart)
        moved = moved + (apart + 1.0) * float(3**k)
    rows = jnp.where(swap, ids_b, ids_a)
    columns = jnp.where(swap, ids_a, ids_b)
    code = 1.0 + rows.astype(f32) + columns.astype(f32) * 512.0 + moved * 262144.0
    sort_lists(jnp.where(ids_b >= 0, code, 0.0), group, WIDTH, ordered_ref)

    leaf_ref[...] = total[:, 0:LEAVES]
    par_ref[...] = total[:, LEAVES + 512 :]
    for q in range(4):
        backs_ref[q] = total[:, LEAVES + q * 128 : LEAVES + q * 128 + 128]


def far_part(image, far, parent, near, cells, pcells, incoming):
    return pl.pallas_call(
        far_kernel,
        name="far_part",
        out_shape=[
            shaped(40, LEAVES), shaped(40, 128), shaped(4, 40, 128),
            jax.ShapeDtypeStruct((2, SORTED), jnp.int32),
        ],
        in_specs=[SM, VM, VM, VM, VM, VM, HB, HB, HB, HB],
        out_specs=[VM] * 4,
        scratch_shapes=[
            pltpu.VMEM((4, 5, 4, LEAF), f32),
            pltpu.VMEM((40, TABLE), f32),
        ] + [pltpu.VMEM((320, 128), f32)] * 4 + [
            pltpu.VMEM((40, TABLE), f32),
            pltpu.SemaphoreType.DMA((4,)),
        ],
        compiler_params=pltpu.CompilerParams(**PARAMS),
    )(
        image, far.transpose(1, 0, 2), parent.transpose(1, 0, 2), near.transpose(1, 0, 2),
        cells, pcells, *incoming,
    )


def shift_terms(terms, offsets):
    for axis in range(3):
        powers = [None, offsets[axis]]
        for _ in range(3):
            powers.append(powers[-1] * offsets[axis])
        moved = {}
        for alpha in ALPHAS:
            total = terms[alpha]
            for k in range(1, 5 - sum(alpha)):
                upper = tuple(alpha[q] + k * (q == axis) for q in range(3))
                total = total + terms[upper] * powers[k] * (1.0 / FACT[k])
            moved[alpha] = total
        terms = moved
    return terms


def horner(get, degree, x, y, z):
    over_x = None
    for i in range(degree, -1, -1):
        over_y = None
        for j in range(degree - i, -1, -1):
            over_z = None
            for k in range(degree - i - j, -1, -1):
                value = get((i, j, k))
                over_z = value if over_z is None else over_z * z + value
            over_y = over_z if over_y is None else over_y * y + over_z
        over_x = over_y if over_x is None else over_x * x + over_y
    return over_x


def last_kernel(
    counts_ref, send_ref, sent_leaves, sent_parents, turned_ref, self_hbm, leaf_ref,
    par_ref, in0, in1, in2, in3, out_ref, slab_ref, terms_ref, field_ref, near_sum, sem,
):
    incoming = (in0, in1, in2, in3)
    lane128 = iota((1, 128), 1)
    fetch_all(((self_hbm.at[pl.ds(0, LEAVES)], near_sum),), sem)
    leaf = leaf_ref[...]
    par = par_ref[...]
    for q in range(4):
        block = get_block(lambda s, q=q: incoming[q][SLOTS + s])
        ids = id_row(sent_leaves, sent_parents, q)
        leaf_hot = onehot_rows(LEAVES, jnp.where(lane128 < SLOTS, ids, -1))
        parent_hot = onehot_rows(128, jnp.where(lane128 >= SLOTS, ids, -1))
        leaf = leaf + pick(block, leaf_hot, True)
        par = par + pick(block, parent_hot, True)

        def arrive(step, _, q=q):
            first = step * 8
            places = [send_ref[0, q * SLOTS + first + k] for k in range(8)]
            values = [near_sum[c] + incoming[q][first + k] for k, c in enumerate(places)]
            for c, value in zip(places, values):
                near_sum[c] = value
            return 0

        lax.fori_loop(0, SLOTS // 8, arrive, 0)
    lane_parent = (iota((128, LEAVES), 1) // CZ % CY // 2) * (CZ // 2) + iota(
        (128, LEAVES), 1
    ) % CZ // 2
    above = pick(par, jnp.where(lane_parent == iota((128, LEAVES), 0), 1.0, 0.0).astype(bf16))
    terms = {alpha: above[n : n + 1, :] for n, alpha in enumerate(ALPHAS)}
    terms = shift_terms(terms, parent_offsets())
    for n, alpha in enumerate(ALPHAS):
        terms_ref[n : n + 1, :] = leaf[n : n + 1, :] + terms[alpha]

    for half in range(2):
        lanes = slice(half * 128, half * 128 + 128)

        def term(alpha):
            return terms_ref[AT[alpha] : AT[alpha] + 1, lanes]

        def potential_at(alpha):
            return term(alpha) * (1.0 / afact(alpha))

        coefs = [{alpha: potential_at(alpha) for alpha in ALPHAS}]
        for axis in range(3):
            coefs.append(
                {
                    alpha: term(add(alpha, unit(axis))) * (-1.0 / afact(alpha))
                    for alpha in ALPHAS
                    if sum(alpha) <= 3
                }
            )

        def chunk(step, _):
            rows = pl.ds(pl.multiple_of(step * 32, 32), 32)
            x, y, z = [turned_ref[comp, rows, lanes] for comp in range(1, 4)]
            for comp in range(4):
                field_ref[comp, rows, lanes] = horner(
                    lambda alpha, comp=comp: coefs[comp][alpha], 3 if comp else 4, x, y, z
                )
            return 0

        lax.fori_loop(0, LEAF // 32, chunk, 0)

    for comp in range(4):
        turned = field_ref[comp].T
        for half in range(2):
            slab_ref[pl.ds(half * LEAVES * 8 + comp, LEAVES, stride=8), :] = turned[
                :, half * 128 : half * 128 + 128
            ]

    lane = iota((4, LEAF), 1)

    def write(c, _):
        value = jnp.concatenate(
            [
                slab_ref[pl.ds(pl.multiple_of(half * LEAVES * 8 + c * 8, 8), 8), :]
                for half in range(2)
            ],
            1,
        )[0:4] + near_sum[c]
        start = pl.multiple_of(c * LEAF, LEAF)
        out_ref[:, pl.ds(start, LEAF)] = jnp.where(lane < counts_ref[c], value, 0.0)
        return 0

    lax.fori_loop(0, LEAVES, write, 0, unroll=8)


def last(counts, send_leaves, send_parents, turned, near, leaf, par, arrived):
    return pl.pallas_call(
        last_kernel,
        name="last",
        out_shape=shaped(4, LEAVES * LEAF),
        in_specs=[SM, SM, VM, VM, VM, HB] + [VM] * 6,
        out_specs=VM,
        scratch_shapes=[
            pltpu.VMEM((LEAVES * 16, 128), f32),
            pltpu.VMEM((40, LEAVES), f32),
            pltpu.VMEM((4, LEAF, LEAVES), f32),
            pltpu.VMEM((LEAVES, 4, LEAF), f32),
            pltpu.SemaphoreType.DMA((1,)),
        ],
        compiler_params=pltpu.CompilerParams(**PARAMS),
    )(
        counts, send_leaves, send_leaves, send_parents, turned, near, leaf, par, *arrived
    )


def image_shift(slab_at, sub_at, slab_count, sub_count):
    rows_out = []
    for direction in range(4):
        reach_x = slab_at + slab_steps[direction]
        reach_y = sub_at + sub_steps[direction]
        jump_x = (reach_x - reach_x % slab_count) * CX
        jump_y = (reach_y - reach_y % sub_count) * CY
        rows_out.append(jnp.stack([jump_x, jump_y]))
    return jnp.stack(rows_out).astype(f32)


def moved_by(value, slab_step, sub_step, slab_count, sub_count):
    pairs = []
    for slab_at in range(slab_count):
        for sub_at in range(sub_count):
            target = (slab_at + slab_step) % slab_count * sub_count + (sub_at + sub_step) % sub_count
            pairs.append((slab_at * sub_count + sub_at, target))
    return lax.ppermute(value, ("slab", "sub"), pairs)


def on_device(
    positions, masses, leaf_counts, send_leaves, send_parents, near_pairs, far_pairs, parent_pairs
):
    slab_count = lax.axis_size("slab")
    sub_count = lax.axis_size("sub")
    slab_at = lax.axis_index("slab")
    sub_at = lax.axis_index("sub")
    at = jnp.stack([slab_at, sub_at]).astype(jnp.int32)
    own, cells, pcells, *outgoing, turned, leaf_order = front(
        at, leaf_counts, send_leaves, send_parents, positions, masses
    )
    incoming = [
        moved_by(outgoing[q], -slab_steps[q], -sub_steps[q], slab_count, sub_count)
        for q in range(4)
    ]
    image = image_shift(slab_at, sub_at, slab_count, sub_count)
    self0 = self_part(0, leaf_order, own)
    leaf, par, backs, ordered = far_part(
        image, far_pairs, parent_pairs, near_pairs, cells, pcells, incoming
    )
    near, *returning = near_part(ordered, own, incoming, backs, self0)
    arrived = [
        moved_by(returning[q], slab_steps[q], sub_steps[q], slab_count, sub_count)
        for q in range(4)
    ]
    near = self_part(1, leaf_order, own, (near,))
    return last(
        leaf_counts, send_leaves, send_parents, turned, near, leaf, par, arrived
    )


def solution(mesh):
    return jax.shard_map(
        on_device,
        mesh=mesh,
        in_specs=(
            P(None, ("slab", "sub")),
            P(("slab", "sub")),
            P(("slab", "sub")),
            P(("slab", "sub"), None),
            P(("slab", "sub"), None),
            P(("slab", "sub"), None, None),
            P(("slab", "sub"), None, None),
            P(("slab", "sub"), None, None),
        ),
        out_specs=P(None, ("slab", "sub")),
        check_vma=False,
    )
```

```python
import functools

import jax
import jax.numpy as jnp
from jax import lax
from jax.experimental import pallas as pl
from jax.experimental.pallas import tpu as pltpu
from jax.sharding import PartitionSpec as P

CX = 2
CY = 4
CZ = 32
LEAVES = 256
LEAF = 256
PARENTS = 32
SLOTS = 64
PSLOTS = 16
NEAR = 256
FAR = 1024
PFAR = 64
PAY = SLOTS + 5
SOFT = 0.0025
WIDTH = 8
SELF_WIDTH = 16
CLASSES = (128, 192, 256)
SORTED = 384
slab_steps = (1, 0, 1, 1)
sub_steps = (0, 1, 1, -1)
f32 = jnp.float32
bf16 = jnp.bfloat16

ALPHAS = [
    (i, j, d - i - j) for d in range(5) for i in range(d, -1, -1) for j in range(d - i, -1, -1)
]
AT = {a: n for n, a in enumerate(ALPHAS)}
FACT = (1.0, 1.0, 2.0, 6.0, 24.0)
TABLE = LEAVES + 4 * 128 + 128


def afact(alpha):
    return FACT[alpha[0]] * FACT[alpha[1]] * FACT[alpha[2]]


def add(a, b):
    return (a[0] + b[0], a[1] + b[1], a[2] + b[2])


def unit(axis):
    return tuple(1 if k == axis else 0 for k in range(3))


def split3(value):
    one = value.astype(bf16)
    rest = value - one.astype(f32)
    two = rest.astype(bf16)
    three = (rest - two.astype(f32)).astype(bf16)
    return one, two, three


def dot_nn(a, b):
    return lax.dot_general(a, b, (((1,), (0,)), ((), ())), preferred_element_type=f32)


def dot_nt(a, b):
    return lax.dot_general(a, b, (((1,), (1,)), ((), ())), preferred_element_type=f32)


def dot_tn(a, b):
    return lax.dot_general(a, b, (((0,), (0,)), ((), ())), preferred_element_type=f32)


def pick(values, onehot, transposed=False):
    parts = jnp.concatenate([part.astype(f32) for part in split3(values)], 0).astype(bf16)
    out = dot_nt(parts, onehot) if transposed else dot_nn(parts, onehot)
    rows = values.shape[0]
    return out[:rows] + out[rows : 2 * rows] + out[2 * rows :]


def iota(shape, dim):
    return lax.broadcasted_iota(jnp.int32, shape, dim)


def onehot_rows(count, ids):
    hit = iota((count, ids.shape[1]), 0) == ids
    return jnp.where(hit, 1.0, 0.0).astype(bf16)


def fetch_all(moves, sem):
    copies = [
        pltpu.make_async_copy(source, target, sem.at[n])
        for n, (source, target) in enumerate(moves)
    ]
    for copy in copies:
        copy.start()
    for copy in copies:
        copy.wait()


def id_row(sent_leaves, sent_parents, q):
    return jnp.concatenate(
        [
            sent_leaves[:, q * SLOTS : (q + 1) * SLOTS],
            sent_parents[:, q * PSLOTS : (q + 1) * PSLOTS],
            jnp.full((1, 128 - SLOTS - PSLOTS), -1, jnp.int32),
        ],
        1,
    )


def put_slab(slab_ref, c, slab):
    wide = jnp.concatenate([slab, jnp.zeros((4, LEAF), f32)], 0)
    for half in range(2):
        rows = pl.ds(pl.multiple_of(half * LEAVES * 8 + c * 8, 8), 8)
        slab_ref[rows, :] = wide[:, half * 128 : half * 128 + 128]


def get_rows(slab_ref, comp):
    return jnp.concatenate(
        [slab_ref[pl.ds(half * LEAVES * 8 + comp, LEAVES, stride=8), :] for half in range(2)], 1
    )


def monomials(x, y, z, w):
    made = {(0, 0, 0): w}
    for alpha in ALPHAS[1:]:
        for axis, value in ((2, z), (1, y), (0, x)):
            if alpha[axis]:
                lower = tuple(alpha[k] - (k == axis) for k in range(3))
                made[alpha] = made[lower] * value
                break
    return made


def shift_moments(moments, offsets):
    choose = ((1,), (1, 1), (1, 2, 1), (1, 3, 3, 1), (1, 4, 6, 4, 1))
    for axis in range(3):
        powers = [None, offsets[axis]]
        for _ in range(3):
            powers.append(powers[-1] * offsets[axis])
        moved = {}
        for alpha in ALPHAS:
            total = moments[alpha]
            for k in range(alpha[axis]):
                lower = tuple(k if q == axis else alpha[q] for q in range(3))
                total = total + moments[lower] * powers[alpha[axis] - k] * float(
                    choose[alpha[axis]][k]
                )
            moved[alpha] = total
        moments = moved
    return moments


def leaf_lanes():
    lane = iota((1, LEAVES), 1)
    return lane // (CY * CZ), lane // CZ % CY, lane % CZ


def parent_offsets():
    cell_x, cell_y, cell_z = leaf_lanes()
    return [(cell % 2).astype(f32) - 0.5 for cell in (cell_x, cell_y, cell_z)]


def front_kernel(
    at_ref, counts_hbm, row_hbm, send_hbm, parents_hbm, pos_hbm, mass_hbm,
    own_ref, cells_ref, pcells_ref, pay0, pay1, pay2, pay3, turned_ref, ordered_ref,
    slab_ref, pos_ref, mass_ref, counts_ref, send_ref, counts_row, sent_leaves, sent_parents, sem,
):
    pays = (pay0, pay1, pay2, pay3)
    pieces = CX * CY
    bodies = LEAVES * LEAF // pieces
    places = [
        pltpu.make_async_copy(
            pos_hbm.at[:, pl.ds(n * bodies, bodies)], pos_ref.at[:, pl.ds(n * bodies, bodies)],
            sem.at[6 + n],
        )
        for n in range(pieces)
    ]
    smaller = [
        pltpu.make_async_copy(source, target, sem.at[n])
        for n, (source, target) in enumerate(
            (
                (counts_hbm, counts_ref), (mass_hbm, mass_ref), (send_hbm, send_ref),
                (row_hbm, counts_row), (send_hbm, sent_leaves), (parents_hbm, sent_parents),
            )
        )
    ]
    for copy in smaller[:2] + places + smaller[2:]:
        copy.start()
    for copy in smaller:
        copy.wait()
    base_x = at_ref[0] * CX
    base_y = at_ref[1] * CY
    row4 = iota((4, LEAF), 0)
    lane = iota((1, LEAF), 1)
    batch = 8

    for x in range(CX):
        for y in range(CY):
            centre = jnp.where(row4 == 1, (base_x + x).astype(f32) + 0.5, 0.0)
            centre = jnp.where(row4 == 2, (base_y + y).astype(f32) + 0.5, centre)
            places[x * CY + y].wait()

            def some_leaves(step, _, x=x, y=y, centre=centre):
                low = step * batch
                first = (x * CY + y) * CZ + low
                from_z = jnp.where(row4 == 3, low.astype(f32) + 0.5, centre)
                for k in range(batch):
                    c = first + k
                    start = pl.multiple_of(c * LEAF, LEAF)
                    place = pos_ref[:, pl.ds(start, LEAF)]
                    mass = jnp.concatenate(
                        [mass_ref[pl.ds(2 * c, 1), :], mass_ref[pl.ds(2 * c + 1, 1), :]], 1
                    )
                    weight = jnp.where(lane < counts_ref[c], mass, 0.0)
                    slab = jnp.concatenate([weight, place], 0) - (
                        from_z + jnp.where(row4 == 3, float(k), 0.0)
                    )
                    own_ref[c] = slab
                    put_slab(slab_ref, c, slab)
                return 0

            lax.fori_loop(0, CZ // batch, some_leaves, 0)

    for comp in range(4):
        turned_ref[comp] = get_rows(slab_ref, comp).T

    for half in range(2):
        lanes = slice(half * 128, half * 128 + 128)

        def chunk(step, totals):
            rows = pl.ds(pl.multiple_of(step * 8, 8), 8)
            w, x, y, z = [turned_ref[comp, rows, lanes] for comp in range(4)]
            made = monomials(x, y, z, w)
            return tuple(total + made[alpha] for total, alpha in zip(totals, ALPHAS))

        totals = lax.fori_loop(
            0, LEAF // 8, chunk, tuple(jnp.zeros((8, 128), f32) for _ in ALPHAS)
        )
        for n, total in enumerate(totals):
            cells_ref[n : n + 1, lanes] = jnp.sum(total, 0, keepdims=True)

    cell_x, cell_y, cell_z = leaf_lanes()
    cells_ref[35:36, :] = (base_x + cell_x).astype(f32) + 0.5
    cells_ref[36:37, :] = (base_y + cell_y).astype(f32) + 0.5
    cells_ref[37:38, :] = cell_z.astype(f32) + 0.5
    cells_ref[38:39, :] = counts_row[...].astype(f32)
    cells_ref[39:40, :] = jnp.zeros((1, LEAVES), f32)

    moments = {alpha: cells_ref[n : n + 1, :] for n, alpha in enumerate(ALPHAS)}
    moved = shift_moments(moments, parent_offsets())
    moved = jnp.concatenate(
        [moved[alpha] for alpha in ALPHAS] + [jnp.zeros((5, LEAVES), f32)], 0
    )
    parent_of = (iota((LEAVES, 128), 0) // CZ % CY // 2) * (CZ // 2) + iota(
        (LEAVES, 128), 0
    ) % CZ // 2
    belongs = jnp.where(parent_of == iota((LEAVES, 128), 1), 1.0, 0.0).astype(bf16)
    pcells = pick(moved, belongs)
    plane = iota((40, 128), 1)
    prow = iota((40, 128), 0)
    pcells = jnp.where(prow == 35, (base_x + 1).astype(f32), pcells)
    pcells = jnp.where(
        prow == 36, (base_y + 2 * (plane // (CZ // 2))).astype(f32) + 1.0, pcells
    )
    pcells = jnp.where(prow == 37, (2 * (plane % (CZ // 2))).astype(f32) + 1.0, pcells)
    pcells_ref[...] = pcells

    lane128 = iota((1, 128), 1)
    for q in range(4):
        pay = pays[q]

        def copy_leaf(k, _, pay=pay, q=q):
            pay[k] = own_ref[send_ref[0, q * SLOTS + k]]
            return 0

        lax.fori_loop(0, SLOTS, copy_leaf, 0, unroll=8)
        ids = id_row(sent_leaves, sent_parents, q)
        leaf_hot = onehot_rows(LEAVES, jnp.where(lane128 < SLOTS, ids, -1))
        parent_hot = onehot_rows(128, jnp.where(lane128 >= SLOTS, ids, -1))
        block = pick(cells_ref[...], leaf_hot) + pick(pcells, parent_hot)
        put_block(pay, block)

    counts = counts_row[...]
    group = jnp.where(counts <= 128, 0, jnp.where(counts <= 192, 1, 2))
    sort_lists(iota((1, LEAVES), 1).astype(f32) + 1.0, group, SELF_WIDTH, ordered_ref)


def put_block(pay, block):
    for s in range(5):
        pay[SLOTS + s, :, 0:128] = block[4 * s : 4 * s + 4]
        pay[SLOTS + s, :, 128:256] = block[20 + 4 * s : 24 + 4 * s]


def get_block(tail):
    return jnp.concatenate(
        [tail(s)[:, 0:128] for s in range(5)] + [tail(s)[:, 128:256] for s in range(5)], 0
    )


VM = pl.BlockSpec(memory_space=pltpu.VMEM)
SM = pl.BlockSpec(memory_space=pltpu.SMEM)
HB = pl.BlockSpec(memory_space=pl.ANY)
HBM = pl.BlockSpec(memory_space=pltpu.MemorySpace.HBM)
PARAMS = dict(vmem_limit_bytes=24 * 1024 * 1024)


def in_hbm(value):
    return pltpu.with_memory_space_constraint(value, pltpu.MemorySpace.HBM)


def shaped(*shape):
    return jax.ShapeDtypeStruct(shape, f32)


def front(at, counts, send_leaves, send_parents, positions, masses):
    return pl.pallas_call(
        front_kernel,
        name="front",
        out_shape=[
            shaped(LEAVES, 4, LEAF), shaped(40, LEAVES), shaped(40, 128),
        ] + [shaped(PAY, 4, LEAF)] * 4 + [
            shaped(4, LEAF, LEAVES), jax.ShapeDtypeStruct((2, SORTED), jnp.int32),
        ],
        in_specs=[SM] + [HBM] * 6,
        out_specs=[VM] * 9,
        scratch_shapes=[
            pltpu.VMEM((LEAVES * 16, 128), f32),
            pltpu.VMEM((3, LEAVES * LEAF), f32),
            pltpu.VMEM((LEAVES * 2, 128), f32),
            pltpu.SMEM((LEAVES,), jnp.int32),
            pltpu.SMEM((1, 4 * SLOTS), jnp.int32),
            pltpu.VMEM((1, LEAVES), jnp.int32),
            pltpu.VMEM((1, 4 * SLOTS), jnp.int32),
            pltpu.VMEM((1, 4 * PSLOTS), jnp.int32),
            pltpu.SemaphoreType.DMA((6 + CX * CY,)),
        ],
        compiler_params=pltpu.CompilerParams(**PARAMS),
    )(
        at,
        *map(
            in_hbm,
            (
                counts, counts.reshape(1, LEAVES), send_leaves, send_parents, positions,
                masses.reshape(-1, 128),
            ),
        ),
    )


def slab8(slab):
    return jnp.concatenate([slab, jnp.zeros((4, LEAF), f32)], 0)


def b_form(points):
    row = iota(points.shape, 0)
    square = jnp.sum(jnp.where(row == 0, 0.0, points * points), 0, keepdims=True)
    return jnp.where(row == 4, square, points)


def a_form(points):
    row = iota(points.shape, 0)
    square = jnp.sum(jnp.where(row == 0, 0.0, points * points), 0, keepdims=True)
    value = jnp.where(row == 0, square + SOFT, -2.0 * points)
    return jnp.where(row == 4, 1.0, value)


def widen(value):
    one = value.astype(bf16).astype(f32)
    rest = value - one
    two = rest.astype(bf16).astype(f32)
    return one, two, rest - two


def squares(a_points, b_points):
    a1, a2, a3 = widen(a_form(a_points))
    b1, b2, b3 = widen(b_form(b_points))
    left = jnp.concatenate([a1, a1, a2, a2, a1, a3], 0).astype(bf16)
    right = jnp.concatenate([b1, b2, b1, b2, b3, b1], 0).astype(bf16)
    return dot_tn(left, right)


def sources(points, weight):
    parts = widen(b_form(points) * weight)
    return jnp.concatenate(parts + (jnp.zeros_like(parts[0]),), 0).astype(bf16)


def fold(out):
    total = out[0:8]
    for first in range(8, out.shape[0] // 8 * 8, 8):
        total = total + out[first : first + 8]
    return total


def finish(total, points):
    row = iota(points.shape, 0)
    field = total - points * total[0:1]
    sign = jnp.where(row == 0, -SOFT, jnp.where(row == 4, -1.0, 1.0))
    terms = jnp.where(row == 4, total, points * (field + total)) * sign
    return jnp.where(row == 0, jnp.sum(terms, 0, keepdims=True), field)[0:4]


def load_points(slab):
    wide = slab8(slab)
    row = iota((8, LEAF), 0)
    return jnp.where(row == 0, 1.0, wide), slab[0:1]


def self_kernel(part, list_ref, own_hbm, *refs):
    if part:
        before_hbm, out_ref, own_ref, before_ref, sem = refs
        moves = ((own_hbm, own_ref), (before_hbm, before_ref))
    else:
        out_ref, own_ref, sem = refs
        moves = ((own_hbm, own_ref),)
    copies = [
        pltpu.make_async_copy(source, target, sem.at[n])
        for n, (source, target) in enumerate(moves)
    ]
    for copy in copies:
        copy.start()
    if not part:

        def begin(c, _):
            out_ref[c] = jnp.zeros((8, LEAF), f32)
            return 0

        lax.fori_loop(0, LEAVES, begin, 0, unroll=8)
    for copy in copies:
        copy.wait()

    def place_of(step, k):
        code = list_ref[0, step * SELF_WIDTH + k]
        leaf = jnp.maximum(code - 1, 0)
        return leaf, jnp.where(code > 0, leaf, LEAVES)

    def some_leaves(step, rows, lanes):
        places = [place_of(step, k) for k in range(SELF_WIDTH)]
        loaded = []
        for leaf, _ in places:
            points, weight = load_points(own_ref[leaf])
            loaded.append((points[:, :rows], weight[:, :rows], points[:, :lanes]))
        spaced = [squares(left, right) for left, _, right in loaded]
        apart = jnp.where(iota((rows, lanes), 0) == iota((rows, lanes), 1), 0.0, 1.0)
        cubes = []
        for value in spaced:
            inverse = lax.rsqrt(value) * apart
            cubes.append(inverse * inverse * inverse)
        high = [cube.astype(bf16) for cube in cubes]
        done = []
        for cube, top, (left, weight, right), (leaf, _) in zip(cubes, high, loaded, places):
            low = (cube - top.astype(f32)).astype(bf16)
            side = sources(left, weight)
            value = fold(dot_nn(side, top)) + fold(dot_nn(side[0:16], low))
            if part:
                value = finish(value + before_ref[leaf, :, 0:lanes], right)
            done.append(value)
        for (_, place), value in zip(places, done):
            out_ref[place, :, 0:lanes] = value

    def finish_some(step):
        places = [place_of(step, k) for k in range(SELF_WIDTH)]
        done = [finish(before_ref[leaf], load_points(own_ref[leaf])[0]) for leaf, _ in places]
        for (_, place), value in zip(places, done):
            out_ref[place] = value

    for n, rows in enumerate(CLASSES):
        first = list_ref[1, n]
        end = list_ref[1, n + 1]
        middle = (first + end + n % 2) >> 1
        lanes = 128 if rows == 128 else LEAF

        def body(step, _, rows=rows, lanes=lanes):
            some_leaves(step, rows, lanes)
            return 0

        lax.fori_loop(middle if part else first, end if part else middle, body, 0)
        if part:

            def rest(step, _):
                finish_some(step)
                return 0

            lax.fori_loop(first, middle, rest, 0)


def self_part(part, ordered, own, *before):
    return pl.pallas_call(
        functools.partial(self_kernel, part),
        name="self_part",
        out_shape=shaped(LEAVES + 8, 4 if part else 8, LEAF),
        in_specs=[SM, HB] + [HB] * part,
        out_specs=VM,
        scratch_shapes=[pltpu.VMEM((LEAVES, 4, LEAF), f32)]
        + [pltpu.VMEM((LEAVES, 8, LEAF), f32)] * part
        + [pltpu.SemaphoreType.DMA((2,))],
        cost_estimate=pl.CostEstimate(
            flops=LEAVES * 20_000_000, bytes_accessed=LEAVES * 8192, transcendentals=0
        ),
        compiler_params=pltpu.CompilerParams(**PARAMS),
    )(ordered, own, *before)


def near_kernel(
    list_ref, own_ref, in0, in1, in2, in3, backs_ref, self_ref,
    out_ref, pay0, pay1, pay2, pay3, table, total, shifts, sem, *held,
):
    pays = (pay0, pay1, pay2, pay3)
    copies = [
        pltpu.make_async_copy(own_ref, table.at[pl.ds(0, LEAVES)], sem.at[0]),
        pltpu.make_async_copy(self_ref.at[pl.ds(0, LEAVES)], total.at[pl.ds(0, LEAVES)], sem.at[5]),
    ]
    for q, part in enumerate((in0, in1, in2, in3)):
        copies.append(
            pltpu.make_async_copy(
                part.at[pl.ds(0, SLOTS)],
                table.at[pl.ds(LEAVES + q * SLOTS, SLOTS)],
                sem.at[1 + q],
            )
        )
    for copy in copies:
        copy.start()

    def clear(c, _):
        total[c] = jnp.zeros((8, LEAF), f32)
        return 0

    lax.fori_loop(LEAVES, 2 * LEAVES + 8, clear, 0, unroll=8)
    row = iota((8, 128), 0)
    for code in range(27):
        step = (code % 3 - 1, code // 3 % 3 - 1, code // 9 - 1)
        value = jnp.zeros((8, 128), f32)
        for k in range(3):
            value = jnp.where(row == k + 1, float(step[k]), value)
        shifts[code] = value
    for copy in copies:
        copy.wait()

    def decode(group, k):
        code = list_ref[0, group * WIDTH + k]
        value = jnp.maximum(code - 1, 0)
        return value & 511, (value >> 9) & 511, value >> 18, code > 0

    def shift_of(code):
        half = shifts[code]
        return jnp.concatenate([half, half], 1)

    def spaced(group, k, rows):
        r, c, code, _ = decode(group, k)
        points_r, _ = load_points(table[r])
        points_c, _ = load_points(table[c])
        return squares((points_r + shift_of(code))[:, :rows], points_c)

    def keep(k, rows, value):
        inverse = lax.rsqrt(value)
        held[k][0:rows, :] = (inverse * inverse * inverse).astype(bf16)

    def products(group, k, rows):
        r, c, code, live = decode(group, k)
        points_r, weight_r = load_points(table[r])
        points_c, weight_c = load_points(table[c])
        shift = shift_of(code)
        cube = held[k][0:rows, :]
        side_r = sources((points_r + shift)[:, :rows], weight_r[:, :rows])
        to_c = fold(dot_nn(side_r, cube))
        to_r = fold(dot_nt(sources(points_c - shift, weight_c), cube))
        return jnp.where(live, r, 2 * LEAVES), jnp.where(live, c, 2 * LEAVES), to_r, to_c

    def settle(done, rows):
        for r, c, to_r, to_c in done:
            total[r, :, 0:rows] = total[r, :, 0:rows] + to_r
            total[c] = total[c] + to_c

    for n, rows in enumerate(CLASSES):
        first = list_ref[1, n]
        end = list_ref[1, n + 1]

        @pl.when(end > first)
        def _(first=first, end=end, rows=rows):
            for k in range(WIDTH):
                keep(k, rows, spaced(first, k, rows))

            def advance(group, _):
                done = []
                for k in range(WIDTH):
                    done.append(products(group, k, rows))
                    keep(k, rows, spaced(group + 1, k, rows))
                settle(done, rows)
                return 0

            lax.fori_loop(first, end - 1, advance, 0)
            settle([products(end - 1, k, rows) for k in range(WIDTH)], rows)

    store = pltpu.make_async_copy(total.at[pl.ds(0, LEAVES)], out_ref, sem.at[6])
    store.start()
    for q in range(4):

        def finish_other(k, _, q=q):
            points, _ = load_points(table[LEAVES + q * SLOTS + k])
            pays[q][k] = finish(total[LEAVES + q * SLOTS + k], points)
            return 0

        lax.fori_loop(0, SLOTS, finish_other, 0, unroll=8)
        put_block(pays[q], backs_ref[q])
    store.wait()


def near_part(ordered, own, incoming, backs, self0):
    return pl.pallas_call(
        near_kernel,
        name="near_part",
        out_shape=[shaped(LEAVES, 8, LEAF)] + [shaped(PAY, 4, LEAF)] * 4,
        in_specs=[SM, HB, HB, HB, HB, HB, VM, HB],
        out_specs=[HB] + [VM] * 4,
        scratch_shapes=[
            pltpu.VMEM((2 * LEAVES, 4, LEAF), f32),
            pltpu.VMEM((2 * LEAVES + 8, 8, LEAF), f32),
            pltpu.VMEM((27, 8, 128), f32),
            pltpu.SemaphoreType.DMA((7,)),
        ] + [pltpu.VMEM((LEAF, LEAF), bf16)] * WIDTH,
        cost_estimate=pl.CostEstimate(
            flops=NEAR * 80_000_000, bytes_accessed=4_000_000, transcendentals=0
        ),
        compiler_params=pltpu.CompilerParams(**PARAMS),
    )(ordered, own, *incoming, backs, self0)


def sort_lists(code, group, width, out_ref):
    count = code.shape[1]
    hot = jnp.where(iota((8, count), 0) == group, 1.0, 0.0)
    earlier = jnp.where(iota((count, count), 0) < iota((count, count), 1), 1.0, 0.0).astype(bf16)
    before = dot_nn(hot.astype(bf16), earlier)
    members = jnp.sum(hot, 1, keepdims=True)
    lane = iota((1, SORTED), 1)
    place = jnp.zeros((1, count), f32)
    groups = jnp.zeros((1, 1), f32)
    ends = jnp.zeros((1, SORTED), f32)
    for n in range(len(CLASSES)):
        place = place + hot[n : n + 1] * (before[n : n + 1] + groups * width)
        groups = groups + jnp.floor((members[n : n + 1] + (width - 1)) * (1.0 / width))
        ends = jnp.where(lane == n + 1, groups, ends)
    place = jnp.where(group >= 0, place, -1.0).astype(jnp.int32)
    ordered = pick(jnp.broadcast_to(code, (8, count)), onehot_rows(SORTED, place), True)
    out_ref[0:1, :] = ordered[0:1].astype(jnp.int32)
    out_ref[1:2, :] = ends.astype(jnp.int32)


def derivatives(x, y, z):
    square = x * x + y * y + z * z
    inverse = 1.0 / jnp.sqrt(square)
    inverse2 = inverse * inverse
    table = {(0, (0, 0, 0)): inverse}
    for m in range(1, 5):
        table[(m, (0, 0, 0))] = table[(m - 1, (0, 0, 0))] * inverse2 * float(-(2 * m - 1))
    place = (x, y, z)

    def entry(m, alpha):
        key = (m, alpha)
        if key not in table:
            axis = [k for k in range(3) if alpha[k]][0]
            lower = tuple(alpha[k] - (k == axis) for k in range(3))
            value = place[axis] * entry(m + 1, lower)
            if lower[axis]:
                lowest = tuple(lower[k] - (k == axis) for k in range(3))
                value = value + float(lower[axis]) * entry(m + 1, lowest)
            table[key] = value
        return table[key]

    return {alpha: entry(0, alpha) for alpha in ALPHAS}


def mutual(a_ref, b_ref, to_a, to_b):
    def rows(n):
        return pl.ds(n * 8, 8)

    lift = a_ref[rows(38), :]
    live = a_ref[rows(39), :] > 0.5
    gap = [
        jnp.where(live, a_ref[rows(35 + k), :] - b_ref[rows(35 + k), :] - (lift if k == 2 else 0.0), 3.0)
        for k in range(3)
    ]
    made = derivatives(*gap)
    for beta in ALPHAS:
        sum_a = None
        sum_b = None
        for alpha in ALPHAS:
            if sum(alpha) + sum(beta) > 4:
                continue
            tensor = made[add(alpha, beta)]
            scale = 1.0 / afact(alpha)
            sign_a = -((-1.0) ** sum(alpha)) * scale
            sign_b = -((-1.0) ** sum(beta)) * scale
            term_a = b_ref[rows(AT[alpha]), :] * sign_a * tensor
            term_b = a_ref[rows(AT[alpha]), :] * sign_b * tensor
            sum_a = term_a if sum_a is None else sum_a + term_a
            sum_b = term_b if sum_b is None else sum_b + term_b
        to_a[rows(AT[beta]), :] = jnp.where(live, sum_a, 0.0)
        to_b[rows(AT[beta]), :] = jnp.where(live, sum_b, 0.0)


def far_kernel(
    image_ref, far_ref, parent_ref, near_ref, cells_ref, pcells_ref, in0, in1, in2, in3,
    leaf_ref, par_ref, backs_ref, ordered_ref, tails, table, left, right, to_a, to_b, total, sem,
):
    copies = []
    for q, part in enumerate((in0, in1, in2, in3)):
        copies.append(
            pltpu.make_async_copy(part.at[pl.ds(SLOTS, 5)], tails.at[q], sem.at[q])
        )
    for copy in copies:
        copy.start()
    table[:, 0:LEAVES] = cells_ref[...]
    table[:, LEAVES + 512 :] = pcells_ref[...]
    row = iota((40, 128), 0)
    to_a[...] = jnp.zeros_like(to_a)
    to_b[...] = jnp.zeros_like(to_b)
    left[...] = jnp.zeros_like(left)
    right[...] = jnp.zeros_like(right)
    for copy in copies:
        copy.wait()
    for q in range(4):
        block = get_block(lambda s, q=q: tails[q, s])
        block = block + jnp.where(
            row == 35, image_ref[q, 0], jnp.where(row == 36, image_ref[q, 1], 0.0)
        )
        table[:, LEAVES + q * 128 : LEAVES + q * 128 + 128] = block
    parts = jnp.concatenate([part.astype(f32) for part in split3(table[...])], 0).astype(bf16)
    total[...] = jnp.zeros_like(total)

    def gathered(hot, first, count):
        out = dot_nn(parts[:, first : first + count], hot)
        return out[0:40] + out[40:80] + out[80:120]

    def leaf_entry(ids):
        other = ids - LEAVES
        return jnp.where(ids < LEAVES, ids, LEAVES + other // SLOTS * 128 + other % SLOTS)

    def parent_entry(ids):
        other = ids - PARENTS
        return jnp.where(
            ids < PARENTS, LEAVES + 512 + ids, LEAVES + other // PSLOTS * 128 + SLOTS + other % PSLOTS
        )

    def hots(ids_a, ids_b, parents):
        if parents:
            return (
                onehot_rows(128, ids_a), LEAVES + 512, 128,
                onehot_rows(640, parent_entry(ids_b) - LEAVES), LEAVES, 640,
            )
        return (
            onehot_rows(LEAVES, ids_a), 0, LEAVES,
            onehot_rows(768, leaf_entry(ids_b)), 0, 768,
        )

    def load(ids_a, ids_b, lifts, g, parents):
        hot_a, first_a, count_a, hot_b, first_b, count_b = hots(ids_a, ids_b, parents)
        from_a = gathered(hot_a, first_a, count_a)
        from_b = gathered(hot_b, first_b, count_b)
        live = jnp.where(ids_b >= 0, 1.0, 0.0)
        from_a = jnp.where(row == 38, lifts.astype(f32) * float(CZ), from_a)
        from_a = jnp.where(row == 39, live, from_a)
        left[pl.ds(g, 40, stride=8), :] = from_a
        right[pl.ds(g, 40, stride=8), :] = from_b

    def store(ids_a, ids_b, g, parents):
        hot_a, first_a, count_a, hot_b, first_b, count_b = hots(ids_a, ids_b, parents)
        sum_a = pick(to_a[pl.ds(g, 40, stride=8), :], hot_a, True)
        sum_b = pick(to_b[pl.ds(g, 40, stride=8), :], hot_b, True)
        total[:, first_a : first_a + count_a] += sum_a
        total[:, first_b : first_b + count_b] += sum_b

    for g in range(FAR // 128):
        lanes = slice(g * 128, g * 128 + 128)
        load(far_ref[0, :, lanes], far_ref[1, :, lanes], far_ref[2, :, lanes], g, False)
    mutual(left, right, to_a, to_b)
    for g in range(FAR // 128):
        lanes = slice(g * 128, g * 128 + 128)
        store(far_ref[0, :, lanes], far_ref[1, :, lanes], g, False)
    ids_a, ids_b, lifts = [
        jnp.concatenate([parent_ref[k], jnp.full((1, 128 - PFAR), -(k == 1), jnp.int32)], 1)
        for k in range(3)
    ]
    load(ids_a, ids_b, lifts, 0, True)
    mutual(left, right, to_a, to_b)
    store(ids_a, ids_b, 0, True)

    ids_a, ids_b, lifts = near_ref[0], near_ref[1], near_ref[2]
    hot_a, _, _, hot_b, _, _ = hots(ids_a, ids_b, False)
    from_a = gathered(hot_a, 0, LEAVES)[35:39]
    from_b = gathered(hot_b, 0, 768)[35:39]
    count_a, count_b = from_a[3:4], from_b[3:4]
    fewer = jnp.minimum(count_a, count_b)
    swap = count_b < count_a
    group = jnp.where(fewer <= 128.0, 0, jnp.where(fewer <= 192.0, 1, 2))
    group = jnp.where(ids_b >= 0, group, -1)
    moved = jnp.zeros((1, NEAR), f32)
    for k in range(3):
        apart = from_a[k : k + 1] - from_b[k : k + 1]
        if k == 2:
            apart = apart - lifts.astype(f32) * float(CZ)
        apart = jnp.where(swap, -apart, apart)
        moved = moved + (apart + 1.0) * float(3**k)
    rows = jnp.where(swap, ids_b, ids_a)
    columns = jnp.where(swap, ids_a, ids_b)
    code = 1.0 + rows.astype(f32) + columns.astype(f32) * 512.0 + moved * 262144.0
    sort_lists(jnp.where(ids_b >= 0, code, 0.0), group, WIDTH, ordered_ref)

    leaf_ref[...] = total[:, 0:LEAVES]
    par_ref[...] = total[:, LEAVES + 512 :]
    for q in range(4):
        backs_ref[q] = total[:, LEAVES + q * 128 : LEAVES + q * 128 + 128]


def far_part(image, far, parent, near, cells, pcells, incoming):
    return pl.pallas_call(
        far_kernel,
        name="far_part",
        out_shape=[
            shaped(40, LEAVES), shaped(40, 128), shaped(4, 40, 128),
            jax.ShapeDtypeStruct((2, SORTED), jnp.int32),
        ],
        in_specs=[SM, VM, VM, VM, VM, VM, HB, HB, HB, HB],
        out_specs=[VM] * 4,
        scratch_shapes=[
            pltpu.VMEM((4, 5, 4, LEAF), f32),
            pltpu.VMEM((40, TABLE), f32),
        ] + [pltpu.VMEM((320, 128), f32)] * 4 + [
            pltpu.VMEM((40, TABLE), f32),
            pltpu.SemaphoreType.DMA((4,)),
        ],
        compiler_params=pltpu.CompilerParams(**PARAMS),
    )(
        image, far.transpose(1, 0, 2), parent.transpose(1, 0, 2), near.transpose(1, 0, 2),
        cells, pcells, *incoming,
    )


def shift_terms(terms, offsets):
    for axis in range(3):
        powers = [None, offsets[axis]]
        for _ in range(3):
            powers.append(powers[-1] * offsets[axis])
        moved = {}
        for alpha in ALPHAS:
            total = terms[alpha]
            for k in range(1, 5 - sum(alpha)):
                upper = tuple(alpha[q] + k * (q == axis) for q in range(3))
                total = total + terms[upper] * powers[k] * (1.0 / FACT[k])
            moved[alpha] = total
        terms = moved
    return terms


def horner(get, degree, x, y, z):
    over_x = None
    for i in range(degree, -1, -1):
        over_y = None
        for j in range(degree - i, -1, -1):
            over_z = None
            for k in range(degree - i - j, -1, -1):
                value = get((i, j, k))
                over_z = value if over_z is None else over_z * z + value
            over_y = over_z if over_y is None else over_y * y + over_z
        over_x = over_y if over_x is None else over_x * x + over_y
    return over_x


def last_kernel(
    counts_ref, send_ref, sent_leaves, sent_parents, turned_ref, self_hbm, leaf_ref,
    par_ref, in0, in1, in2, in3, out_ref, slab_ref, terms_ref, field_ref, near_sum, sem,
):
    incoming = (in0, in1, in2, in3)
    lane128 = iota((1, 128), 1)
    fetch_all(((self_hbm.at[pl.ds(0, LEAVES)], near_sum),), sem)
    leaf = leaf_ref[...]
    par = par_ref[...]
    for q in range(4):
        block = get_block(lambda s, q=q: incoming[q][SLOTS + s])
        ids = id_row(sent_leaves, sent_parents, q)
        leaf_hot = onehot_rows(LEAVES, jnp.where(lane128 < SLOTS, ids, -1))
        parent_hot = onehot_rows(128, jnp.where(lane128 >= SLOTS, ids, -1))
        leaf = leaf + pick(block, leaf_hot, True)
        par = par + pick(block, parent_hot, True)

        def arrive(step, _, q=q):
            first = step * 8
            places = [send_ref[0, q * SLOTS + first + k] for k in range(8)]
            values = [near_sum[c] + incoming[q][first + k] for k, c in enumerate(places)]
            for c, value in zip(places, values):
                near_sum[c] = value
            return 0

        lax.fori_loop(0, SLOTS // 8, arrive, 0)
    lane_parent = (iota((128, LEAVES), 1) // CZ % CY // 2) * (CZ // 2) + iota(
        (128, LEAVES), 1
    ) % CZ // 2
    above = pick(par, jnp.where(lane_parent == iota((128, LEAVES), 0), 1.0, 0.0).astype(bf16))
    terms = {alpha: above[n : n + 1, :] for n, alpha in enumerate(ALPHAS)}
    terms = shift_terms(terms, parent_offsets())
    for n, alpha in enumerate(ALPHAS):
        terms_ref[n : n + 1, :] = leaf[n : n + 1, :] + terms[alpha]

    for half in range(2):
        lanes = slice(half * 128, half * 128 + 128)

        def term(alpha):
            return terms_ref[AT[alpha] : AT[alpha] + 1, lanes]

        def potential_at(alpha):
            return term(alpha) * (1.0 / afact(alpha))

        coefs = [{alpha: potential_at(alpha) for alpha in ALPHAS}]
        for axis in range(3):
            coefs.append(
                {
                    alpha: term(add(alpha, unit(axis))) * (-1.0 / afact(alpha))
                    for alpha in ALPHAS
                    if sum(alpha) <= 3
                }
            )

        def chunk(step, _):
            rows = pl.ds(pl.multiple_of(step * 32, 32), 32)
            x, y, z = [turned_ref[comp, rows, lanes] for comp in range(1, 4)]
            for comp in range(4):
                field_ref[comp, rows, lanes] = horner(
                    lambda alpha, comp=comp: coefs[comp][alpha], 3 if comp else 4, x, y, z
                )
            return 0

        lax.fori_loop(0, LEAF // 32, chunk, 0)

    for comp in range(4):
        turned = field_ref[comp].T
        for half in range(2):
            slab_ref[pl.ds(half * LEAVES * 8 + comp, LEAVES, stride=8), :] = turned[
                :, half * 128 : half * 128 + 128
            ]

    lane = iota((4, LEAF), 1)

    def write(c, _):
        value = jnp.concatenate(
            [
                slab_ref[pl.ds(pl.multiple_of(half * LEAVES * 8 + c * 8, 8), 8), :]
                for half in range(2)
            ],
            1,
        )[0:4] + near_sum[c]
        start = pl.multiple_of(c * LEAF, LEAF)
        out_ref[:, pl.ds(start, LEAF)] = jnp.where(lane < counts_ref[c], value, 0.0)
        return 0

    lax.fori_loop(0, LEAVES, write, 0, unroll=8)


def last(counts, send_leaves, send_parents, turned, near, leaf, par, arrived):
    return pl.pallas_call(
        last_kernel,
        name="last",
        out_shape=shaped(4, LEAVES * LEAF),
        in_specs=[SM, SM, VM, VM, VM, HB] + [VM] * 6,
        out_specs=VM,
        scratch_shapes=[
            pltpu.VMEM((LEAVES * 16, 128), f32),
            pltpu.VMEM((40, LEAVES), f32),
            pltpu.VMEM((4, LEAF, LEAVES), f32),
            pltpu.VMEM((LEAVES, 4, LEAF), f32),
            pltpu.SemaphoreType.DMA((1,)),
        ],
        compiler_params=pltpu.CompilerParams(**PARAMS),
    )(
        counts, send_leaves, send_leaves, send_parents, turned, near, leaf, par, *arrived
    )


def image_shift(slab_at, sub_at, slab_count, sub_count):
    rows_out = []
    for direction in range(4):
        reach_x = slab_at + slab_steps[direction]
        reach_y = sub_at + sub_steps[direction]
        jump_x = (reach_x - reach_x % slab_count) * CX
        jump_y = (reach_y - reach_y % sub_count) * CY
        rows_out.append(jnp.stack([jump_x, jump_y]))
    return jnp.stack(rows_out).astype(f32)


def moved_by(value, slab_step, sub_step, slab_count, sub_count):
    pairs = []
    for slab_at in range(slab_count):
        for sub_at in range(sub_count):
            target = (slab_at + slab_step) % slab_count * sub_count + (sub_at + sub_step) % sub_count
            pairs.append((slab_at * sub_count + sub_at, target))
    return lax.ppermute(value, ("slab", "sub"), pairs)


def on_device(
    positions, masses, leaf_counts, send_leaves, send_parents, near_pairs, far_pairs, parent_pairs
):
    slab_count = lax.axis_size("slab")
    sub_count = lax.axis_size("sub")
    slab_at = lax.axis_index("slab")
    sub_at = lax.axis_index("sub")
    at = jnp.stack([slab_at, sub_at]).astype(jnp.int32)
    own, cells, pcells, *outgoing, turned, leaf_order = front(
        at, leaf_counts, send_leaves, send_parents, positions, masses
    )
    incoming = [
        moved_by(outgoing[q], -slab_steps[q], -sub_steps[q], slab_count, sub_count)
        for q in range(4)
    ]
    image = image_shift(slab_at, sub_at, slab_count, sub_count)
    self0 = self_part(0, leaf_order, own)
    leaf, par, backs, ordered = far_part(
        image, far_pairs, parent_pairs, near_pairs, cells, pcells, incoming
    )
    near, *returning = near_part(ordered, own, incoming, backs, self0)
    arrived = [
        moved_by(returning[q], slab_steps[q], sub_steps[q], slab_count, sub_count)
        for q in range(4)
    ]
    near = self_part(1, leaf_order, own, near)
    return last(
        leaf_counts, send_leaves, send_parents, turned, near, leaf, par, arrived
    )


def solution(mesh):
    return jax.shard_map(
        on_device,
        mesh=mesh,
        in_specs=(
            P(None, ("slab", "sub")),
            P(("slab", "sub")),
            P(("slab", "sub")),
            P(("slab", "sub"), None),
            P(("slab", "sub"), None),
            P(("slab", "sub"), None, None),
            P(("slab", "sub"), None, None),
            P(("slab", "sub"), None, None),
        ),
        out_specs=P(None, ("slab", "sub")),
        check_vma=False,
    )
```

```python
import functools

import jax
import jax.numpy as jnp
from jax import lax
from jax.experimental import pallas as pl
from jax.experimental.pallas import tpu as pltpu
from jax.sharding import PartitionSpec as P

CX = 2
CY = 4
CZ = 32
LEAVES = 256
LEAF = 256
PARENTS = 32
SLOTS = 64
PSLOTS = 16
NEAR = 256
FAR = 1024
PFAR = 64
PAY = SLOTS + 5
SOFT = 0.0025
WIDTH = 8
SELF_WIDTH = 16
CLASSES = (128, 192, 256)
SORTED = 384
slab_steps = (1, 0, 1, 1)
sub_steps = (0, 1, 1, -1)
f32 = jnp.float32
bf16 = jnp.bfloat16

ALPHAS = [
    (i, j, d - i - j) for d in range(5) for i in range(d, -1, -1) for j in range(d - i, -1, -1)
]
AT = {a: n for n, a in enumerate(ALPHAS)}
FACT = (1.0, 1.0, 2.0, 6.0, 24.0)
TABLE = LEAVES + 4 * 128 + 128


def afact(alpha):
    return FACT[alpha[0]] * FACT[alpha[1]] * FACT[alpha[2]]


def add(a, b):
    return (a[0] + b[0], a[1] + b[1], a[2] + b[2])


def unit(axis):
    return tuple(1 if k == axis else 0 for k in range(3))


def split3(value):
    one = value.astype(bf16)
    rest = value - one.astype(f32)
    two = rest.astype(bf16)
    three = (rest - two.astype(f32)).astype(bf16)
    return one, two, three


def dot_nn(a, b):
    return lax.dot_general(a, b, (((1,), (0,)), ((), ())), preferred_element_type=f32)


def dot_nt(a, b):
    return lax.dot_general(a, b, (((1,), (1,)), ((), ())), preferred_element_type=f32)


def dot_tn(a, b):
    return lax.dot_general(a, b, (((0,), (0,)), ((), ())), preferred_element_type=f32)


def pick(values, onehot, transposed=False):
    parts = jnp.concatenate([part.astype(f32) for part in split3(values)], 0).astype(bf16)
    out = dot_nt(parts, onehot) if transposed else dot_nn(parts, onehot)
    rows = values.shape[0]
    return out[:rows] + out[rows : 2 * rows] + out[2 * rows :]


def iota(shape, dim):
    return lax.broadcasted_iota(jnp.int32, shape, dim)


def onehot_rows(count, ids):
    hit = iota((count, ids.shape[1]), 0) == ids
    return jnp.where(hit, 1.0, 0.0).astype(bf16)


def fetch_all(moves, sem):
    copies = [
        pltpu.make_async_copy(source, target, sem.at[n])
        for n, (source, target) in enumerate(moves)
    ]
    for copy in copies:
        copy.start()
    for copy in copies:
        copy.wait()


def id_row(sent_leaves, sent_parents, q):
    return jnp.concatenate(
        [
            sent_leaves[:, q * SLOTS : (q + 1) * SLOTS],
            sent_parents[:, q * PSLOTS : (q + 1) * PSLOTS],
            jnp.full((1, 128 - SLOTS - PSLOTS), -1, jnp.int32),
        ],
        1,
    )


def put_slab(slab_ref, c, slab):
    wide = jnp.concatenate([slab, jnp.zeros((4, LEAF), f32)], 0)
    for half in range(2):
        rows = pl.ds(pl.multiple_of(half * LEAVES * 8 + c * 8, 8), 8)
        slab_ref[rows, :] = wide[:, half * 128 : half * 128 + 128]


def get_rows(slab_ref, comp):
    return jnp.concatenate(
        [slab_ref[pl.ds(half * LEAVES * 8 + comp, LEAVES, stride=8), :] for half in range(2)], 1
    )


def monomials(x, y, z, w):
    made = {(0, 0, 0): w}
    for alpha in ALPHAS[1:]:
        for axis, value in ((2, z), (1, y), (0, x)):
            if alpha[axis]:
                lower = tuple(alpha[k] - (k == axis) for k in range(3))
                made[alpha] = made[lower] * value
                break
    return made


def shift_moments(moments, offsets):
    choose = ((1,), (1, 1), (1, 2, 1), (1, 3, 3, 1), (1, 4, 6, 4, 1))
    for axis in range(3):
        powers = [None, offsets[axis]]
        for _ in range(3):
            powers.append(powers[-1] * offsets[axis])
        moved = {}
        for alpha in ALPHAS:
            total = moments[alpha]
            for k in range(alpha[axis]):
                lower = tuple(k if q == axis else alpha[q] for q in range(3))
                total = total + moments[lower] * powers[alpha[axis] - k] * float(
                    choose[alpha[axis]][k]
                )
            moved[alpha] = total
        moments = moved
    return moments


def leaf_lanes():
    lane = iota((1, LEAVES), 1)
    return lane // (CY * CZ), lane // CZ % CY, lane % CZ


def parent_offsets():
    cell_x, cell_y, cell_z = leaf_lanes()
    return [(cell % 2).astype(f32) - 0.5 for cell in (cell_x, cell_y, cell_z)]


def front_kernel(
    at_ref, counts_hbm, row_hbm, send_hbm, parents_hbm, pos_hbm, mass_hbm,
    own_ref, cells_ref, pcells_ref, pay0, pay1, pay2, pay3, turned_ref, ordered_ref,
    slab_ref, pos_ref, mass_ref, counts_ref, send_ref, counts_row, sent_leaves, sent_parents, sem,
):
    pays = (pay0, pay1, pay2, pay3)
    pieces = CX * CY
    bodies = LEAVES * LEAF // pieces
    places = [
        pltpu.make_async_copy(
            pos_hbm.at[:, pl.ds(n * bodies, bodies)], pos_ref.at[:, pl.ds(n * bodies, bodies)],
            sem.at[6 + n],
        )
        for n in range(pieces)
    ]
    smaller = [
        pltpu.make_async_copy(source, target, sem.at[n])
        for n, (source, target) in enumerate(
            (
                (counts_hbm, counts_ref), (mass_hbm, mass_ref), (send_hbm, send_ref),
                (row_hbm, counts_row), (send_hbm, sent_leaves), (parents_hbm, sent_parents),
            )
        )
    ]
    for copy in smaller[:2] + places + smaller[2:]:
        copy.start()
    for copy in smaller:
        copy.wait()
    base_x = at_ref[0] * CX
    base_y = at_ref[1] * CY
    row4 = iota((4, LEAF), 0)
    lane = iota((1, LEAF), 1)
    batch = 8

    for x in range(CX):
        for y in range(CY):
            centre = jnp.where(row4 == 1, (base_x + x).astype(f32) + 0.5, 0.0)
            centre = jnp.where(row4 == 2, (base_y + y).astype(f32) + 0.5, centre)
            places[x * CY + y].wait()

            def some_leaves(step, _, x=x, y=y, centre=centre):
                low = step * batch
                first = (x * CY + y) * CZ + low
                from_z = jnp.where(row4 == 3, low.astype(f32) + 0.5, centre)
                for k in range(batch):
                    c = first + k
                    start = pl.multiple_of(c * LEAF, LEAF)
                    place = pos_ref[:, pl.ds(start, LEAF)]
                    mass = jnp.concatenate(
                        [mass_ref[pl.ds(2 * c, 1), :], mass_ref[pl.ds(2 * c + 1, 1), :]], 1
                    )
                    weight = jnp.where(lane < counts_ref[c], mass, 0.0)
                    slab = jnp.concatenate([weight, place], 0) - (
                        from_z + jnp.where(row4 == 3, float(k), 0.0)
                    )
                    own_ref[c] = slab
                    put_slab(slab_ref, c, slab)
                return 0

            lax.fori_loop(0, CZ // batch, some_leaves, 0)

    for comp in range(4):
        turned_ref[comp] = get_rows(slab_ref, comp).T

    for half in range(2):
        lanes = slice(half * 128, half * 128 + 128)

        def chunk(step, totals):
            rows = pl.ds(pl.multiple_of(step * 8, 8), 8)
            w, x, y, z = [turned_ref[comp, rows, lanes] for comp in range(4)]
            made = monomials(x, y, z, w)
            return tuple(total + made[alpha] for total, alpha in zip(totals, ALPHAS))

        totals = lax.fori_loop(
            0, LEAF // 8, chunk, tuple(jnp.zeros((8, 128), f32) for _ in ALPHAS), unroll=2
        )
        for n, total in enumerate(totals):
            cells_ref[n : n + 1, lanes] = jnp.sum(total, 0, keepdims=True)

    cell_x, cell_y, cell_z = leaf_lanes()
    cells_ref[35:36, :] = (base_x + cell_x).astype(f32) + 0.5
    cells_ref[36:37, :] = (base_y + cell_y).astype(f32) + 0.5
    cells_ref[37:38, :] = cell_z.astype(f32) + 0.5
    cells_ref[38:39, :] = counts_row[...].astype(f32)
    cells_ref[39:40, :] = jnp.zeros((1, LEAVES), f32)

    moments = {alpha: cells_ref[n : n + 1, :] for n, alpha in enumerate(ALPHAS)}
    moved = shift_moments(moments, parent_offsets())
    moved = jnp.concatenate(
        [moved[alpha] for alpha in ALPHAS] + [jnp.zeros((5, LEAVES), f32)], 0
    )
    parent_of = (iota((LEAVES, 128), 0) // CZ % CY // 2) * (CZ // 2) + iota(
        (LEAVES, 128), 0
    ) % CZ // 2
    belongs = jnp.where(parent_of == iota((LEAVES, 128), 1), 1.0, 0.0).astype(bf16)
    pcells = pick(moved, belongs)
    plane = iota((40, 128), 1)
    prow = iota((40, 128), 0)
    pcells = jnp.where(prow == 35, (base_x + 1).astype(f32), pcells)
    pcells = jnp.where(
        prow == 36, (base_y + 2 * (plane // (CZ // 2))).astype(f32) + 1.0, pcells
    )
    pcells = jnp.where(prow == 37, (2 * (plane % (CZ // 2))).astype(f32) + 1.0, pcells)
    pcells_ref[...] = pcells

    lane128 = iota((1, 128), 1)
    for q in range(4):
        pay = pays[q]

        def copy_leaf(k, _, pay=pay, q=q):
            pay[k] = own_ref[send_ref[0, q * SLOTS + k]]
            return 0

        lax.fori_loop(0, SLOTS, copy_leaf, 0, unroll=8)
        ids = id_row(sent_leaves, sent_parents, q)
        leaf_hot = onehot_rows(LEAVES, jnp.where(lane128 < SLOTS, ids, -1))
        parent_hot = onehot_rows(128, jnp.where(lane128 >= SLOTS, ids, -1))
        block = pick(cells_ref[...], leaf_hot) + pick(pcells, parent_hot)
        put_block(pay, block)

    counts = counts_row[...]
    group = jnp.where(counts <= 128, 0, jnp.where(counts <= 192, 1, 2))
    sort_lists(iota((1, LEAVES), 1).astype(f32) + 1.0, group, SELF_WIDTH, ordered_ref)


def put_block(pay, block):
    for s in range(5):
        pay[SLOTS + s, :, 0:128] = block[4 * s : 4 * s + 4]
        pay[SLOTS + s, :, 128:256] = block[20 + 4 * s : 24 + 4 * s]


def get_block(tail):
    return jnp.concatenate(
        [tail(s)[:, 0:128] for s in range(5)] + [tail(s)[:, 128:256] for s in range(5)], 0
    )


VM = pl.BlockSpec(memory_space=pltpu.VMEM)
SM = pl.BlockSpec(memory_space=pltpu.SMEM)
HB = pl.BlockSpec(memory_space=pl.ANY)
HBM = pl.BlockSpec(memory_space=pltpu.MemorySpace.HBM)
PARAMS = dict(vmem_limit_bytes=24 * 1024 * 1024)


def in_hbm(value):
    return pltpu.with_memory_space_constraint(value, pltpu.MemorySpace.HBM)


def shaped(*shape):
    return jax.ShapeDtypeStruct(shape, f32)


def front(at, counts, send_leaves, send_parents, positions, masses):
    return pl.pallas_call(
        front_kernel,
        name="front",
        out_shape=[
            shaped(LEAVES, 4, LEAF), shaped(40, LEAVES), shaped(40, 128),
        ] + [shaped(PAY, 4, LEAF)] * 4 + [
            shaped(4, LEAF, LEAVES), jax.ShapeDtypeStruct((2, SORTED), jnp.int32),
        ],
        in_specs=[SM] + [HBM] * 6,
        out_specs=[VM] * 9,
        scratch_shapes=[
            pltpu.VMEM((LEAVES * 16, 128), f32),
            pltpu.VMEM((3, LEAVES * LEAF), f32),
            pltpu.VMEM((LEAVES * 2, 128), f32),
            pltpu.SMEM((LEAVES,), jnp.int32),
            pltpu.SMEM((1, 4 * SLOTS), jnp.int32),
            pltpu.VMEM((1, LEAVES), jnp.int32),
            pltpu.VMEM((1, 4 * SLOTS), jnp.int32),
            pltpu.VMEM((1, 4 * PSLOTS), jnp.int32),
            pltpu.SemaphoreType.DMA((6 + CX * CY,)),
        ],
        compiler_params=pltpu.CompilerParams(**PARAMS),
    )(
        at,
        *map(
            in_hbm,
            (
                counts, counts.reshape(1, LEAVES), send_leaves, send_parents, positions,
                masses.reshape(-1, 128),
            ),
        ),
    )


def slab8(slab):
    return jnp.concatenate([slab, jnp.zeros((4, LEAF), f32)], 0)


def b_form(points):
    row = iota(points.shape, 0)
    square = jnp.sum(jnp.where(row == 0, 0.0, points * points), 0, keepdims=True)
    return jnp.where(row == 4, square, points)


def a_form(points):
    row = iota(points.shape, 0)
    square = jnp.sum(jnp.where(row == 0, 0.0, points * points), 0, keepdims=True)
    value = jnp.where(row == 0, square + SOFT, -2.0 * points)
    return jnp.where(row == 4, 1.0, value)


def widen(value):
    one = value.astype(bf16).astype(f32)
    rest = value - one
    two = rest.astype(bf16).astype(f32)
    return one, two, rest - two


def square_blocks(a_value, b_value):
    a1, a2, a3 = widen(a_value)
    b1, b2, b3 = widen(b_value)
    left = jnp.concatenate([a1, a1, a2, a2, a1, a3], 0).astype(bf16)
    right = jnp.concatenate([b1, b2, b1, b2, b3, b1], 0).astype(bf16)
    return dot_tn(left, right)


def squares(a_points, b_points):
    return square_blocks(a_form(a_points), b_form(b_points))


def weighted(formed, weight):
    parts = widen(formed * weight)
    return jnp.concatenate(parts + (jnp.zeros_like(parts[0]),), 0).astype(bf16)


def sources(points, weight):
    return weighted(b_form(points), weight)


def fold(out):
    total = out[0:8]
    for first in range(8, out.shape[0] // 8 * 8, 8):
        total = total + out[first : first + 8]
    return total


def finish(total, points):
    row = iota(points.shape, 0)
    field = total - points * total[0:1]
    sign = jnp.where(row == 0, -SOFT, jnp.where(row == 4, -1.0, 1.0))
    terms = jnp.where(row == 4, total, points * (field + total)) * sign
    return jnp.where(row == 0, jnp.sum(terms, 0, keepdims=True), field)[0:4]


def load_points(slab):
    wide = slab8(slab)
    row = iota((8, LEAF), 0)
    return jnp.where(row == 0, 1.0, wide), slab[0:1]


def self_kernel(part, list_ref, own_hbm, *refs):
    if part:
        before_hbm, out_ref, own_ref, before_ref, sem = refs
        moves = ((own_hbm, own_ref), (before_hbm, before_ref))
    else:
        out_ref, own_ref, sem = refs
        moves = ((own_hbm, own_ref),)
    copies = [
        pltpu.make_async_copy(source, target, sem.at[n])
        for n, (source, target) in enumerate(moves)
    ]
    for copy in copies:
        copy.start()
    if not part:

        def begin(c, _):
            out_ref[c] = jnp.zeros((8, LEAF), f32)
            return 0

        lax.fori_loop(0, LEAVES, begin, 0, unroll=8)
    for copy in copies:
        copy.wait()

    def place_of(step, k):
        code = list_ref[0, step * SELF_WIDTH + k]
        leaf = jnp.maximum(code - 1, 0)
        return leaf, jnp.where(code > 0, leaf, LEAVES)

    def some_leaves(step, rows, lanes):
        places = [place_of(step, k) for k in range(SELF_WIDTH)]
        loaded = []
        for leaf, _ in places:
            points, weight = load_points(own_ref[leaf])
            loaded.append((points[:, :rows], weight[:, :rows], points[:, :lanes]))
        spaced = [squares(left, right) for left, _, right in loaded]
        apart = jnp.where(iota((rows, lanes), 0) == iota((rows, lanes), 1), 0.0, 1.0)
        cubes = []
        for value in spaced:
            inverse = lax.rsqrt(value) * apart
            cubes.append(inverse * inverse * inverse)
        high = [cube.astype(bf16) for cube in cubes]
        done = []
        for cube, top, (left, weight, right), (leaf, _) in zip(cubes, high, loaded, places):
            low = (cube - top.astype(f32)).astype(bf16)
            side = sources(left, weight)
            value = fold(dot_nn(side, top)) + fold(dot_nn(side[0:16], low))
            if part:
                value = finish(value + before_ref[leaf, :, 0:lanes], right)
            done.append(value)
        for (_, place), value in zip(places, done):
            out_ref[place, :, 0:lanes] = value

    def finish_some(step):
        places = [place_of(step, k) for k in range(SELF_WIDTH)]
        done = [finish(before_ref[leaf], load_points(own_ref[leaf])[0]) for leaf, _ in places]
        for (_, place), value in zip(places, done):
            out_ref[place] = value

    for n, rows in enumerate(CLASSES):
        first = list_ref[1, n]
        end = list_ref[1, n + 1]
        middle = (first + end + n % 2) >> 1
        lanes = 128 if rows == 128 else LEAF

        def body(step, _, rows=rows, lanes=lanes):
            some_leaves(step, rows, lanes)
            return 0

        lax.fori_loop(middle if part else first, end if part else middle, body, 0)
        if part:

            def rest(step, _):
                finish_some(step)
                return 0

            lax.fori_loop(first, middle, rest, 0)


def self_part(part, ordered, own, *before):
    return pl.pallas_call(
        functools.partial(self_kernel, part),
        name="self_part",
        out_shape=shaped(LEAVES + 8, 4 if part else 8, LEAF),
        in_specs=[SM, HB] + [HB] * part,
        out_specs=VM,
        scratch_shapes=[pltpu.VMEM((LEAVES, 4, LEAF), f32)]
        + [pltpu.VMEM((LEAVES, 8, LEAF), f32)] * part
        + [pltpu.SemaphoreType.DMA((2,))],
        cost_estimate=pl.CostEstimate(
            flops=LEAVES * 20_000_000, bytes_accessed=LEAVES * 8192, transcendentals=0
        ),
        compiler_params=pltpu.CompilerParams(**PARAMS),
    )(ordered, own, *before)


def near_kernel(
    list_ref, own_ref, in0, in1, in2, in3, backs_ref, self_ref,
    out_ref, pay0, pay1, pay2, pay3, table, total, shifts, formed_r, kept_c, sem, *held,
):
    pays = (pay0, pay1, pay2, pay3)
    copies = [
        pltpu.make_async_copy(own_ref, table.at[pl.ds(0, LEAVES)], sem.at[0]),
        pltpu.make_async_copy(self_ref.at[pl.ds(0, LEAVES)], total.at[pl.ds(0, LEAVES)], sem.at[5]),
    ]
    for q, part in enumerate((in0, in1, in2, in3)):
        copies.append(
            pltpu.make_async_copy(
                part.at[pl.ds(0, SLOTS)],
                table.at[pl.ds(LEAVES + q * SLOTS, SLOTS)],
                sem.at[1 + q],
            )
        )
    for copy in copies:
        copy.start()

    def clear(c, _):
        total[c] = jnp.zeros((8, LEAF), f32)
        return 0

    lax.fori_loop(LEAVES, 2 * LEAVES + 8, clear, 0, unroll=8)
    row = iota((8, 128), 0)
    for code in range(27):
        step = (code % 3 - 1, code // 3 % 3 - 1, code // 9 - 1)
        value = jnp.zeros((8, 128), f32)
        for k in range(3):
            value = jnp.where(row == k + 1, float(step[k]), value)
        shifts[code] = value
    for copy in copies:
        copy.wait()

    def decode(group, k):
        code = list_ref[0, group * WIDTH + k]
        value = jnp.maximum(code - 1, 0)
        return value & 511, (value >> 9) & 511, value >> 18, code > 0

    def shift_of(code):
        half = shifts[code]
        return jnp.concatenate([half, half], 1)

    def spaced(group, k, rows):
        r, c, code, _ = decode(group, k)
        points_r, _ = load_points(table[r])
        points_c, _ = load_points(table[c])
        points_r = (points_r + shift_of(code))[:, :rows]
        formed_r[k, :, 0:rows] = b_form(points_r)
        kept_c[k] = points_c
        return squares(points_r, points_c)

    def keep(k, rows, value):
        inverse = lax.rsqrt(value)
        held[k][0:rows, :] = (inverse * inverse * inverse).astype(bf16)

    def products(group, k, rows):
        r, c, code, live = decode(group, k)
        cube = held[k][0:rows, :]
        side_r = weighted(formed_r[k, :, 0:rows], table[r, 0:1, 0:rows])
        to_c = fold(dot_nn(side_r, cube))
        side_c = sources(kept_c[k] - shift_of(code), table[c, 0:1, :])
        to_r = fold(dot_nt(side_c, cube))
        return jnp.where(live, r, 2 * LEAVES), jnp.where(live, c, 2 * LEAVES), to_r, to_c

    def settle(done, rows):
        for r, c, to_r, to_c in done:
            total[r, :, 0:rows] = total[r, :, 0:rows] + to_r
            total[c] = total[c] + to_c

    for n, rows in enumerate(CLASSES):
        first = list_ref[1, n]
        end = list_ref[1, n + 1]

        @pl.when(end > first)
        def _(first=first, end=end, rows=rows):
            for k in range(WIDTH):
                keep(k, rows, spaced(first, k, rows))

            def advance(group, _):
                done = []
                for k in range(WIDTH):
                    done.append(products(group, k, rows))
                    keep(k, rows, spaced(group + 1, k, rows))
                settle(done, rows)
                return 0

            lax.fori_loop(first, end - 1, advance, 0)
            settle([products(end - 1, k, rows) for k in range(WIDTH)], rows)

    store = pltpu.make_async_copy(total.at[pl.ds(0, LEAVES)], out_ref, sem.at[6])
    store.start()
    for q in range(4):

        def finish_other(k, _, q=q):
            points, _ = load_points(table[LEAVES + q * SLOTS + k])
            pays[q][k] = finish(total[LEAVES + q * SLOTS + k], points)
            return 0

        lax.fori_loop(0, SLOTS, finish_other, 0, unroll=8)
        put_block(pays[q], backs_ref[q])
    store.wait()


def near_part(ordered, own, incoming, backs, self0):
    return pl.pallas_call(
        near_kernel,
        name="near_part",
        out_shape=[shaped(LEAVES, 8, LEAF)] + [shaped(PAY, 4, LEAF)] * 4,
        in_specs=[SM, HB, HB, HB, HB, HB, VM, HB],
        out_specs=[HB] + [VM] * 4,
        scratch_shapes=[
            pltpu.VMEM((2 * LEAVES, 4, LEAF), f32),
            pltpu.VMEM((2 * LEAVES + 8, 8, LEAF), f32),
            pltpu.VMEM((27, 8, 128), f32),
            pltpu.VMEM((WIDTH, 8, LEAF), f32),
            pltpu.VMEM((WIDTH, 8, LEAF), f32),
            pltpu.SemaphoreType.DMA((7,)),
        ] + [pltpu.VMEM((LEAF, LEAF), bf16)] * WIDTH,
        cost_estimate=pl.CostEstimate(
            flops=NEAR * 80_000_000, bytes_accessed=4_000_000, transcendentals=0
        ),
        compiler_params=pltpu.CompilerParams(**PARAMS),
    )(ordered, own, *incoming, backs, self0)


def sort_lists(code, group, width, out_ref):
    count = code.shape[1]
    hot = jnp.where(iota((8, count), 0) == group, 1.0, 0.0)
    earlier = jnp.where(iota((count, count), 0) < iota((count, count), 1), 1.0, 0.0).astype(bf16)
    before = dot_nn(hot.astype(bf16), earlier)
    members = jnp.sum(hot, 1, keepdims=True)
    lane = iota((1, SORTED), 1)
    place = jnp.zeros((1, count), f32)
    groups = jnp.zeros((1, 1), f32)
    ends = jnp.zeros((1, SORTED), f32)
    for n in range(len(CLASSES)):
        place = place + hot[n : n + 1] * (before[n : n + 1] + groups * width)
        groups = groups + jnp.floor((members[n : n + 1] + (width - 1)) * (1.0 / width))
        ends = jnp.where(lane == n + 1, groups, ends)
    place = jnp.where(group >= 0, place, -1.0).astype(jnp.int32)
    ordered = pick(jnp.broadcast_to(code, (8, count)), onehot_rows(SORTED, place), True)
    out_ref[0:1, :] = ordered[0:1].astype(jnp.int32)
    out_ref[1:2, :] = ends.astype(jnp.int32)


def derivatives(x, y, z):
    square = x * x + y * y + z * z
    inverse = 1.0 / jnp.sqrt(square)
    inverse2 = inverse * inverse
    table = {(0, (0, 0, 0)): inverse}
    for m in range(1, 5):
        table[(m, (0, 0, 0))] = table[(m - 1, (0, 0, 0))] * inverse2 * float(-(2 * m - 1))
    place = (x, y, z)

    def entry(m, alpha):
        key = (m, alpha)
        if key not in table:
            axis = [k for k in range(3) if alpha[k]][0]
            lower = tuple(alpha[k] - (k == axis) for k in range(3))
            value = place[axis] * entry(m + 1, lower)
            if lower[axis]:
                lowest = tuple(lower[k] - (k == axis) for k in range(3))
                value = value + float(lower[axis]) * entry(m + 1, lowest)
            table[key] = value
        return table[key]

    return {alpha: entry(0, alpha) for alpha in ALPHAS}


def mutual(a_ref, b_ref, to_a, to_b):
    def rows(n):
        return pl.ds(n * 8, 8)

    lift = a_ref[rows(38), :]
    live = a_ref[rows(39), :] > 0.5
    gap = [
        jnp.where(live, a_ref[rows(35 + k), :] - b_ref[rows(35 + k), :] - (lift if k == 2 else 0.0), 3.0)
        for k in range(3)
    ]
    made = derivatives(*gap)
    for beta in ALPHAS:
        sum_a = None
        sum_b = None
        for alpha in ALPHAS:
            if sum(alpha) + sum(beta) > 4:
                continue
            tensor = made[add(alpha, beta)]
            scale = 1.0 / afact(alpha)
            sign_a = -((-1.0) ** sum(alpha)) * scale
            sign_b = -((-1.0) ** sum(beta)) * scale
            term_a = b_ref[rows(AT[alpha]), :] * sign_a * tensor
            term_b = a_ref[rows(AT[alpha]), :] * sign_b * tensor
            sum_a = term_a if sum_a is None else sum_a + term_a
            sum_b = term_b if sum_b is None else sum_b + term_b
        to_a[rows(AT[beta]), :] = jnp.where(live, sum_a, 0.0)
        to_b[rows(AT[beta]), :] = jnp.where(live, sum_b, 0.0)


def far_kernel(
    image_ref, far_ref, parent_ref, near_ref, cells_ref, pcells_ref, in0, in1, in2, in3,
    leaf_ref, par_ref, backs_ref, ordered_ref, tails, table, left, right, to_a, to_b, total, sem,
):
    copies = []
    for q, part in enumerate((in0, in1, in2, in3)):
        copies.append(
            pltpu.make_async_copy(part.at[pl.ds(SLOTS, 5)], tails.at[q], sem.at[q])
        )
    for copy in copies:
        copy.start()
    table[:, 0:LEAVES] = cells_ref[...]
    table[:, LEAVES + 512 :] = pcells_ref[...]
    row = iota((40, 128), 0)
    to_a[...] = jnp.zeros_like(to_a)
    to_b[...] = jnp.zeros_like(to_b)
    left[...] = jnp.zeros_like(left)
    right[...] = jnp.zeros_like(right)
    for copy in copies:
        copy.wait()
    for q in range(4):
        block = get_block(lambda s, q=q: tails[q, s])
        block = block + jnp.where(
            row == 35, image_ref[q, 0], jnp.where(row == 36, image_ref[q, 1], 0.0)
        )
        table[:, LEAVES + q * 128 : LEAVES + q * 128 + 128] = block
    parts = jnp.concatenate([part.astype(f32) for part in split3(table[...])], 0).astype(bf16)
    total[...] = jnp.zeros_like(total)

    def gathered(hot, first, count):
        out = dot_nn(parts[:, first : first + count], hot)
        return out[0:40] + out[40:80] + out[80:120]

    def leaf_entry(ids):
        other = ids - LEAVES
        return jnp.where(ids < LEAVES, ids, LEAVES + other // SLOTS * 128 + other % SLOTS)

    def parent_entry(ids):
        other = ids - PARENTS
        return jnp.where(
            ids < PARENTS, LEAVES + 512 + ids, LEAVES + other // PSLOTS * 128 + SLOTS + other % PSLOTS
        )

    def hots(ids_a, ids_b, parents):
        if parents:
            return (
                onehot_rows(128, ids_a), LEAVES + 512, 128,
                onehot_rows(640, parent_entry(ids_b) - LEAVES), LEAVES, 640,
            )
        return (
            onehot_rows(LEAVES, ids_a), 0, LEAVES,
            onehot_rows(768, leaf_entry(ids_b)), 0, 768,
        )

    def load(ids_a, ids_b, lifts, g, parents):
        hot_a, first_a, count_a, hot_b, first_b, count_b = hots(ids_a, ids_b, parents)
        from_a = gathered(hot_a, first_a, count_a)
        from_b = gathered(hot_b, first_b, count_b)
        live = jnp.where(ids_b >= 0, 1.0, 0.0)
        from_a = jnp.where(row == 38, lifts.astype(f32) * float(CZ), from_a)
        from_a = jnp.where(row == 39, live, from_a)
        left[pl.ds(g, 40, stride=8), :] = from_a
        right[pl.ds(g, 40, stride=8), :] = from_b

    def store(ids_a, ids_b, g, parents):
        hot_a, first_a, count_a, hot_b, first_b, count_b = hots(ids_a, ids_b, parents)
        sum_a = pick(to_a[pl.ds(g, 40, stride=8), :], hot_a, True)
        sum_b = pick(to_b[pl.ds(g, 40, stride=8), :], hot_b, True)
        total[:, first_a : first_a + count_a] += sum_a
        total[:, first_b : first_b + count_b] += sum_b

    for g in range(FAR // 128):
        lanes = slice(g * 128, g * 128 + 128)
        load(far_ref[0, :, lanes], far_ref[1, :, lanes], far_ref[2, :, lanes], g, False)
    mutual(left, right, to_a, to_b)
    for g in range(FAR // 128):
        lanes = slice(g * 128, g * 128 + 128)
        store(far_ref[0, :, lanes], far_ref[1, :, lanes], g, False)
    ids_a, ids_b, lifts = [
        jnp.concatenate([parent_ref[k], jnp.full((1, 128 - PFAR), -(k == 1), jnp.int32)], 1)
        for k in range(3)
    ]
    load(ids_a, ids_b, lifts, 0, True)
    mutual(left, right, to_a, to_b)
    store(ids_a, ids_b, 0, True)

    ids_a, ids_b, lifts = near_ref[0], near_ref[1], near_ref[2]
    hot_a, _, _, hot_b, _, _ = hots(ids_a, ids_b, False)
    from_a = gathered(hot_a, 0, LEAVES)[35:39]
    from_b = gathered(hot_b, 0, 768)[35:39]
    count_a, count_b = from_a[3:4], from_b[3:4]
    fewer = jnp.minimum(count_a, count_b)
    swap = count_b < count_a
    group = jnp.where(fewer <= 128.0, 0, jnp.where(fewer <= 192.0, 1, 2))
    group = jnp.where(ids_b >= 0, group, -1)
    moved = jnp.zeros((1, NEAR), f32)
    for k in range(3):
        apart = from_a[k : k + 1] - from_b[k : k + 1]
        if k == 2:
            apart = apart - lifts.astype(f32) * float(CZ)
        apart = jnp.where(swap, -apart, apart)
        moved = moved + (apart + 1.0) * float(3**k)
    rows = jnp.where(swap, ids_b, ids_a)
    columns = jnp.where(swap, ids_a, ids_b)
    code = 1.0 + rows.astype(f32) + columns.astype(f32) * 512.0 + moved * 262144.0
    sort_lists(jnp.where(ids_b >= 0, code, 0.0), group, WIDTH, ordered_ref)

    leaf_ref[...] = total[:, 0:LEAVES]
    par_ref[...] = total[:, LEAVES + 512 :]
    for q in range(4):
        backs_ref[q] = total[:, LEAVES + q * 128 : LEAVES + q * 128 + 128]


def far_part(image, far, parent, near, cells, pcells, incoming):
    return pl.pallas_call(
        far_kernel,
        name="far_part",
        out_shape=[
            shaped(40, LEAVES), shaped(40, 128), shaped(4, 40, 128),
            jax.ShapeDtypeStruct((2, SORTED), jnp.int32),
        ],
        in_specs=[SM, VM, VM, VM, VM, VM, HB, HB, HB, HB],
        out_specs=[VM] * 4,
        scratch_shapes=[
            pltpu.VMEM((4, 5, 4, LEAF), f32),
            pltpu.VMEM((40, TABLE), f32),
        ] + [pltpu.VMEM((320, 128), f32)] * 4 + [
            pltpu.VMEM((40, TABLE), f32),
            pltpu.SemaphoreType.DMA((4,)),
        ],
        compiler_params=pltpu.CompilerParams(**PARAMS),
    )(
        image, far.transpose(1, 0, 2), parent.transpose(1, 0, 2), near.transpose(1, 0, 2),
        cells, pcells, *incoming,
    )


def shift_terms(terms, offsets):
    for axis in range(3):
        powers = [None, offsets[axis]]
        for _ in range(3):
            powers.append(powers[-1] * offsets[axis])
        moved = {}
        for alpha in ALPHAS:
            total = terms[alpha]
            for k in range(1, 5 - sum(alpha)):
                upper = tuple(alpha[q] + k * (q == axis) for q in range(3))
                total = total + terms[upper] * powers[k] * (1.0 / FACT[k])
            moved[alpha] = total
        terms = moved
    return terms


def horner(coefs, x):
    value = coefs[-1]
    for coef in reversed(coefs[:-1]):
        value = value * x + coef
    return value


def horner_both(coefs, x):
    value, slope = coefs[-1], None
    for coef in reversed(coefs[:-1]):
        slope = value if slope is None else slope * x + value
        value = value * x + coef
    return value, slope


def polynomial(get, x, y, z):
    over_y, over_dy, over_dz = [], [], []
    for i in range(5):
        over_z = [
            horner_both([get((i, j, k)) for k in range(5 - i - j)], z) for j in range(5 - i)
        ]
        value, slope = horner_both([pair[0] for pair in over_z], y)
        over_y.append(value)
        if i < 4:
            over_dy.append(slope)
            over_dz.append(horner([pair[1] for pair in over_z[:-1]], y))
    value, slope = horner_both(over_y, x)
    return value, slope, horner(over_dy, x), horner(over_dz, x)


def last_kernel(
    counts_ref, send_ref, sent_leaves, sent_parents, turned_ref, self_hbm, leaf_ref,
    par_ref, in0, in1, in2, in3, out_ref, slab_ref, terms_ref, field_ref, near_sum, sem,
):
    incoming = (in0, in1, in2, in3)
    lane128 = iota((1, 128), 1)
    fetch_all(((self_hbm.at[pl.ds(0, LEAVES)], near_sum),), sem)
    leaf = leaf_ref[...]
    par = par_ref[...]
    for q in range(4):
        block = get_block(lambda s, q=q: incoming[q][SLOTS + s])
        ids = id_row(sent_leaves, sent_parents, q)
        leaf_hot = onehot_rows(LEAVES, jnp.where(lane128 < SLOTS, ids, -1))
        parent_hot = onehot_rows(128, jnp.where(lane128 >= SLOTS, ids, -1))
        leaf = leaf + pick(block, leaf_hot, True)
        par = par + pick(block, parent_hot, True)

        def arrive(step, _, q=q):
            first = step * 8
            places = [send_ref[0, q * SLOTS + first + k] for k in range(8)]
            values = [near_sum[c] + incoming[q][first + k] for k, c in enumerate(places)]
            for c, value in zip(places, values):
                near_sum[c] = value
            return 0

        lax.fori_loop(0, SLOTS // 8, arrive, 0)
    lane_parent = (iota((128, LEAVES), 1) // CZ % CY // 2) * (CZ // 2) + iota(
        (128, LEAVES), 1
    ) % CZ // 2
    above = pick(par, jnp.where(lane_parent == iota((128, LEAVES), 0), 1.0, 0.0).astype(bf16))
    terms = {alpha: above[n : n + 1, :] for n, alpha in enumerate(ALPHAS)}
    terms = shift_terms(terms, parent_offsets())
    for n, alpha in enumerate(ALPHAS):
        terms_ref[n : n + 1, :] = leaf[n : n + 1, :] + terms[alpha]

    for half in range(2):
        lanes = slice(half * 128, half * 128 + 128)

        def term(alpha):
            return terms_ref[AT[alpha] : AT[alpha] + 1, lanes]

        coefs = {alpha: term(alpha) * (1.0 / afact(alpha)) for alpha in ALPHAS}

        def chunk(step, _, coefs=coefs, lanes=lanes):
            rows = pl.ds(pl.multiple_of(step * 32, 32), 32)
            x, y, z = [turned_ref[comp, rows, lanes] for comp in range(1, 4)]
            value, *slopes = polynomial(lambda alpha: coefs[alpha], x, y, z)
            field_ref[0, rows, lanes] = value
            for comp, slope in enumerate(slopes):
                field_ref[comp + 1, rows, lanes] = -slope
            return 0

        lax.fori_loop(0, LEAF // 32, chunk, 0)

    for comp in range(4):
        turned = field_ref[comp].T
        for half in range(2):
            slab_ref[pl.ds(half * LEAVES * 8 + comp, LEAVES, stride=8), :] = turned[
                :, half * 128 : half * 128 + 128
            ]

    lane = iota((4, LEAF), 1)

    def write(c, _):
        value = jnp.concatenate(
            [
                slab_ref[pl.ds(pl.multiple_of(half * LEAVES * 8 + c * 8, 8), 8), :]
                for half in range(2)
            ],
            1,
        )[0:4] + near_sum[c]
        start = pl.multiple_of(c * LEAF, LEAF)
        out_ref[:, pl.ds(start, LEAF)] = jnp.where(lane < counts_ref[c], value, 0.0)
        return 0

    lax.fori_loop(0, LEAVES, write, 0, unroll=8)


def last(counts, send_leaves, send_parents, turned, near, leaf, par, arrived):
    return pl.pallas_call(
        last_kernel,
        name="last",
        out_shape=shaped(4, LEAVES * LEAF),
        in_specs=[SM, SM, VM, VM, VM, HB] + [VM] * 6,
        out_specs=VM,
        scratch_shapes=[
            pltpu.VMEM((LEAVES * 16, 128), f32),
            pltpu.VMEM((40, LEAVES), f32),
            pltpu.VMEM((4, LEAF, LEAVES), f32),
            pltpu.VMEM((LEAVES, 4, LEAF), f32),
            pltpu.SemaphoreType.DMA((1,)),
        ],
        compiler_params=pltpu.CompilerParams(**PARAMS),
    )(
        counts, send_leaves, send_leaves, send_parents, turned, near, leaf, par, *arrived
    )


def image_shift(slab_at, sub_at, slab_count, sub_count):
    rows_out = []
    for direction in range(4):
        reach_x = slab_at + slab_steps[direction]
        reach_y = sub_at + sub_steps[direction]
        jump_x = (reach_x - reach_x % slab_count) * CX
        jump_y = (reach_y - reach_y % sub_count) * CY
        rows_out.append(jnp.stack([jump_x, jump_y]))
    return jnp.stack(rows_out).astype(f32)


def moved_by(value, slab_step, sub_step, slab_count, sub_count):
    pairs = []
    for slab_at in range(slab_count):
        for sub_at in range(sub_count):
            target = (slab_at + slab_step) % slab_count * sub_count + (sub_at + sub_step) % sub_count
            pairs.append((slab_at * sub_count + sub_at, target))
    return lax.ppermute(value, ("slab", "sub"), pairs)


def on_device(
    positions, masses, leaf_counts, send_leaves, send_parents, near_pairs, far_pairs, parent_pairs
):
    slab_count = lax.axis_size("slab")
    sub_count = lax.axis_size("sub")
    slab_at = lax.axis_index("slab")
    sub_at = lax.axis_index("sub")
    at = jnp.stack([slab_at, sub_at]).astype(jnp.int32)
    own, cells, pcells, *outgoing, turned, leaf_order = front(
        at, leaf_counts, send_leaves, send_parents, positions, masses
    )
    incoming = [
        moved_by(outgoing[q], -slab_steps[q], -sub_steps[q], slab_count, sub_count)
        for q in range(4)
    ]
    image = image_shift(slab_at, sub_at, slab_count, sub_count)
    self0 = self_part(0, leaf_order, own)
    leaf, par, backs, ordered = far_part(
        image, far_pairs, parent_pairs, near_pairs, cells, pcells, incoming
    )
    near, *returning = near_part(ordered, own, incoming, backs, self0)
    arrived = [
        moved_by(returning[q], slab_steps[q], sub_steps[q], slab_count, sub_count)
        for q in range(4)
    ]
    near = self_part(1, leaf_order, own, near)
    return last(
        leaf_counts, send_leaves, send_parents, turned, near, leaf, par, arrived
    )


def solution(mesh):
    return jax.shard_map(
        on_device,
        mesh=mesh,
        in_specs=(
            P(None, ("slab", "sub")),
            P(("slab", "sub")),
            P(("slab", "sub")),
            P(("slab", "sub"), None),
            P(("slab", "sub"), None),
            P(("slab", "sub"), None, None),
            P(("slab", "sub"), None, None),
            P(("slab", "sub"), None, None),
        ),
        out_specs=P(None, ("slab", "sub")),
        check_vma=False,
    )
```

```python
import functools

import jax
import jax.numpy as jnp
from jax import lax
from jax.experimental import pallas as pl
from jax.experimental.pallas import tpu as pltpu
from jax.sharding import PartitionSpec as P

CX = 2
CY = 4
CZ = 32
LEAVES = 256
LEAF = 256
PARENTS = 32
SLOTS = 64
PSLOTS = 16
NEAR = 256
FAR = 1024
PFAR = 64
PAY = SLOTS + 5
SOFT = 0.0025
WIDTH = 8
SELF_WIDTH = 16
CLASSES = (128, 192, 256)
SORTED = 384
slab_steps = (1, 0, 1, 1)
sub_steps = (0, 1, 1, -1)
f32 = jnp.float32
bf16 = jnp.bfloat16

ALPHAS = [
    (i, j, d - i - j) for d in range(5) for i in range(d, -1, -1) for j in range(d - i, -1, -1)
]
AT = {a: n for n, a in enumerate(ALPHAS)}
FACT = (1.0, 1.0, 2.0, 6.0, 24.0)
TABLE = LEAVES + 4 * 128 + 128


def afact(alpha):
    return FACT[alpha[0]] * FACT[alpha[1]] * FACT[alpha[2]]


def add(a, b):
    return (a[0] + b[0], a[1] + b[1], a[2] + b[2])


def unit(axis):
    return tuple(1 if k == axis else 0 for k in range(3))


def split3(value):
    one = value.astype(bf16)
    rest = value - one.astype(f32)
    two = rest.astype(bf16)
    three = (rest - two.astype(f32)).astype(bf16)
    return one, two, three


def dot_nn(a, b):
    return lax.dot_general(a, b, (((1,), (0,)), ((), ())), preferred_element_type=f32)


def dot_nt(a, b):
    return lax.dot_general(a, b, (((1,), (1,)), ((), ())), preferred_element_type=f32)


def dot_tn(a, b):
    return lax.dot_general(a, b, (((0,), (0,)), ((), ())), preferred_element_type=f32)


def pick(values, onehot, transposed=False):
    parts = jnp.concatenate([part.astype(f32) for part in split3(values)], 0).astype(bf16)
    out = dot_nt(parts, onehot) if transposed else dot_nn(parts, onehot)
    rows = values.shape[0]
    return out[:rows] + out[rows : 2 * rows] + out[2 * rows :]


def iota(shape, dim):
    return lax.broadcasted_iota(jnp.int32, shape, dim)


def onehot_rows(count, ids):
    hit = iota((count, ids.shape[1]), 0) == ids
    return jnp.where(hit, 1.0, 0.0).astype(bf16)


def id_row(sent_leaves, sent_parents, q):
    return jnp.concatenate(
        [
            sent_leaves[:, q * SLOTS : (q + 1) * SLOTS],
            sent_parents[:, q * PSLOTS : (q + 1) * PSLOTS],
            jnp.full((1, 128 - SLOTS - PSLOTS), -1, jnp.int32),
        ],
        1,
    )


def put_slab(slab_ref, c, slab):
    wide = jnp.concatenate([slab, jnp.zeros((4, LEAF), f32)], 0)
    for half in range(2):
        rows = pl.ds(pl.multiple_of(half * LEAVES * 8 + c * 8, 8), 8)
        slab_ref[rows, :] = wide[:, half * 128 : half * 128 + 128]


def get_rows(slab_ref, comp):
    return jnp.concatenate(
        [slab_ref[pl.ds(half * LEAVES * 8 + comp, LEAVES, stride=8), :] for half in range(2)], 1
    )


def monomials(x, y, z, w):
    made = {(0, 0, 0): w}
    for alpha in ALPHAS[1:]:
        for axis, value in ((2, z), (1, y), (0, x)):
            if alpha[axis]:
                lower = tuple(alpha[k] - (k == axis) for k in range(3))
                made[alpha] = made[lower] * value
                break
    return made


def shift_moments(moments, offsets):
    choose = ((1,), (1, 1), (1, 2, 1), (1, 3, 3, 1), (1, 4, 6, 4, 1))
    for axis in range(3):
        powers = [None, offsets[axis]]
        for _ in range(3):
            powers.append(powers[-1] * offsets[axis])
        moved = {}
        for alpha in ALPHAS:
            total = moments[alpha]
            for k in range(alpha[axis]):
                lower = tuple(k if q == axis else alpha[q] for q in range(3))
                total = total + moments[lower] * powers[alpha[axis] - k] * float(
                    choose[alpha[axis]][k]
                )
            moved[alpha] = total
        moments = moved
    return moments


def leaf_lanes():
    lane = iota((1, LEAVES), 1)
    return lane // (CY * CZ), lane // CZ % CY, lane % CZ


def parent_offsets():
    cell_x, cell_y, cell_z = leaf_lanes()
    return [(cell % 2).astype(f32) - 0.5 for cell in (cell_x, cell_y, cell_z)]


def front_kernel(
    at_ref, counts_hbm, row_hbm, send_hbm, parents_hbm, pos_hbm, mass_hbm,
    own_ref, cells_ref, pcells_ref, pay0, pay1, pay2, pay3, turned_ref, ordered_ref,
    slab_ref, pos_ref, mass_ref, counts_ref, send_ref, counts_row, sent_leaves, sent_parents, sem,
):
    pays = (pay0, pay1, pay2, pay3)
    pieces = CX * CY
    bodies = LEAVES * LEAF // pieces
    places = [
        pltpu.make_async_copy(
            pos_hbm.at[:, pl.ds(n * bodies, bodies)], pos_ref.at[:, pl.ds(n * bodies, bodies)],
            sem.at[6 + n],
        )
        for n in range(pieces)
    ]
    smaller = [
        pltpu.make_async_copy(source, target, sem.at[n])
        for n, (source, target) in enumerate(
            (
                (counts_hbm, counts_ref), (mass_hbm, mass_ref), (send_hbm, send_ref),
                (row_hbm, counts_row), (send_hbm, sent_leaves), (parents_hbm, sent_parents),
            )
        )
    ]
    for copy in smaller[:2] + places + smaller[2:]:
        copy.start()
    for copy in smaller:
        copy.wait()
    base_x = at_ref[0] * CX
    base_y = at_ref[1] * CY
    row4 = iota((4, LEAF), 0)
    lane = iota((1, LEAF), 1)
    batch = 8

    for x in range(CX):
        for y in range(CY):
            centre = jnp.where(row4 == 1, (base_x + x).astype(f32) + 0.5, 0.0)
            centre = jnp.where(row4 == 2, (base_y + y).astype(f32) + 0.5, centre)
            places[x * CY + y].wait()

            def some_leaves(step, _, x=x, y=y, centre=centre):
                low = step * batch
                first = (x * CY + y) * CZ + low
                from_z = jnp.where(row4 == 3, low.astype(f32) + 0.5, centre)
                for k in range(batch):
                    c = first + k
                    start = pl.multiple_of(c * LEAF, LEAF)
                    place = pos_ref[:, pl.ds(start, LEAF)]
                    mass = jnp.concatenate(
                        [mass_ref[pl.ds(2 * c, 1), :], mass_ref[pl.ds(2 * c + 1, 1), :]], 1
                    )
                    weight = jnp.where(lane < counts_ref[c], mass, 0.0)
                    slab = jnp.concatenate([weight, place], 0) - (
                        from_z + jnp.where(row4 == 3, float(k), 0.0)
                    )
                    own_ref[c] = slab
                    put_slab(slab_ref, c, slab)
                return 0

            lax.fori_loop(0, CZ // batch, some_leaves, 0)

    for comp in range(4):
        turned_ref[comp] = get_rows(slab_ref, comp).T

    for half in range(2):
        lanes = slice(half * 128, half * 128 + 128)

        def chunk(step, totals):
            rows = pl.ds(pl.multiple_of(step * 8, 8), 8)
            w, x, y, z = [turned_ref[comp, rows, lanes] for comp in range(4)]
            made = monomials(x, y, z, w)
            return tuple(total + made[alpha] for total, alpha in zip(totals, ALPHAS))

        totals = lax.fori_loop(
            0, LEAF // 8, chunk, tuple(jnp.zeros((8, 128), f32) for _ in ALPHAS), unroll=2
        )
        for n, total in enumerate(totals):
            cells_ref[n : n + 1, lanes] = jnp.sum(total, 0, keepdims=True)

    cell_x, cell_y, cell_z = leaf_lanes()
    cells_ref[35:36, :] = (base_x + cell_x).astype(f32) + 0.5
    cells_ref[36:37, :] = (base_y + cell_y).astype(f32) + 0.5
    cells_ref[37:38, :] = cell_z.astype(f32) + 0.5
    cells_ref[38:39, :] = counts_row[...].astype(f32)
    cells_ref[39:40, :] = jnp.zeros((1, LEAVES), f32)

    moments = {alpha: cells_ref[n : n + 1, :] for n, alpha in enumerate(ALPHAS)}
    moved = shift_moments(moments, parent_offsets())
    moved = jnp.concatenate(
        [moved[alpha] for alpha in ALPHAS] + [jnp.zeros((5, LEAVES), f32)], 0
    )
    parent_of = (iota((LEAVES, 128), 0) // CZ % CY // 2) * (CZ // 2) + iota(
        (LEAVES, 128), 0
    ) % CZ // 2
    belongs = jnp.where(parent_of == iota((LEAVES, 128), 1), 1.0, 0.0).astype(bf16)
    pcells = pick(moved, belongs)
    plane = iota((40, 128), 1)
    prow = iota((40, 128), 0)
    pcells = jnp.where(prow == 35, (base_x + 1).astype(f32), pcells)
    pcells = jnp.where(
        prow == 36, (base_y + 2 * (plane // (CZ // 2))).astype(f32) + 1.0, pcells
    )
    pcells = jnp.where(prow == 37, (2 * (plane % (CZ // 2))).astype(f32) + 1.0, pcells)
    pcells_ref[...] = pcells

    lane128 = iota((1, 128), 1)
    for q in range(4):
        pay = pays[q]

        def copy_leaf(k, _, pay=pay, q=q):
            pay[k] = own_ref[send_ref[0, q * SLOTS + k]]
            return 0

        lax.fori_loop(0, SLOTS, copy_leaf, 0, unroll=8)
        ids = id_row(sent_leaves, sent_parents, q)
        leaf_hot = onehot_rows(LEAVES, jnp.where(lane128 < SLOTS, ids, -1))
        parent_hot = onehot_rows(128, jnp.where(lane128 >= SLOTS, ids, -1))
        block = pick(cells_ref[...], leaf_hot) + pick(pcells, parent_hot)
        put_block(pay, block)

    counts = counts_row[...]
    group = jnp.where(counts <= 128, 0, jnp.where(counts <= 192, 1, 2))
    sort_lists(iota((1, LEAVES), 1).astype(f32) + 1.0, group, SELF_WIDTH, ordered_ref)


def put_block(pay, block):
    for s in range(5):
        pay[SLOTS + s, :, 0:128] = block[4 * s : 4 * s + 4]
        pay[SLOTS + s, :, 128:256] = block[20 + 4 * s : 24 + 4 * s]


def get_block(tail):
    return jnp.concatenate(
        [tail(s)[:, 0:128] for s in range(5)] + [tail(s)[:, 128:256] for s in range(5)], 0
    )


VM = pl.BlockSpec(memory_space=pltpu.VMEM)
SM = pl.BlockSpec(memory_space=pltpu.SMEM)
HB = pl.BlockSpec(memory_space=pl.ANY)
HBM = pl.BlockSpec(memory_space=pltpu.MemorySpace.HBM)
PARAMS = dict(vmem_limit_bytes=24 * 1024 * 1024)


def in_hbm(value):
    return pltpu.with_memory_space_constraint(value, pltpu.MemorySpace.HBM)


def shaped(*shape):
    return jax.ShapeDtypeStruct(shape, f32)


def front(at, counts, send_leaves, send_parents, positions, masses):
    return pl.pallas_call(
        front_kernel,
        name="front",
        out_shape=[
            shaped(LEAVES, 4, LEAF), shaped(40, LEAVES), shaped(40, 128),
        ] + [shaped(PAY, 4, LEAF)] * 4 + [
            shaped(4, LEAF, LEAVES), jax.ShapeDtypeStruct((2, SORTED), jnp.int32),
        ],
        in_specs=[SM] + [HBM] * 6,
        out_specs=[VM] * 9,
        scratch_shapes=[
            pltpu.VMEM((LEAVES * 16, 128), f32),
            pltpu.VMEM((3, LEAVES * LEAF), f32),
            pltpu.VMEM((LEAVES * 2, 128), f32),
            pltpu.SMEM((LEAVES,), jnp.int32),
            pltpu.SMEM((1, 4 * SLOTS), jnp.int32),
            pltpu.VMEM((1, LEAVES), jnp.int32),
            pltpu.VMEM((1, 4 * SLOTS), jnp.int32),
            pltpu.VMEM((1, 4 * PSLOTS), jnp.int32),
            pltpu.SemaphoreType.DMA((6 + CX * CY,)),
        ],
        compiler_params=pltpu.CompilerParams(**PARAMS),
    )(
        at,
        *map(
            in_hbm,
            (
                counts, counts.reshape(1, LEAVES), send_leaves, send_parents, positions,
                masses.reshape(-1, 128),
            ),
        ),
    )


def slab8(slab):
    return jnp.concatenate([slab, jnp.zeros((4, LEAF), f32)], 0)


def b_form(points):
    row = iota(points.shape, 0)
    square = jnp.sum(jnp.where(row == 0, 0.0, points * points), 0, keepdims=True)
    return jnp.where(row == 4, square, points)


def a_form(formed):
    row = iota(formed.shape, 0)
    value = jnp.where(row == 0, formed[4:5] + SOFT, -2.0 * formed)
    return jnp.where(row == 4, 1.0, value)


def widen(value):
    one = value.astype(bf16).astype(f32)
    rest = value - one
    two = rest.astype(bf16).astype(f32)
    return one, two, rest - two


def squares(a_formed, b_formed):
    a1, a2, a3 = widen(a_form(a_formed))
    b1, b2, b3 = widen(b_formed)
    left = jnp.concatenate([a1, a1, a2, a2, a1, a3], 0).astype(bf16)
    right = jnp.concatenate([b1, b2, b1, b2, b3, b1], 0).astype(bf16)
    return dot_tn(left, right)


def weighted(formed, weight):
    parts = widen(formed * weight)
    return jnp.concatenate(parts + (jnp.zeros_like(parts[0]),), 0).astype(bf16)


def sources(points, weight):
    return weighted(b_form(points), weight)


def fold(out):
    total = out[0:8]
    for first in range(8, out.shape[0] // 8 * 8, 8):
        total = total + out[first : first + 8]
    return total


def finish(total, points):
    row = iota(points.shape, 0)
    field = total - points * total[0:1]
    sign = jnp.where(row == 0, -SOFT, jnp.where(row == 4, -1.0, 1.0))
    terms = jnp.where(row == 4, total, points * (field + total)) * sign
    return jnp.where(row == 0, jnp.sum(terms, 0, keepdims=True), field)[0:4]


def load_points(slab):
    wide = slab8(slab)
    row = iota((8, LEAF), 0)
    return jnp.where(row == 0, 1.0, wide), slab[0:1]


def self_kernel(part, list_ref, own_ref, *refs):
    out_ref = refs[-1]
    before_ref = refs[0]
    if not part:

        def begin(c, _):
            out_ref[c] = jnp.zeros((8, LEAF), f32)
            return 0

        lax.fori_loop(0, LEAVES, begin, 0, unroll=8)

    def place_of(step, k):
        code = list_ref[0, step * SELF_WIDTH + k]
        leaf = jnp.maximum(code - 1, 0)
        return leaf, jnp.where(code > 0, leaf, LEAVES)

    def some_leaves(step, rows, lanes):
        places = [place_of(step, k) for k in range(SELF_WIDTH)]
        loaded = []
        for leaf, _ in places:
            points, weight = load_points(own_ref[leaf])
            right = points[:, :lanes]
            formed = b_form(right)
            loaded.append((formed[:, :rows], weight[:, :rows], right, formed))
        spaced = [squares(left, formed) for left, _, _, formed in loaded]
        apart = jnp.where(iota((rows, lanes), 0) == iota((rows, lanes), 1), 0.0, 1.0)
        cubes = []
        for value in spaced:
            inverse = lax.rsqrt(value) * apart
            cubes.append(inverse * inverse * inverse)
        high = [cube.astype(bf16) for cube in cubes]
        done = []
        for cube, top, (left, weight, right, _), (leaf, _) in zip(cubes, high, loaded, places):
            low = (cube - top.astype(f32)).astype(bf16)
            side = weighted(left, weight)
            value = fold(dot_nn(side, top)) + fold(dot_nn(side[0:16], low))
            if part:
                value = finish(value + before_ref[leaf, :, 0:lanes], right)
            done.append(value)
        for (_, place), value in zip(places, done):
            out_ref[place, :, 0:lanes] = value

    def finish_some(step):
        places = [place_of(step, k) for k in range(SELF_WIDTH)]
        done = [finish(before_ref[leaf], load_points(own_ref[leaf])[0]) for leaf, _ in places]
        for (_, place), value in zip(places, done):
            out_ref[place] = value

    for n, rows in enumerate(CLASSES):
        first = list_ref[1, n]
        end = list_ref[1, n + 1]
        middle = (first + end + n % 2) >> 1
        lanes = 128 if rows == 128 else LEAF

        def body(step, _, rows=rows, lanes=lanes):
            some_leaves(step, rows, lanes)
            return 0

        lax.fori_loop(middle if part else first, end if part else middle, body, 0)
        if part:

            def rest(step, _):
                finish_some(step)
                return 0

            lax.fori_loop(first, middle, rest, 0)


def self_part(part, ordered, own, *before):
    return pl.pallas_call(
        functools.partial(self_kernel, part),
        name="self_part",
        out_shape=shaped(LEAVES + 8, 4 if part else 8, LEAF),
        in_specs=[SM, VM] + [VM] * part,
        out_specs=VM,
        cost_estimate=pl.CostEstimate(
            flops=LEAVES * 20_000_000, bytes_accessed=LEAVES * 8192, transcendentals=0
        ),
        compiler_params=pltpu.CompilerParams(**PARAMS),
    )(ordered, own, *before)


def near_kernel(
    list_ref, own_ref, in0, in1, in2, in3, backs_ref, self_ref,
    out_ref, pay0, pay1, pay2, pay3, table, total, shifts, formed_r, kept_c, sem, *held,
):
    pays = (pay0, pay1, pay2, pay3)
    copies = [
        pltpu.make_async_copy(own_ref, table.at[pl.ds(0, LEAVES)], sem.at[0]),
        pltpu.make_async_copy(self_ref.at[pl.ds(0, LEAVES)], total.at[pl.ds(0, LEAVES)], sem.at[5]),
    ]
    for q, part in enumerate((in0, in1, in2, in3)):
        copies.append(
            pltpu.make_async_copy(
                part.at[pl.ds(0, SLOTS)],
                table.at[pl.ds(LEAVES + q * SLOTS, SLOTS)],
                sem.at[1 + q],
            )
        )
    for copy in copies:
        copy.start()

    def clear(c, _):
        total[c] = jnp.zeros((8, LEAF), f32)
        return 0

    lax.fori_loop(LEAVES, 2 * LEAVES + 8, clear, 0, unroll=8)
    row = iota((8, 128), 0)
    for code in range(27):
        step = (code % 3 - 1, code // 3 % 3 - 1, code // 9 - 1)
        value = jnp.zeros((8, 128), f32)
        for k in range(3):
            value = jnp.where(row == k + 1, float(step[k]), value)
        shifts[code] = value
    for copy in copies:
        copy.wait()

    def decode(group, k):
        code = list_ref[0, group * WIDTH + k]
        value = jnp.maximum(code - 1, 0)
        return value & 511, (value >> 9) & 511, value >> 18, code > 0

    def shift_of(code):
        half = shifts[code]
        return jnp.concatenate([half, half], 1)

    def spaced(group, k, rows):
        r, c, code, _ = decode(group, k)
        points_r, _ = load_points(table[r])
        points_c, _ = load_points(table[c])
        points_r = (points_r + shift_of(code))[:, :rows]
        formed = b_form(points_r)
        formed_r[k, :, 0:rows] = formed
        kept_c[k] = points_c
        return squares(formed, b_form(points_c))

    def keep(k, rows, value):
        inverse = lax.rsqrt(value)
        held[k][0:rows, :] = (inverse * inverse * inverse).astype(bf16)

    def products(group, k, rows):
        r, c, code, live = decode(group, k)
        cube = held[k][0:rows, :]
        side_r = weighted(formed_r[k, :, 0:rows], table[r, 0:1, 0:rows])
        to_c = fold(dot_nn(side_r, cube))
        side_c = sources(kept_c[k] - shift_of(code), table[c, 0:1, :])
        to_r = fold(dot_nt(side_c, cube))
        return jnp.where(live, r, 2 * LEAVES), jnp.where(live, c, 2 * LEAVES), to_r, to_c

    def settle(done, rows):
        for r, c, to_r, to_c in done:
            total[r, :, 0:rows] = total[r, :, 0:rows] + to_r
            total[c] = total[c] + to_c

    for n, rows in enumerate(CLASSES):
        first = list_ref[1, n]
        end = list_ref[1, n + 1]

        @pl.when(end > first)
        def _(first=first, end=end, rows=rows):
            for k in range(WIDTH):
                keep(k, rows, spaced(first, k, rows))

            def advance(group, _):
                done = []
                for k in range(WIDTH):
                    done.append(products(group, k, rows))
                    keep(k, rows, spaced(group + 1, k, rows))
                settle(done, rows)
                return 0

            lax.fori_loop(first, end - 1, advance, 0)
            settle([products(end - 1, k, rows) for k in range(WIDTH)], rows)

    store = pltpu.make_async_copy(total.at[pl.ds(0, LEAVES)], out_ref, sem.at[6])
    store.start()
    for q in range(4):

        def finish_other(k, _, q=q):
            points, _ = load_points(table[LEAVES + q * SLOTS + k])
            pays[q][k] = finish(total[LEAVES + q * SLOTS + k], points)
            return 0

        lax.fori_loop(0, SLOTS, finish_other, 0, unroll=8)
        put_block(pays[q], backs_ref[q])
    store.wait()


def near_part(ordered, own, incoming, backs, self0):
    return pl.pallas_call(
        near_kernel,
        name="near_part",
        out_shape=[shaped(LEAVES, 8, LEAF)] + [shaped(PAY, 4, LEAF)] * 4,
        in_specs=[SM, HB, HB, HB, HB, HB, VM, HB],
        out_specs=[HB] + [VM] * 4,
        scratch_shapes=[
            pltpu.VMEM((2 * LEAVES, 4, LEAF), f32),
            pltpu.VMEM((2 * LEAVES + 8, 8, LEAF), f32),
            pltpu.VMEM((27, 8, 128), f32),
            pltpu.VMEM((WIDTH, 8, LEAF), f32),
            pltpu.VMEM((WIDTH, 8, LEAF), f32),
            pltpu.SemaphoreType.DMA((7,)),
        ] + [pltpu.VMEM((LEAF, LEAF), bf16)] * WIDTH,
        cost_estimate=pl.CostEstimate(
            flops=NEAR * 80_000_000, bytes_accessed=4_000_000, transcendentals=0
        ),
        compiler_params=pltpu.CompilerParams(**PARAMS),
    )(ordered, own, *incoming, backs, self0)


def sort_lists(code, group, width, out_ref):
    count = code.shape[1]
    hot = jnp.where(iota((8, count), 0) == group, 1.0, 0.0)
    earlier = jnp.where(iota((count, count), 0) < iota((count, count), 1), 1.0, 0.0).astype(bf16)
    before = dot_nn(hot.astype(bf16), earlier)
    members = jnp.sum(hot, 1, keepdims=True)
    lane = iota((1, SORTED), 1)
    place = jnp.zeros((1, count), f32)
    groups = jnp.zeros((1, 1), f32)
    ends = jnp.zeros((1, SORTED), f32)
    for n in range(len(CLASSES)):
        place = place + hot[n : n + 1] * (before[n : n + 1] + groups * width)
        groups = groups + jnp.floor((members[n : n + 1] + (width - 1)) * (1.0 / width))
        ends = jnp.where(lane == n + 1, groups, ends)
    place = jnp.where(group >= 0, place, -1.0).astype(jnp.int32)
    ordered = pick(jnp.broadcast_to(code, (8, count)), onehot_rows(SORTED, place), True)
    out_ref[0:1, :] = ordered[0:1].astype(jnp.int32)
    out_ref[1:2, :] = ends.astype(jnp.int32)


def derivatives(x, y, z):
    square = x * x + y * y + z * z
    inverse = 1.0 / jnp.sqrt(square)
    inverse2 = inverse * inverse
    table = {(0, (0, 0, 0)): inverse}
    for m in range(1, 5):
        table[(m, (0, 0, 0))] = table[(m - 1, (0, 0, 0))] * inverse2 * float(-(2 * m - 1))
    place = (x, y, z)

    def entry(m, alpha):
        key = (m, alpha)
        if key not in table:
            axis = [k for k in range(3) if alpha[k]][0]
            lower = tuple(alpha[k] - (k == axis) for k in range(3))
            value = place[axis] * entry(m + 1, lower)
            if lower[axis]:
                lowest = tuple(lower[k] - (k == axis) for k in range(3))
                value = value + float(lower[axis]) * entry(m + 1, lowest)
            table[key] = value
        return table[key]

    return {alpha: entry(0, alpha) for alpha in ALPHAS}


def mutual(a_ref, b_ref, to_a, to_b):
    def rows(n):
        return pl.ds(n * 8, 8)

    lift = a_ref[rows(38), :]
    live = a_ref[rows(39), :] > 0.5
    gap = [
        jnp.where(live, a_ref[rows(35 + k), :] - b_ref[rows(35 + k), :] - (lift if k == 2 else 0.0), 3.0)
        for k in range(3)
    ]
    made = derivatives(*gap)
    for beta in ALPHAS:
        sum_a = None
        sum_b = None
        for alpha in ALPHAS:
            if sum(alpha) + sum(beta) > 4:
                continue
            tensor = made[add(alpha, beta)]
            scale = 1.0 / afact(alpha)
            sign_a = -((-1.0) ** sum(alpha)) * scale
            sign_b = -((-1.0) ** sum(beta)) * scale
            term_a = b_ref[rows(AT[alpha]), :] * sign_a * tensor
            term_b = a_ref[rows(AT[alpha]), :] * sign_b * tensor
            sum_a = term_a if sum_a is None else sum_a + term_a
            sum_b = term_b if sum_b is None else sum_b + term_b
        to_a[rows(AT[beta]), :] = jnp.where(live, sum_a, 0.0)
        to_b[rows(AT[beta]), :] = jnp.where(live, sum_b, 0.0)


def far_kernel(
    image_ref, far_ref, parent_ref, near_ref, cells_ref, pcells_ref, in0, in1, in2, in3,
    leaf_ref, par_ref, backs_ref, ordered_ref, tails, table, left, right, to_a, to_b, total, sem,
):
    copies = []
    for q, part in enumerate((in0, in1, in2, in3)):
        copies.append(
            pltpu.make_async_copy(part.at[pl.ds(SLOTS, 5)], tails.at[q], sem.at[q])
        )
    for copy in copies:
        copy.start()
    table[:, 0:LEAVES] = cells_ref[...]
    table[:, LEAVES + 512 :] = pcells_ref[...]
    row = iota((40, 128), 0)
    to_a[...] = jnp.zeros_like(to_a)
    to_b[...] = jnp.zeros_like(to_b)
    left[...] = jnp.zeros_like(left)
    right[...] = jnp.zeros_like(right)
    for copy in copies:
        copy.wait()
    for q in range(4):
        block = get_block(lambda s, q=q: tails[q, s])
        block = block + jnp.where(
            row == 35, image_ref[q, 0], jnp.where(row == 36, image_ref[q, 1], 0.0)
        )
        table[:, LEAVES + q * 128 : LEAVES + q * 128 + 128] = block
    parts = jnp.concatenate([part.astype(f32) for part in split3(table[...])], 0).astype(bf16)
    total[...] = jnp.zeros_like(total)

    def gathered(hot, first, count):
        out = dot_nn(parts[:, first : first + count], hot)
        return out[0:40] + out[40:80] + out[80:120]

    def leaf_entry(ids):
        other = ids - LEAVES
        return jnp.where(ids < LEAVES, ids, LEAVES + other // SLOTS * 128 + other % SLOTS)

    def parent_entry(ids):
        other = ids - PARENTS
        return jnp.where(
            ids < PARENTS, LEAVES + 512 + ids, LEAVES + other // PSLOTS * 128 + SLOTS + other % PSLOTS
        )

    def hots(ids_a, ids_b, parents):
        if parents:
            return (
                onehot_rows(128, ids_a), LEAVES + 512, 128,
                onehot_rows(640, parent_entry(ids_b) - LEAVES), LEAVES, 640,
            )
        return (
            onehot_rows(LEAVES, ids_a), 0, LEAVES,
            onehot_rows(768, leaf_entry(ids_b)), 0, 768,
        )

    def load(ids_a, ids_b, lifts, g, parents):
        hot_a, first_a, count_a, hot_b, first_b, count_b = hots(ids_a, ids_b, parents)
        from_a = gathered(hot_a, first_a, count_a)
        from_b = gathered(hot_b, first_b, count_b)
        live = jnp.where(ids_b >= 0, 1.0, 0.0)
        from_a = jnp.where(row == 38, lifts.astype(f32) * float(CZ), from_a)
        from_a = jnp.where(row == 39, live, from_a)
        left[pl.ds(g, 40, stride=8), :] = from_a
        right[pl.ds(g, 40, stride=8), :] = from_b

    def store(ids_a, ids_b, g, parents):
        hot_a, first_a, count_a, hot_b, first_b, count_b = hots(ids_a, ids_b, parents)
        sum_a = pick(to_a[pl.ds(g, 40, stride=8), :], hot_a, True)
        sum_b = pick(to_b[pl.ds(g, 40, stride=8), :], hot_b, True)
        total[:, first_a : first_a + count_a] += sum_a
        total[:, first_b : first_b + count_b] += sum_b

    for g in range(FAR // 128):
        lanes = slice(g * 128, g * 128 + 128)
        load(far_ref[0, :, lanes], far_ref[1, :, lanes], far_ref[2, :, lanes], g, False)
    mutual(left, right, to_a, to_b)
    for g in range(FAR // 128):
        lanes = slice(g * 128, g * 128 + 128)
        store(far_ref[0, :, lanes], far_ref[1, :, lanes], g, False)
    ids_a, ids_b, lifts = [
        jnp.concatenate([parent_ref[k], jnp.full((1, 128 - PFAR), -(k == 1), jnp.int32)], 1)
        for k in range(3)
    ]
    load(ids_a, ids_b, lifts, 0, True)
    mutual(left, right, to_a, to_b)
    store(ids_a, ids_b, 0, True)

    ids_a, ids_b, lifts = near_ref[0], near_ref[1], near_ref[2]
    hot_a, _, _, hot_b, _, _ = hots(ids_a, ids_b, False)
    from_a = gathered(hot_a, 0, LEAVES)[35:39]
    from_b = gathered(hot_b, 0, 768)[35:39]
    count_a, count_b = from_a[3:4], from_b[3:4]
    fewer = jnp.minimum(count_a, count_b)
    swap = count_b < count_a
    group = jnp.where(fewer <= 128.0, 0, jnp.where(fewer <= 192.0, 1, 2))
    group = jnp.where(ids_b >= 0, group, -1)
    moved = jnp.zeros((1, NEAR), f32)
    for k in range(3):
        apart = from_a[k : k + 1] - from_b[k : k + 1]
        if k == 2:
            apart = apart - lifts.astype(f32) * float(CZ)
        apart = jnp.where(swap, -apart, apart)
        moved = moved + (apart + 1.0) * float(3**k)
    rows = jnp.where(swap, ids_b, ids_a)
    columns = jnp.where(swap, ids_a, ids_b)
    code = 1.0 + rows.astype(f32) + columns.astype(f32) * 512.0 + moved * 262144.0
    sort_lists(jnp.where(ids_b >= 0, code, 0.0), group, WIDTH, ordered_ref)

    leaf_ref[...] = total[:, 0:LEAVES]
    par_ref[...] = total[:, LEAVES + 512 :]
    for q in range(4):
        backs_ref[q] = total[:, LEAVES + q * 128 : LEAVES + q * 128 + 128]


def far_part(image, far, parent, near, cells, pcells, incoming):
    return pl.pallas_call(
        far_kernel,
        name="far_part",
        out_shape=[
            shaped(40, LEAVES), shaped(40, 128), shaped(4, 40, 128),
            jax.ShapeDtypeStruct((2, SORTED), jnp.int32),
        ],
        in_specs=[SM, VM, VM, VM, VM, VM, HB, HB, HB, HB],
        out_specs=[VM] * 4,
        scratch_shapes=[
            pltpu.VMEM((4, 5, 4, LEAF), f32),
            pltpu.VMEM((40, TABLE), f32),
        ] + [pltpu.VMEM((320, 128), f32)] * 4 + [
            pltpu.VMEM((40, TABLE), f32),
            pltpu.SemaphoreType.DMA((4,)),
        ],
        compiler_params=pltpu.CompilerParams(**PARAMS),
    )(
        image, far.transpose(1, 0, 2), parent.transpose(1, 0, 2), near.transpose(1, 0, 2),
        cells, pcells, *incoming,
    )


def shift_terms(terms, offsets):
    for axis in range(3):
        powers = [None, offsets[axis]]
        for _ in range(3):
            powers.append(powers[-1] * offsets[axis])
        moved = {}
        for alpha in ALPHAS:
            total = terms[alpha]
            for k in range(1, 5 - sum(alpha)):
                upper = tuple(alpha[q] + k * (q == axis) for q in range(3))
                total = total + terms[upper] * powers[k] * (1.0 / FACT[k])
            moved[alpha] = total
        terms = moved
    return terms


def horner(coefs, x):
    value = coefs[-1]
    for coef in reversed(coefs[:-1]):
        value = value * x + coef
    return value


def horner_both(coefs, x):
    value, slope = coefs[-1], None
    for coef in reversed(coefs[:-1]):
        slope = value if slope is None else slope * x + value
        value = value * x + coef
    return value, slope


def polynomial(get, x, y, z):
    over_y, over_dy, over_dz = [], [], []
    for i in range(5):
        over_z = [
            horner_both([get((i, j, k)) for k in range(5 - i - j)], z) for j in range(5 - i)
        ]
        value, slope = horner_both([pair[0] for pair in over_z], y)
        over_y.append(value)
        if i < 4:
            over_dy.append(slope)
            over_dz.append(horner([pair[1] for pair in over_z[:-1]], y))
    value, slope = horner_both(over_y, x)
    return value, slope, horner(over_dy, x), horner(over_dz, x)


def last_kernel(
    counts_ref, send_ref, sent_leaves, sent_parents, turned_ref, self_hbm, leaf_ref,
    par_ref, in0, in1, in2, in3, out_ref, slab_ref, terms_ref, field_ref, near_sum, sem,
):
    incoming = (in0, in1, in2, in3)
    lane128 = iota((1, 128), 1)
    fetch = pltpu.make_async_copy(self_hbm.at[pl.ds(0, LEAVES)], near_sum, sem.at[0])
    fetch.start()
    leaf = leaf_ref[...]
    par = par_ref[...]
    for q in range(4):
        block = get_block(lambda s, q=q: incoming[q][SLOTS + s])
        ids = id_row(sent_leaves, sent_parents, q)
        leaf_hot = onehot_rows(LEAVES, jnp.where(lane128 < SLOTS, ids, -1))
        parent_hot = onehot_rows(128, jnp.where(lane128 >= SLOTS, ids, -1))
        leaf = leaf + pick(block, leaf_hot, True)
        par = par + pick(block, parent_hot, True)

    fetch.wait()
    for q in range(4):

        def arrive(step, _, q=q):
            first = step * 8
            places = [send_ref[0, q * SLOTS + first + k] for k in range(8)]
            values = [near_sum[c] + incoming[q][first + k] for k, c in enumerate(places)]
            for c, value in zip(places, values):
                near_sum[c] = value
            return 0

        lax.fori_loop(0, SLOTS // 8, arrive, 0)
    lane_parent = (iota((128, LEAVES), 1) // CZ % CY // 2) * (CZ // 2) + iota(
        (128, LEAVES), 1
    ) % CZ // 2
    above = pick(par, jnp.where(lane_parent == iota((128, LEAVES), 0), 1.0, 0.0).astype(bf16))
    terms = {alpha: above[n : n + 1, :] for n, alpha in enumerate(ALPHAS)}
    terms = shift_terms(terms, parent_offsets())
    for n, alpha in enumerate(ALPHAS):
        terms_ref[n : n + 1, :] = leaf[n : n + 1, :] + terms[alpha]

    for half in range(2):
        lanes = slice(half * 128, half * 128 + 128)

        def term(alpha):
            return terms_ref[AT[alpha] : AT[alpha] + 1, lanes]

        coefs = {alpha: term(alpha) * (1.0 / afact(alpha)) for alpha in ALPHAS}

        def chunk(step, _, coefs=coefs, lanes=lanes):
            rows = pl.ds(pl.multiple_of(step * 32, 32), 32)
            x, y, z = [turned_ref[comp, rows, lanes] for comp in range(1, 4)]
            value, *slopes = polynomial(lambda alpha: coefs[alpha], x, y, z)
            field_ref[0, rows, lanes] = value
            for comp, slope in enumerate(slopes):
                field_ref[comp + 1, rows, lanes] = -slope
            return 0

        lax.fori_loop(0, LEAF // 32, chunk, 0)

    for comp in range(4):
        turned = field_ref[comp].T
        for half in range(2):
            slab_ref[pl.ds(half * LEAVES * 8 + comp, LEAVES, stride=8), :] = turned[
                :, half * 128 : half * 128 + 128
            ]

    lane = iota((4, LEAF), 1)

    def write(c, _):
        value = jnp.concatenate(
            [
                slab_ref[pl.ds(pl.multiple_of(half * LEAVES * 8 + c * 8, 8), 8), :]
                for half in range(2)
            ],
            1,
        )[0:4] + near_sum[c]
        start = pl.multiple_of(c * LEAF, LEAF)
        out_ref[:, pl.ds(start, LEAF)] = jnp.where(lane < counts_ref[c], value, 0.0)
        return 0

    lax.fori_loop(0, LEAVES, write, 0, unroll=8)


def last(counts, send_leaves, send_parents, turned, near, leaf, par, arrived):
    return pl.pallas_call(
        last_kernel,
        name="last",
        out_shape=shaped(4, LEAVES * LEAF),
        in_specs=[SM, SM, VM, VM, VM, HB] + [VM] * 6,
        out_specs=VM,
        scratch_shapes=[
            pltpu.VMEM((LEAVES * 16, 128), f32),
            pltpu.VMEM((40, LEAVES), f32),
            pltpu.VMEM((4, LEAF, LEAVES), f32),
            pltpu.VMEM((LEAVES, 4, LEAF), f32),
            pltpu.SemaphoreType.DMA((1,)),
        ],
        compiler_params=pltpu.CompilerParams(**PARAMS),
    )(
        counts, send_leaves, send_leaves, send_parents, turned, near, leaf, par, *arrived
    )


def image_shift(slab_at, sub_at, slab_count, sub_count):
    rows_out = []
    for direction in range(4):
        reach_x = slab_at + slab_steps[direction]
        reach_y = sub_at + sub_steps[direction]
        jump_x = (reach_x - reach_x % slab_count) * CX
        jump_y = (reach_y - reach_y % sub_count) * CY
        rows_out.append(jnp.stack([jump_x, jump_y]))
    return jnp.stack(rows_out).astype(f32)


def moved_by(value, slab_step, sub_step, slab_count, sub_count):
    pairs = []
    for slab_at in range(slab_count):
        for sub_at in range(sub_count):
            target = (slab_at + slab_step) % slab_count * sub_count + (sub_at + sub_step) % sub_count
            pairs.append((slab_at * sub_count + sub_at, target))
    return lax.ppermute(value, ("slab", "sub"), pairs)


def on_device(
    positions, masses, leaf_counts, send_leaves, send_parents, near_pairs, far_pairs, parent_pairs
):
    slab_count = lax.axis_size("slab")
    sub_count = lax.axis_size("sub")
    slab_at = lax.axis_index("slab")
    sub_at = lax.axis_index("sub")
    at = jnp.stack([slab_at, sub_at]).astype(jnp.int32)
    own, cells, pcells, *outgoing, turned, leaf_order = front(
        at, leaf_counts, send_leaves, send_parents, positions, masses
    )
    incoming = [
        moved_by(outgoing[q], -slab_steps[q], -sub_steps[q], slab_count, sub_count)
        for q in range(4)
    ]
    image = image_shift(slab_at, sub_at, slab_count, sub_count)
    self0 = self_part(0, leaf_order, own)
    leaf, par, backs, ordered = far_part(
        image, far_pairs, parent_pairs, near_pairs, cells, pcells, incoming
    )
    near, *returning = near_part(ordered, own, incoming, backs, self0)
    arrived = [
        moved_by(returning[q], slab_steps[q], sub_steps[q], slab_count, sub_count)
        for q in range(4)
    ]
    near = self_part(1, leaf_order, own, near)
    return last(
        leaf_counts, send_leaves, send_parents, turned, near, leaf, par, arrived
    )


def solution(mesh):
    return jax.shard_map(
        on_device,
        mesh=mesh,
        in_specs=(
            P(None, ("slab", "sub")),
            P(("slab", "sub")),
            P(("slab", "sub")),
            P(("slab", "sub"), None),
            P(("slab", "sub"), None),
            P(("slab", "sub"), None, None),
            P(("slab", "sub"), None, None),
            P(("slab", "sub"), None, None),
        ),
        out_specs=P(None, ("slab", "sub")),
        check_vma=False,
    )
```

```python
import functools

import jax
import jax.numpy as jnp
from jax import lax
from jax.experimental import pallas as pl
from jax.experimental.pallas import tpu as pltpu
from jax.sharding import PartitionSpec as P

CX = 2
CY = 4
CZ = 32
LEAVES = 256
LEAF = 256
PARENTS = 32
SLOTS = 64
PSLOTS = 16
NEAR = 256
FAR = 1024
PFAR = 64
PAY = SLOTS + 5
SOFT = 0.0025
WIDTH = 8
SELF_WIDTH = 16
CLASSES = (128, 192, 256)
SORTED = 384
slab_steps = (1, 0, 1, 1)
sub_steps = (0, 1, 1, -1)
f32 = jnp.float32
bf16 = jnp.bfloat16

ALPHAS = [
    (i, j, d - i - j) for d in range(5) for i in range(d, -1, -1) for j in range(d - i, -1, -1)
]
AT = {a: n for n, a in enumerate(ALPHAS)}
FACT = (1.0, 1.0, 2.0, 6.0, 24.0)
TABLE = LEAVES + 4 * 128 + 128


def afact(alpha):
    return FACT[alpha[0]] * FACT[alpha[1]] * FACT[alpha[2]]


def add(a, b):
    return (a[0] + b[0], a[1] + b[1], a[2] + b[2])


def unit(axis):
    return tuple(1 if k == axis else 0 for k in range(3))


def split3(value):
    one = value.astype(bf16)
    rest = value - one.astype(f32)
    two = rest.astype(bf16)
    three = (rest - two.astype(f32)).astype(bf16)
    return one, two, three


def dot_nn(a, b):
    return lax.dot_general(a, b, (((1,), (0,)), ((), ())), preferred_element_type=f32)


def dot_nt(a, b):
    return lax.dot_general(a, b, (((1,), (1,)), ((), ())), preferred_element_type=f32)


def dot_tn(a, b):
    return lax.dot_general(a, b, (((0,), (0,)), ((), ())), preferred_element_type=f32)


def pick(values, onehot, transposed=False):
    parts = jnp.concatenate([part.astype(f32) for part in split3(values)], 0).astype(bf16)
    out = dot_nt(parts, onehot) if transposed else dot_nn(parts, onehot)
    rows = values.shape[0]
    return out[:rows] + out[rows : 2 * rows] + out[2 * rows :]


def iota(shape, dim):
    return lax.broadcasted_iota(jnp.int32, shape, dim)


def onehot_rows(count, ids):
    hit = iota((count, ids.shape[1]), 0) == ids
    return jnp.where(hit, 1.0, 0.0).astype(bf16)


def id_row(sent_leaves, sent_parents, q):
    return jnp.concatenate(
        [
            sent_leaves[:, q * SLOTS : (q + 1) * SLOTS],
            sent_parents[:, q * PSLOTS : (q + 1) * PSLOTS],
            jnp.full((1, 128 - SLOTS - PSLOTS), -1, jnp.int32),
        ],
        1,
    )


def put_slab(slab_ref, c, slab):
    wide = jnp.concatenate([slab, jnp.zeros((4, LEAF), f32)], 0)
    for half in range(2):
        rows = pl.ds(pl.multiple_of(half * LEAVES * 8 + c * 8, 8), 8)
        slab_ref[rows, :] = wide[:, half * 128 : half * 128 + 128]


def get_rows(slab_ref, comp):
    return jnp.concatenate(
        [slab_ref[pl.ds(half * LEAVES * 8 + comp, LEAVES, stride=8), :] for half in range(2)], 1
    )


def monomials(x, y, z, w):
    made = {(0, 0, 0): w}
    for alpha in ALPHAS[1:]:
        for axis, value in ((2, z), (1, y), (0, x)):
            if alpha[axis]:
                lower = tuple(alpha[k] - (k == axis) for k in range(3))
                made[alpha] = made[lower] * value
                break
    return made


def shift_moments(moments, offsets):
    choose = ((1,), (1, 1), (1, 2, 1), (1, 3, 3, 1), (1, 4, 6, 4, 1))
    for axis in range(3):
        powers = [None, offsets[axis]]
        for _ in range(3):
            powers.append(powers[-1] * offsets[axis])
        moved = {}
        for alpha in ALPHAS:
            total = moments[alpha]
            for k in range(alpha[axis]):
                lower = tuple(k if q == axis else alpha[q] for q in range(3))
                total = total + moments[lower] * powers[alpha[axis] - k] * float(
                    choose[alpha[axis]][k]
                )
            moved[alpha] = total
        moments = moved
    return moments


def leaf_lanes():
    lane = iota((1, LEAVES), 1)
    return lane // (CY * CZ), lane // CZ % CY, lane % CZ


def parent_offsets():
    cell_x, cell_y, cell_z = leaf_lanes()
    return [(cell % 2).astype(f32) - 0.5 for cell in (cell_x, cell_y, cell_z)]


def front_kernel(
    at_ref, counts_hbm, row_hbm, send_hbm, parents_hbm, pos_hbm, mass_hbm,
    own_ref, cells_ref, pcells_ref, pay0, pay1, pay2, pay3, turned_ref, ordered_ref,
    slab_ref, pos_ref, mass_ref, counts_ref, send_ref, counts_row, sent_leaves, sent_parents, sem,
):
    pays = (pay0, pay1, pay2, pay3)
    pieces = CX * CY
    bodies = LEAVES * LEAF // pieces
    places = [
        pltpu.make_async_copy(
            pos_hbm.at[:, pl.ds(n * bodies, bodies)], pos_ref.at[:, pl.ds(n * bodies, bodies)],
            sem.at[6 + n],
        )
        for n in range(pieces)
    ]
    smaller = [
        pltpu.make_async_copy(source, target, sem.at[n])
        for n, (source, target) in enumerate(
            (
                (counts_hbm, counts_ref), (mass_hbm, mass_ref), (send_hbm, send_ref),
                (row_hbm, counts_row), (send_hbm, sent_leaves), (parents_hbm, sent_parents),
            )
        )
    ]
    for copy in smaller[:2] + places + smaller[2:]:
        copy.start()
    for copy in smaller:
        copy.wait()
    base_x = at_ref[0] * CX
    base_y = at_ref[1] * CY
    row4 = iota((4, LEAF), 0)
    lane = iota((1, LEAF), 1)
    batch = 8

    for x in range(CX):
        for y in range(CY):
            centre = jnp.where(row4 == 1, (base_x + x).astype(f32) + 0.5, 0.0)
            centre = jnp.where(row4 == 2, (base_y + y).astype(f32) + 0.5, centre)
            places[x * CY + y].wait()

            def some_leaves(step, _, x=x, y=y, centre=centre):
                low = step * batch
                first = (x * CY + y) * CZ + low
                from_z = jnp.where(row4 == 3, low.astype(f32) + 0.5, centre)
                for k in range(batch):
                    c = first + k
                    start = pl.multiple_of(c * LEAF, LEAF)
                    place = pos_ref[:, pl.ds(start, LEAF)]
                    mass = jnp.concatenate(
                        [mass_ref[pl.ds(2 * c, 1), :], mass_ref[pl.ds(2 * c + 1, 1), :]], 1
                    )
                    weight = jnp.where(lane < counts_ref[c], mass, 0.0)
                    slab = jnp.concatenate([weight, place], 0) - (
                        from_z + jnp.where(row4 == 3, float(k), 0.0)
                    )
                    own_ref[c] = slab
                    put_slab(slab_ref, c, slab)
                return 0

            lax.fori_loop(0, CZ // batch, some_leaves, 0)

    for comp in range(4):
        turned_ref[comp] = get_rows(slab_ref, comp).T

    for half in range(2):
        lanes = slice(half * 128, half * 128 + 128)

        def chunk(step, totals):
            rows = pl.ds(pl.multiple_of(step * 8, 8), 8)
            w, x, y, z = [turned_ref[comp, rows, lanes] for comp in range(4)]
            made = monomials(x, y, z, w)
            return tuple(total + made[alpha] for total, alpha in zip(totals, ALPHAS))

        totals = lax.fori_loop(
            0, LEAF // 8, chunk, tuple(jnp.zeros((8, 128), f32) for _ in ALPHAS), unroll=2
        )
        for n, total in enumerate(totals):
            cells_ref[n : n + 1, lanes] = jnp.sum(total, 0, keepdims=True)

    cell_x, cell_y, cell_z = leaf_lanes()
    cells_ref[35:36, :] = (base_x + cell_x).astype(f32) + 0.5
    cells_ref[36:37, :] = (base_y + cell_y).astype(f32) + 0.5
    cells_ref[37:38, :] = cell_z.astype(f32) + 0.5
    cells_ref[38:39, :] = counts_row[...].astype(f32)
    cells_ref[39:40, :] = jnp.zeros((1, LEAVES), f32)

    moments = {alpha: cells_ref[n : n + 1, :] for n, alpha in enumerate(ALPHAS)}
    moved = shift_moments(moments, parent_offsets())
    moved = jnp.concatenate(
        [moved[alpha] for alpha in ALPHAS] + [jnp.zeros((5, LEAVES), f32)], 0
    )
    parent_of = (iota((LEAVES, 128), 0) // CZ % CY // 2) * (CZ // 2) + iota(
        (LEAVES, 128), 0
    ) % CZ // 2
    belongs = jnp.where(parent_of == iota((LEAVES, 128), 1), 1.0, 0.0).astype(bf16)
    pcells = pick(moved, belongs)
    plane = iota((40, 128), 1)
    prow = iota((40, 128), 0)
    pcells = jnp.where(prow == 35, (base_x + 1).astype(f32), pcells)
    pcells = jnp.where(
        prow == 36, (base_y + 2 * (plane // (CZ // 2))).astype(f32) + 1.0, pcells
    )
    pcells = jnp.where(prow == 37, (2 * (plane % (CZ // 2))).astype(f32) + 1.0, pcells)
    pcells_ref[...] = pcells

    lane128 = iota((1, 128), 1)
    for q in range(4):
        pay = pays[q]

        def copy_leaf(k, _, pay=pay, q=q):
            pay[k] = own_ref[send_ref[0, q * SLOTS + k]]
            return 0

        lax.fori_loop(0, SLOTS, copy_leaf, 0, unroll=8)
        ids = id_row(sent_leaves, sent_parents, q)
        leaf_hot = onehot_rows(LEAVES, jnp.where(lane128 < SLOTS, ids, -1))
        parent_hot = onehot_rows(128, jnp.where(lane128 >= SLOTS, ids, -1))
        block = pick(cells_ref[...], leaf_hot) + pick(pcells, parent_hot)
        put_block(pay, block)

    counts = counts_row[...]
    group = jnp.where(counts <= 128, 0, jnp.where(counts <= 192, 1, 2))
    sort_lists(iota((1, LEAVES), 1).astype(f32) + 1.0, group, SELF_WIDTH, ordered_ref)


def put_block(pay, block):
    for s in range(5):
        pay[SLOTS + s, :, 0:128] = block[4 * s : 4 * s + 4]
        pay[SLOTS + s, :, 128:256] = block[20 + 4 * s : 24 + 4 * s]


def get_block(tail):
    return jnp.concatenate(
        [tail(s)[:, 0:128] for s in range(5)] + [tail(s)[:, 128:256] for s in range(5)], 0
    )


VM = pl.BlockSpec(memory_space=pltpu.VMEM)
SM = pl.BlockSpec(memory_space=pltpu.SMEM)
HB = pl.BlockSpec(memory_space=pl.ANY)
HBM = pl.BlockSpec(memory_space=pltpu.MemorySpace.HBM)
PARAMS = dict(vmem_limit_bytes=24 * 1024 * 1024)


def in_hbm(value):
    return pltpu.with_memory_space_constraint(value, pltpu.MemorySpace.HBM)


def shaped(*shape):
    return jax.ShapeDtypeStruct(shape, f32)


def front(at, counts, send_leaves, send_parents, positions, masses):
    return pl.pallas_call(
        front_kernel,
        name="front",
        out_shape=[
            shaped(LEAVES, 4, LEAF), shaped(40, LEAVES), shaped(40, 128),
        ] + [shaped(PAY, 4, LEAF)] * 4 + [
            shaped(4, LEAF, LEAVES), jax.ShapeDtypeStruct((2, SORTED), jnp.int32),
        ],
        in_specs=[SM] + [HBM] * 6,
        out_specs=[VM] * 9,
        scratch_shapes=[
            pltpu.VMEM((LEAVES * 16, 128), f32),
            pltpu.VMEM((3, LEAVES * LEAF), f32),
            pltpu.VMEM((LEAVES * 2, 128), f32),
            pltpu.SMEM((LEAVES,), jnp.int32),
            pltpu.SMEM((1, 4 * SLOTS), jnp.int32),
            pltpu.VMEM((1, LEAVES), jnp.int32),
            pltpu.VMEM((1, 4 * SLOTS), jnp.int32),
            pltpu.VMEM((1, 4 * PSLOTS), jnp.int32),
            pltpu.SemaphoreType.DMA((6 + CX * CY,)),
        ],
        compiler_params=pltpu.CompilerParams(**PARAMS),
    )(
        at,
        *map(
            in_hbm,
            (
                counts, counts.reshape(1, LEAVES), send_leaves, send_parents, positions,
                masses.reshape(-1, 128),
            ),
        ),
    )


def slab8(slab):
    return jnp.concatenate([slab, jnp.zeros((4, LEAF), f32)], 0)


def b_form(points):
    row = iota(points.shape, 0)
    square = jnp.sum(jnp.where(row == 0, 0.0, points * points), 0, keepdims=True)
    return jnp.where(row == 4, square, points)


def a_form(formed):
    row = iota(formed.shape, 0)
    value = jnp.where(row == 0, formed[4:5] + SOFT, -2.0 * formed)
    return jnp.where(row == 4, 1.0, value)


def widen(value):
    one = value.astype(bf16).astype(f32)
    rest = value - one
    two = rest.astype(bf16).astype(f32)
    return one, two, rest - two


def squares(a_formed, b_formed):
    a1, a2, a3 = widen(a_form(a_formed))
    b1, b2, b3 = widen(b_formed)
    left = jnp.concatenate([a1, a1, a2, a2, a1, a3], 0).astype(bf16)
    right = jnp.concatenate([b1, b2, b1, b2, b3, b1], 0).astype(bf16)
    return dot_tn(left, right)


def weighted(formed, weight):
    parts = widen(formed * weight)
    return jnp.concatenate(parts + (jnp.zeros_like(parts[0]),), 0).astype(bf16)


def sources(points, weight):
    return weighted(b_form(points), weight)


def fold(out):
    total = out[0:8]
    for first in range(8, out.shape[0] // 8 * 8, 8):
        total = total + out[first : first + 8]
    return total


def finish(total, points):
    row = iota(points.shape, 0)
    field = total - points * total[0:1]
    sign = jnp.where(row == 0, -SOFT, jnp.where(row == 4, -1.0, 1.0))
    terms = jnp.where(row == 4, total, points * (field + total)) * sign
    return jnp.where(row == 0, jnp.sum(terms, 0, keepdims=True), field)[0:4]


def load_points(slab):
    wide = slab8(slab)
    row = iota((8, LEAF), 0)
    return jnp.where(row == 0, 1.0, wide), slab[0:1]


def self_kernel(part, list_ref, own_ref, *refs):
    out_ref = refs[-1]
    before_ref = refs[0]
    if not part:

        def begin(c, _):
            out_ref[c] = jnp.zeros((8, LEAF), f32)
            return 0

        lax.fori_loop(0, LEAVES, begin, 0, unroll=8)

    def place_of(step, k):
        code = list_ref[0, step * SELF_WIDTH + k]
        leaf = jnp.maximum(code - 1, 0)
        return leaf, jnp.where(code > 0, leaf, LEAVES)

    def some_leaves(step, rows, lanes):
        places = [place_of(step, k) for k in range(SELF_WIDTH)]
        loaded = []
        for leaf, _ in places:
            points, weight = load_points(own_ref[leaf])
            right = points[:, :lanes]
            formed = b_form(right)
            loaded.append((formed[:, :rows], weight[:, :rows], right, formed))
        spaced = [squares(left, formed) for left, _, _, formed in loaded]
        apart = jnp.where(iota((rows, lanes), 0) == iota((rows, lanes), 1), 0.0, 1.0)
        cubes = []
        for value in spaced:
            inverse = lax.rsqrt(value) * apart
            cubes.append(inverse * inverse * inverse)
        high = [cube.astype(bf16) for cube in cubes]
        done = []
        for cube, top, (left, weight, right, _), (leaf, _) in zip(cubes, high, loaded, places):
            low = (cube - top.astype(f32)).astype(bf16)
            side = weighted(left, weight)
            value = fold(dot_nn(side, top)) + fold(dot_nn(side[0:16], low))
            if part:
                value = finish(value + before_ref[leaf, :, 0:lanes], right)
            done.append(value)
        for (_, place), value in zip(places, done):
            out_ref[place, :, 0:lanes] = value

    def finish_some(step):
        places = [place_of(step, k) for k in range(SELF_WIDTH)]
        done = [finish(before_ref[leaf], load_points(own_ref[leaf])[0]) for leaf, _ in places]
        for (_, place), value in zip(places, done):
            out_ref[place] = value

    for n, rows in enumerate(CLASSES):
        first = list_ref[1, n]
        end = list_ref[1, n + 1]
        middle = jnp.minimum((first + end + n) >> 1, end)
        lanes = 128 if rows == 128 else LEAF

        def body(step, _, rows=rows, lanes=lanes):
            some_leaves(step, rows, lanes)
            return 0

        lax.fori_loop(middle if part else first, end if part else middle, body, 0)
        if part:

            def rest(step, _):
                finish_some(step)
                return 0

            lax.fori_loop(first, middle, rest, 0)


def self_part(part, ordered, own, *before):
    return pl.pallas_call(
        functools.partial(self_kernel, part),
        name="self_part",
        out_shape=shaped(LEAVES + 8, 4 if part else 8, LEAF),
        in_specs=[SM, VM] + [VM] * part,
        out_specs=VM,
        cost_estimate=pl.CostEstimate(
            flops=LEAVES * 20_000_000, bytes_accessed=LEAVES * 8192, transcendentals=0
        ),
        compiler_params=pltpu.CompilerParams(**PARAMS),
    )(ordered, own, *before)


def near_kernel(
    list_ref, own_ref, in0, in1, in2, in3, backs_ref, self_ref,
    out_ref, pay0, pay1, pay2, pay3, table, total, shifts, formed_r, kept_c, sem, *held,
):
    pays = (pay0, pay1, pay2, pay3)
    copies = [
        pltpu.make_async_copy(own_ref, table.at[pl.ds(0, LEAVES)], sem.at[0]),
        pltpu.make_async_copy(self_ref.at[pl.ds(0, LEAVES)], total.at[pl.ds(0, LEAVES)], sem.at[5]),
    ]
    for q, part in enumerate((in0, in1, in2, in3)):
        copies.append(
            pltpu.make_async_copy(
                part.at[pl.ds(0, SLOTS)],
                table.at[pl.ds(LEAVES + q * SLOTS, SLOTS)],
                sem.at[1 + q],
            )
        )
    for copy in copies:
        copy.start()

    def clear(c, _):
        total[c] = jnp.zeros((8, LEAF), f32)
        return 0

    lax.fori_loop(LEAVES, 2 * LEAVES + 8, clear, 0, unroll=8)
    row = iota((8, 128), 0)
    for code in range(27):
        step = (code % 3 - 1, code // 3 % 3 - 1, code // 9 - 1)
        value = jnp.zeros((8, 128), f32)
        for k in range(3):
            value = jnp.where(row == k + 1, float(step[k]), value)
        shifts[code] = value
    for copy in copies:
        copy.wait()

    def decode(group, k):
        code = list_ref[0, group * WIDTH + k]
        value = jnp.maximum(code - 1, 0)
        return value & 511, (value >> 9) & 511, value >> 18, code > 0

    def shift_of(code):
        half = shifts[code]
        return jnp.concatenate([half, half], 1)

    def spaced(group, k, rows):
        r, c, code, _ = decode(group, k)
        points_r, _ = load_points(table[r])
        points_c, _ = load_points(table[c])
        points_r = (points_r + shift_of(code))[:, :rows]
        formed = b_form(points_r)
        formed_r[k, :, 0:rows] = formed
        kept_c[k] = points_c
        return squares(formed, b_form(points_c))

    def keep(k, rows, value):
        inverse = lax.rsqrt(value)
        held[k][0:rows, :] = (inverse * inverse * inverse).astype(bf16)

    def products(group, k, rows):
        r, c, code, live = decode(group, k)
        cube = held[k][0:rows, :]
        side_r = weighted(formed_r[k, :, 0:rows], table[r, 0:1, 0:rows])
        to_c = fold(dot_nn(side_r, cube))
        side_c = sources(kept_c[k] - shift_of(code), table[c, 0:1, :])
        to_r = fold(dot_nt(side_c, cube))
        return jnp.where(live, r, 2 * LEAVES), jnp.where(live, c, 2 * LEAVES), to_r, to_c

    def settle(done, rows):
        for r, c, to_r, to_c in done:
            total[r, :, 0:rows] = total[r, :, 0:rows] + to_r
            total[c] = total[c] + to_c

    for n, rows in enumerate(CLASSES):
        first = list_ref[1, n]
        end = list_ref[1, n + 1]

        @pl.when(end > first)
        def _(first=first, end=end, rows=rows):
            for k in range(WIDTH):
                keep(k, rows, spaced(first, k, rows))

            def advance(group, _):
                done = []
                for k in range(WIDTH):
                    done.append(products(group, k, rows))
                    keep(k, rows, spaced(group + 1, k, rows))
                settle(done, rows)
                return 0

            lax.fori_loop(first, end - 1, advance, 0)
            settle([products(end - 1, k, rows) for k in range(WIDTH)], rows)

    store = pltpu.make_async_copy(total.at[pl.ds(0, LEAVES)], out_ref, sem.at[6])
    store.start()
    for q in range(4):

        def finish_other(k, _, q=q):
            points, _ = load_points(table[LEAVES + q * SLOTS + k])
            pays[q][k] = finish(total[LEAVES + q * SLOTS + k], points)
            return 0

        lax.fori_loop(0, SLOTS, finish_other, 0, unroll=8)
        put_block(pays[q], backs_ref[q])
    store.wait()


def near_part(ordered, own, incoming, backs, self0):
    return pl.pallas_call(
        near_kernel,
        name="near_part",
        out_shape=[shaped(LEAVES, 8, LEAF)] + [shaped(PAY, 4, LEAF)] * 4,
        in_specs=[SM, HB, HB, HB, HB, HB, VM, HB],
        out_specs=[HB] + [VM] * 4,
        scratch_shapes=[
            pltpu.VMEM((2 * LEAVES, 4, LEAF), f32),
            pltpu.VMEM((2 * LEAVES + 8, 8, LEAF), f32),
            pltpu.VMEM((27, 8, 128), f32),
            pltpu.VMEM((WIDTH, 8, LEAF), f32),
            pltpu.VMEM((WIDTH, 8, LEAF), f32),
            pltpu.SemaphoreType.DMA((7,)),
        ] + [pltpu.VMEM((LEAF, LEAF), bf16)] * WIDTH,
        cost_estimate=pl.CostEstimate(
            flops=NEAR * 80_000_000, bytes_accessed=4_000_000, transcendentals=0
        ),
        compiler_params=pltpu.CompilerParams(**PARAMS),
    )(ordered, own, *incoming, backs, self0)


def sort_lists(code, group, width, out_ref):
    count = code.shape[1]
    hot = jnp.where(iota((8, count), 0) == group, 1.0, 0.0)
    earlier = jnp.where(iota((count, count), 0) < iota((count, count), 1), 1.0, 0.0).astype(bf16)
    before = dot_nn(hot.astype(bf16), earlier)
    members = jnp.sum(hot, 1, keepdims=True)
    lane = iota((1, SORTED), 1)
    place = jnp.zeros((1, count), f32)
    groups = jnp.zeros((1, 1), f32)
    ends = jnp.zeros((1, SORTED), f32)
    for n in range(len(CLASSES)):
        place = place + hot[n : n + 1] * (before[n : n + 1] + groups * width)
        groups = groups + jnp.floor((members[n : n + 1] + (width - 1)) * (1.0 / width))
        ends = jnp.where(lane == n + 1, groups, ends)
    place = jnp.where(group >= 0, place, -1.0).astype(jnp.int32)
    ordered = pick(jnp.broadcast_to(code, (8, count)), onehot_rows(SORTED, place), True)
    out_ref[0:1, :] = ordered[0:1].astype(jnp.int32)
    out_ref[1:2, :] = ends.astype(jnp.int32)


def derivatives(x, y, z):
    square = x * x + y * y + z * z
    inverse = 1.0 / jnp.sqrt(square)
    inverse2 = inverse * inverse
    table = {(0, (0, 0, 0)): inverse}
    for m in range(1, 5):
        table[(m, (0, 0, 0))] = table[(m - 1, (0, 0, 0))] * inverse2 * float(-(2 * m - 1))
    place = (x, y, z)

    def entry(m, alpha):
        key = (m, alpha)
        if key not in table:
            axis = [k for k in range(3) if alpha[k]][0]
            lower = tuple(alpha[k] - (k == axis) for k in range(3))
            value = place[axis] * entry(m + 1, lower)
            if lower[axis]:
                lowest = tuple(lower[k] - (k == axis) for k in range(3))
                value = value + float(lower[axis]) * entry(m + 1, lowest)
            table[key] = value
        return table[key]

    return {alpha: entry(0, alpha) for alpha in ALPHAS}


def mutual(a_ref, b_ref, to_a, to_b):
    def rows(n):
        return pl.ds(n * 8, 8)

    lift = a_ref[rows(38), :]
    live = a_ref[rows(39), :] > 0.5
    gap = [
        jnp.where(live, a_ref[rows(35 + k), :] - b_ref[rows(35 + k), :] - (lift if k == 2 else 0.0), 3.0)
        for k in range(3)
    ]
    made = derivatives(*gap)
    for beta in ALPHAS:
        sum_a = None
        sum_b = None
        for alpha in ALPHAS:
            if sum(alpha) + sum(beta) > 4:
                continue
            tensor = made[add(alpha, beta)]
            scale = 1.0 / afact(alpha)
            sign_a = -((-1.0) ** sum(alpha)) * scale
            sign_b = -((-1.0) ** sum(beta)) * scale
            term_a = b_ref[rows(AT[alpha]), :] * sign_a * tensor
            term_b = a_ref[rows(AT[alpha]), :] * sign_b * tensor
            sum_a = term_a if sum_a is None else sum_a + term_a
            sum_b = term_b if sum_b is None else sum_b + term_b
        to_a[rows(AT[beta]), :] = jnp.where(live, sum_a, 0.0)
        to_b[rows(AT[beta]), :] = jnp.where(live, sum_b, 0.0)


def far_kernel(
    image_ref, far_ref, parent_ref, near_ref, cells_ref, pcells_ref, in0, in1, in2, in3,
    leaf_ref, par_ref, backs_ref, ordered_ref, tails, table, left, right, to_a, to_b, total, sem,
):
    copies = []
    for q, part in enumerate((in0, in1, in2, in3)):
        copies.append(
            pltpu.make_async_copy(part.at[pl.ds(SLOTS, 5)], tails.at[q], sem.at[q])
        )
    for copy in copies:
        copy.start()
    table[:, 0:LEAVES] = cells_ref[...]
    table[:, LEAVES + 512 :] = pcells_ref[...]
    row = iota((40, 128), 0)
    to_a[...] = jnp.zeros_like(to_a)
    to_b[...] = jnp.zeros_like(to_b)
    left[...] = jnp.zeros_like(left)
    right[...] = jnp.zeros_like(right)
    for copy in copies:
        copy.wait()
    for q in range(4):
        block = get_block(lambda s, q=q: tails[q, s])
        block = block + jnp.where(
            row == 35, image_ref[q, 0], jnp.where(row == 36, image_ref[q, 1], 0.0)
        )
        table[:, LEAVES + q * 128 : LEAVES + q * 128 + 128] = block
    parts = jnp.concatenate([part.astype(f32) for part in split3(table[...])], 0).astype(bf16)
    total[...] = jnp.zeros_like(total)

    def gathered(hot, first, count):
        out = dot_nn(parts[:, first : first + count], hot)
        return out[0:40] + out[40:80] + out[80:120]

    def leaf_entry(ids):
        other = ids - LEAVES
        return jnp.where(ids < LEAVES, ids, LEAVES + other // SLOTS * 128 + other % SLOTS)

    def parent_entry(ids):
        other = ids - PARENTS
        return jnp.where(
            ids < PARENTS, LEAVES + 512 + ids, LEAVES + other // PSLOTS * 128 + SLOTS + other % PSLOTS
        )

    def hots(ids_a, ids_b, parents):
        if parents:
            return (
                onehot_rows(128, ids_a), LEAVES + 512, 128,
                onehot_rows(640, parent_entry(ids_b) - LEAVES), LEAVES, 640,
            )
        return (
            onehot_rows(LEAVES, ids_a), 0, LEAVES,
            onehot_rows(768, leaf_entry(ids_b)), 0, 768,
        )

    def load(ids_a, ids_b, lifts, g, parents):
        hot_a, first_a, count_a, hot_b, first_b, count_b = hots(ids_a, ids_b, parents)
        from_a = gathered(hot_a, first_a, count_a)
        from_b = gathered(hot_b, first_b, count_b)
        live = jnp.where(ids_b >= 0, 1.0, 0.0)
        from_a = jnp.where(row == 38, lifts.astype(f32) * float(CZ), from_a)
        from_a = jnp.where(row == 39, live, from_a)
        left[pl.ds(g, 40, stride=8), :] = from_a
        right[pl.ds(g, 40, stride=8), :] = from_b

    def store(ids_a, ids_b, g, parents):
        hot_a, first_a, count_a, hot_b, first_b, count_b = hots(ids_a, ids_b, parents)
        sum_a = pick(to_a[pl.ds(g, 40, stride=8), :], hot_a, True)
        sum_b = pick(to_b[pl.ds(g, 40, stride=8), :], hot_b, True)
        total[:, first_a : first_a + count_a] += sum_a
        total[:, first_b : first_b + count_b] += sum_b

    for g in range(FAR // 128):
        lanes = slice(g * 128, g * 128 + 128)
        load(far_ref[0, :, lanes], far_ref[1, :, lanes], far_ref[2, :, lanes], g, False)
    mutual(left, right, to_a, to_b)
    for g in range(FAR // 128):
        lanes = slice(g * 128, g * 128 + 128)
        store(far_ref[0, :, lanes], far_ref[1, :, lanes], g, False)
    ids_a, ids_b, lifts = [
        jnp.concatenate([parent_ref[k], jnp.full((1, 128 - PFAR), -(k == 1), jnp.int32)], 1)
        for k in range(3)
    ]
    load(ids_a, ids_b, lifts, 0, True)
    mutual(left, right, to_a, to_b)
    store(ids_a, ids_b, 0, True)

    ids_a, ids_b, lifts = near_ref[0], near_ref[1], near_ref[2]
    hot_a, _, _, hot_b, _, _ = hots(ids_a, ids_b, False)
    from_a = gathered(hot_a, 0, LEAVES)[35:39]
    from_b = gathered(hot_b, 0, 768)[35:39]
    count_a, count_b = from_a[3:4], from_b[3:4]
    fewer = jnp.minimum(count_a, count_b)
    swap = count_b < count_a
    group = jnp.where(fewer <= 128.0, 0, jnp.where(fewer <= 192.0, 1, 2))
    group = jnp.where(ids_b >= 0, group, -1)
    moved = jnp.zeros((1, NEAR), f32)
    for k in range(3):
        apart = from_a[k : k + 1] - from_b[k : k + 1]
        if k == 2:
            apart = apart - lifts.astype(f32) * float(CZ)
        apart = jnp.where(swap, -apart, apart)
        moved = moved + (apart + 1.0) * float(3**k)
    rows = jnp.where(swap, ids_b, ids_a)
    columns = jnp.where(swap, ids_a, ids_b)
    code = 1.0 + rows.astype(f32) + columns.astype(f32) * 512.0 + moved * 262144.0
    sort_lists(jnp.where(ids_b >= 0, code, 0.0), group, WIDTH, ordered_ref)

    leaf_ref[...] = total[:, 0:LEAVES]
    par_ref[...] = total[:, LEAVES + 512 :]
    for q in range(4):
        backs_ref[q] = total[:, LEAVES + q * 128 : LEAVES + q * 128 + 128]


def far_part(image, far, parent, near, cells, pcells, incoming):
    return pl.pallas_call(
        far_kernel,
        name="far_part",
        out_shape=[
            shaped(40, LEAVES), shaped(40, 128), shaped(4, 40, 128),
            jax.ShapeDtypeStruct((2, SORTED), jnp.int32),
        ],
        in_specs=[SM, VM, VM, VM, VM, VM, HB, HB, HB, HB],
        out_specs=[VM] * 4,
        scratch_shapes=[
            pltpu.VMEM((4, 5, 4, LEAF), f32),
            pltpu.VMEM((40, TABLE), f32),
        ] + [pltpu.VMEM((320, 128), f32)] * 4 + [
            pltpu.VMEM((40, TABLE), f32),
            pltpu.SemaphoreType.DMA((4,)),
        ],
        compiler_params=pltpu.CompilerParams(**PARAMS),
    )(
        image, far.transpose(1, 0, 2), parent.transpose(1, 0, 2), near.transpose(1, 0, 2),
        cells, pcells, *incoming,
    )


def shift_terms(terms, offsets):
    for axis in range(3):
        powers = [None, offsets[axis]]
        for _ in range(3):
            powers.append(powers[-1] * offsets[axis])
        moved = {}
        for alpha in ALPHAS:
            total = terms[alpha]
            for k in range(1, 5 - sum(alpha)):
                upper = tuple(alpha[q] + k * (q == axis) for q in range(3))
                total = total + terms[upper] * powers[k] * (1.0 / FACT[k])
            moved[alpha] = total
        terms = moved
    return terms


def horner(coefs, x):
    value = coefs[-1]
    for coef in reversed(coefs[:-1]):
        value = value * x + coef
    return value


def horner_both(coefs, x):
    value, slope = coefs[-1], None
    for coef in reversed(coefs[:-1]):
        slope = value if slope is None else slope * x + value
        value = value * x + coef
    return value, slope


def polynomial(get, x, y, z):
    over_y, over_dy, over_dz = [], [], []
    for i in range(5):
        over_z = [
            horner_both([get((i, j, k)) for k in range(5 - i - j)], z) for j in range(5 - i)
        ]
        value, slope = horner_both([pair[0] for pair in over_z], y)
        over_y.append(value)
        if i < 4:
            over_dy.append(slope)
            over_dz.append(horner([pair[1] for pair in over_z[:-1]], y))
    value, slope = horner_both(over_y, x)
    return value, slope, horner(over_dy, x), horner(over_dz, x)


def last_kernel(
    counts_ref, send_ref, sent_leaves, sent_parents, turned_ref, self_hbm, leaf_ref,
    par_ref, in0, in1, in2, in3, out_ref, slab_ref, terms_ref, field_ref, near_sum, sem,
):
    incoming = (in0, in1, in2, in3)
    lane128 = iota((1, 128), 1)
    fetch = pltpu.make_async_copy(self_hbm.at[pl.ds(0, LEAVES)], near_sum, sem.at[0])
    fetch.start()
    leaf = leaf_ref[...]
    par = par_ref[...]
    for q in range(4):
        block = get_block(lambda s, q=q: incoming[q][SLOTS + s])
        ids = id_row(sent_leaves, sent_parents, q)
        leaf_hot = onehot_rows(LEAVES, jnp.where(lane128 < SLOTS, ids, -1))
        parent_hot = onehot_rows(128, jnp.where(lane128 >= SLOTS, ids, -1))
        leaf = leaf + pick(block, leaf_hot, True)
        par = par + pick(block, parent_hot, True)

    fetch.wait()
    for q in range(4):

        def arrive(step, _, q=q):
            first = step * 8
            places = [send_ref[0, q * SLOTS + first + k] for k in range(8)]
            values = [near_sum[c] + incoming[q][first + k] for k, c in enumerate(places)]
            for c, value in zip(places, values):
                near_sum[c] = value
            return 0

        lax.fori_loop(0, SLOTS // 8, arrive, 0)
    lane_parent = (iota((128, LEAVES), 1) // CZ % CY // 2) * (CZ // 2) + iota(
        (128, LEAVES), 1
    ) % CZ // 2
    above = pick(par, jnp.where(lane_parent == iota((128, LEAVES), 0), 1.0, 0.0).astype(bf16))
    terms = {alpha: above[n : n + 1, :] for n, alpha in enumerate(ALPHAS)}
    terms = shift_terms(terms, parent_offsets())
    for n, alpha in enumerate(ALPHAS):
        terms_ref[n : n + 1, :] = leaf[n : n + 1, :] + terms[alpha]

    for half in range(2):
        lanes = slice(half * 128, half * 128 + 128)

        def term(alpha):
            return terms_ref[AT[alpha] : AT[alpha] + 1, lanes]

        coefs = {alpha: term(alpha) * (1.0 / afact(alpha)) for alpha in ALPHAS}

        def chunk(step, _, coefs=coefs, lanes=lanes):
            rows = pl.ds(pl.multiple_of(step * 32, 32), 32)
            x, y, z = [turned_ref[comp, rows, lanes] for comp in range(1, 4)]
            value, *slopes = polynomial(lambda alpha: coefs[alpha], x, y, z)
            field_ref[0, rows, lanes] = value
            for comp, slope in enumerate(slopes):
                field_ref[comp + 1, rows, lanes] = -slope
            return 0

        lax.fori_loop(0, LEAF // 32, chunk, 0)

    for comp in range(4):
        turned = field_ref[comp].T
        for half in range(2):
            slab_ref[pl.ds(half * LEAVES * 8 + comp, LEAVES, stride=8), :] = turned[
                :, half * 128 : half * 128 + 128
            ]

    lane = iota((4, LEAF), 1)

    def write(c, _):
        value = jnp.concatenate(
            [
                slab_ref[pl.ds(pl.multiple_of(half * LEAVES * 8 + c * 8, 8), 8), :]
                for half in range(2)
            ],
            1,
        )[0:4] + near_sum[c]
        start = pl.multiple_of(c * LEAF, LEAF)
        out_ref[:, pl.ds(start, LEAF)] = jnp.where(lane < counts_ref[c], value, 0.0)
        return 0

    lax.fori_loop(0, LEAVES, write, 0, unroll=8)


def last(counts, send_leaves, send_parents, turned, near, leaf, par, arrived):
    return pl.pallas_call(
        last_kernel,
        name="last",
        out_shape=shaped(4, LEAVES * LEAF),
        in_specs=[SM, SM, VM, VM, VM, HB] + [VM] * 6,
        out_specs=VM,
        scratch_shapes=[
            pltpu.VMEM((LEAVES * 16, 128), f32),
            pltpu.VMEM((40, LEAVES), f32),
            pltpu.VMEM((4, LEAF, LEAVES), f32),
            pltpu.VMEM((LEAVES, 4, LEAF), f32),
            pltpu.SemaphoreType.DMA((1,)),
        ],
        compiler_params=pltpu.CompilerParams(**PARAMS),
    )(
        counts, send_leaves, send_leaves, send_parents, turned, near, leaf, par, *arrived
    )


def image_shift(slab_at, sub_at, slab_count, sub_count):
    rows_out = []
    for direction in range(4):
        reach_x = slab_at + slab_steps[direction]
        reach_y = sub_at + sub_steps[direction]
        jump_x = (reach_x - reach_x % slab_count) * CX
        jump_y = (reach_y - reach_y % sub_count) * CY
        rows_out.append(jnp.stack([jump_x, jump_y]))
    return jnp.stack(rows_out).astype(f32)


def moved_by(value, slab_step, sub_step, slab_count, sub_count):
    pairs = []
    for slab_at in range(slab_count):
        for sub_at in range(sub_count):
            target = (slab_at + slab_step) % slab_count * sub_count + (sub_at + sub_step) % sub_count
            pairs.append((slab_at * sub_count + sub_at, target))
    return lax.ppermute(value, ("slab", "sub"), pairs)


def on_device(
    positions, masses, leaf_counts, send_leaves, send_parents, near_pairs, far_pairs, parent_pairs
):
    slab_count = lax.axis_size("slab")
    sub_count = lax.axis_size("sub")
    slab_at = lax.axis_index("slab")
    sub_at = lax.axis_index("sub")
    at = jnp.stack([slab_at, sub_at]).astype(jnp.int32)
    own, cells, pcells, *outgoing, turned, leaf_order = front(
        at, leaf_counts, send_leaves, send_parents, positions, masses
    )
    incoming = [
        moved_by(outgoing[q], -slab_steps[q], -sub_steps[q], slab_count, sub_count)
        for q in range(4)
    ]
    image = image_shift(slab_at, sub_at, slab_count, sub_count)
    self0 = self_part(0, leaf_order, own)
    leaf, par, backs, ordered = far_part(
        image, far_pairs, parent_pairs, near_pairs, cells, pcells, incoming
    )
    near, *returning = near_part(ordered, own, incoming, backs, self0)
    arrived = [
        moved_by(returning[q], slab_steps[q], sub_steps[q], slab_count, sub_count)
        for q in range(4)
    ]
    near = self_part(1, leaf_order, own, near)
    return last(
        leaf_counts, send_leaves, send_parents, turned, near, leaf, par, arrived
    )


def solution(mesh):
    return jax.shard_map(
        on_device,
        mesh=mesh,
        in_specs=(
            P(None, ("slab", "sub")),
            P(("slab", "sub")),
            P(("slab", "sub")),
            P(("slab", "sub"), None),
            P(("slab", "sub"), None),
            P(("slab", "sub"), None, None),
            P(("slab", "sub"), None, None),
            P(("slab", "sub"), None, None),
        ),
        out_specs=P(None, ("slab", "sub")),
        check_vma=False,
    )
```
